32 devices in a mesh: section: 2 (over core), seq: 16 (over z, y, x).
Axes of the slice: x: 2, y: 2, z: 4, core: 2. Of those that a mesh axis runs over, the one named last changes fastest.
Arguments:
- fields: bfloat16 [8, 2048, 2048], P(None, 'seq'), may hold values from -6 to 6
- cotangent: bfloat16 [2, 2048, 2048], P(None, 'seq'), may hold values from -0.08984375 to 0.08984375
- assignment: int32 [8], replicated, may hold values from 0 to 7, each once
- norm_gain: float32 [2, 2048], P('section'), may hold values from 0.1 to 1.9
- value_inner: bfloat16 [2, 16, 128, 128], P('section'), may hold values from -0.5 to 0.5
- value_outer: bfloat16 [2, 16, 16, 128], P('section'), may hold values from -1.5 to 1.5
- gate_inner: bfloat16 [2, 16, 128, 128], P('section'), may hold values from -0.5 to 0.5
- gate_outer: bfloat16 [2, 16, 16, 128], P('section'), may hold values from -1.5 to 1.5
- seq_inner: bfloat16 [2, 16, 128, 128], P('section', 'seq'), may hold values from -0.5 to 0.5
- seq_outer: bfloat16 [2, 128, 16, 16], P('section', 'seq'), may hold values from -1.5 to 1.5
Outputs:
- final_rows: bfloat16 [2, 2048, 2048], P(None, 'seq')
- grad_gain: float32 [2, 2048], P('section')
- grad_value_inner: float32 [2, 16, 128, 128], P('section')
- grad_value_outer: float32 [2, 16, 16, 128], P('section')
- grad_gate_inner: float32 [2, 16, 128, 128], P('section')
- grad_gate_outer: float32 [2, 16, 16, 128], P('section')
- grad_seq_inner: float32 [2, 16, 128, 128], P('section', 'seq')
- grad_seq_outer: float32 [2, 128, 16, 16], P('section', 'seq')
The draws below stay inside these ranges and needn't reach their ends.
Inputs may be any that keep to these rules, and one draw needn't show every extreme that they name: `assignment`: a permutation of 0 to 7.
All inputs are finite; a program needn't handle non-finite values.
Results may differ from the reference program's by a relative error of at most 0.029.
Values may be sent and summed in bfloat16 or wider, within the bound.
A program may use at most 128 MiB of HBM per device.

```python
import jax
import jax.numpy as jnp
from jax import lax

D = 2048
WB = 128
BS = 128
MB = 2
NF = 8
L = 2048
NB = 16
KB = 16
N_SECTION = 2


def steps_of(stream_key, extent, shards, low, largest):
    level = 1.0
    for dim, shards_of in shards:
        heights = jax.random.uniform(jax.random.fold_in(jax.random.fold_in(stream_key, 6), dim), (shards_of,), jnp.float32, low / len(shards), largest / len(shards))
        level = level * jnp.repeat(jnp.exp(heights), extent[dim] // shards_of).reshape((-1,) + (1,) * (len(extent) - 1 - dim))
    return level


def normal_values(key, shape, width, most, pieces=(), held_as=jnp.bfloat16):
    loudness = steps_of(key, shape, pieces, -0.22, 0.18) if pieces else 1.0
    entries = jax.random.normal(key, shape, jnp.float32) * width * loudness
    return jnp.minimum(jnp.maximum(entries, -most), most).astype(held_as)


def setup_inputs(seed: int = 0) -> dict:
    keys = jax.random.split(jax.random.key(seed), 11)
    fields = normal_values(keys[0], (NF, L, D), 1.0, 6.0, ((1, 16),))
    cotangent = normal_values(keys[1], (MB, L, D), 0.015, 0.08984375, ((1, 16),))
    assignment = jax.random.permutation(keys[2], NF).astype(jnp.int32)
    norm_gain = jnp.clip(1.0 + 0.18 * jax.random.normal(keys[3], (N_SECTION, D), jnp.float32), 0.1, 1.9)
    value_inner = normal_values(keys[4], (N_SECTION, KB, WB, WB), WB ** -0.5, 0.5, ((0, 2),))
    value_outer = normal_values(keys[5], (N_SECTION, KB, KB, WB), KB ** -0.5, 1.5, ((0, 2),))
    gate_inner = normal_values(keys[6], (N_SECTION, KB, WB, WB), WB ** -0.5, 0.5, ((0, 2),))
    gate_outer = normal_values(keys[7], (N_SECTION, KB, KB, WB), KB ** -0.5, 1.5, ((0, 2),))
    seq_inner = normal_values(keys[8], (N_SECTION, NB, BS, BS), BS ** -0.5, 0.5, ((0, 2), (1, 16)))
    seq_outer = normal_values(keys[9], (N_SECTION, BS, NB, NB), NB ** -0.5, 1.5, ((0, 2), (1, 16)))
    return dict(fields=fields, cotangent=cotangent, assignment=assignment, norm_gain=norm_gain, value_inner=value_inner, value_outer=value_outer, gate_inner=gate_inner, gate_outer=gate_outer, seq_inner=seq_inner, seq_outer=seq_outer)


EPSILON = 1e-06

def width_mix(hidden, inner, outer):
    count = hidden.shape[0]
    blocks = hidden.reshape(count, KB, WB).astype(jnp.float32)
    middle = jnp.einsum('nkj,kjq->nkq', blocks, inner.astype(jnp.float32)).astype(jnp.bfloat16)
    mixed = jnp.einsum('nkq,klq->nlq', middle.astype(jnp.float32), outer.astype(jnp.float32))
    return (mixed.reshape(count, D).astype(jnp.bfloat16), middle)

def width_back(hidden, middle, inner, outer, upstream):
    count = hidden.shape[0]
    blocks = hidden.reshape(count, KB, WB).astype(jnp.float32)
    up_blocks = upstream.reshape(count, KB, WB).astype(jnp.float32)
    grad_outer = jnp.einsum('nkq,nlq->klq', middle.astype(jnp.float32), up_blocks)
    grad_middle = jnp.einsum('nlq,klq->nkq', up_blocks, outer.astype(jnp.float32)).astype(jnp.bfloat16)
    grad_inner = jnp.einsum('nkj,nkq->kjq', blocks, grad_middle.astype(jnp.float32))
    grad_hidden = jnp.einsum('nkq,kjq->nkj', grad_middle.astype(jnp.float32), inner.astype(jnp.float32))
    return (grad_hidden.reshape(count, D), grad_inner, grad_outer)

def front(inputs, weights):
    wide = inputs.astype(jnp.float32)
    factor = lax.rsqrt(lax.optimization_barrier(jnp.mean(wide * wide, axis=-1, keepdims=True)) + EPSILON)
    hidden = (wide * factor * weights[0]).astype(jnp.bfloat16)
    values, value_mid = width_mix(hidden, weights[1], weights[2])
    gates, gate_mid = width_mix(hidden, weights[3], weights[4])
    return (wide, factor, hidden, values, value_mid, gates, gate_mid)

def seq_forward(values, weights):
    blocks = values.reshape(-1, BS, D).astype(jnp.float32)
    first_mix = jnp.einsum('bpi,bic->bpc', weights[5].astype(jnp.float32), blocks).astype(jnp.bfloat16)
    second = jnp.einsum('ipb,bic->pic', weights[6].astype(jnp.float32), first_mix.astype(jnp.float32))
    return (first_mix, second.astype(jnp.bfloat16).reshape(-1, D))

def layer(inputs, weights):
    wide, factor, hidden, values, value_mid, gates, gate_mid = front(inputs, weights)
    first_mix, mixed = seq_forward(values, weights)
    return (wide + mixed.astype(jnp.float32) * gates.astype(jnp.float32)).astype(jnp.bfloat16)

def layer_back(inputs, upstream, weights):
    wide, factor, hidden, values, value_mid, gates, gate_mid = front(inputs, weights)
    first_mix, mixed = seq_forward(values, weights)
    up_wide = upstream.astype(jnp.float32)
    grad_mixed = (up_wide * gates.astype(jnp.float32)).astype(jnp.bfloat16)
    grad_gates = (up_wide * mixed.astype(jnp.float32)).astype(jnp.bfloat16)
    grad_blocks = grad_mixed.reshape(-1, BS, D).astype(jnp.float32)
    grad_first = jnp.einsum('ipb,pic->bic', weights[6].astype(jnp.float32), grad_blocks).astype(jnp.bfloat16)
    grad_sout = jnp.einsum('pic,bic->ipb', grad_blocks, first_mix.astype(jnp.float32))
    grad_values = jnp.einsum('bpi,bpc->bic', weights[5].astype(jnp.float32), grad_first.astype(jnp.float32))
    grad_values = grad_values.astype(jnp.bfloat16).reshape(-1, D)
    grad_sin = jnp.einsum('bpc,bic->bpi', grad_first.astype(jnp.float32), values.reshape(-1, BS, D).astype(jnp.float32))
    hidden_v, grad_vin, grad_vout = width_back(hidden, value_mid, weights[1], weights[2], grad_values)
    hidden_g, grad_gin, grad_gout = width_back(hidden, gate_mid, weights[3], weights[4], grad_gates)
    grad_hidden = hidden_v + hidden_g
    grad_norm = lax.optimization_barrier(jnp.sum(grad_hidden * wide * factor, axis=0))
    scaled = weights[0] * grad_hidden
    grad_input = up_wide + factor * scaled - wide * factor ** 3 * lax.optimization_barrier(jnp.mean(scaled * wide, axis=-1, keepdims=True))
    return (grad_input.astype(jnp.bfloat16), (grad_norm, grad_vin, grad_vout, grad_gin, grad_gout, grad_sin, grad_sout))

def reference(fields, cotangent, assignment, norm_gain, value_inner, value_outer, gate_inner, gate_outer, seq_inner, seq_outer):
    arrays = (norm_gain, value_inner, value_outer, gate_inner, gate_outer, seq_inner, seq_outer)
    weights_zero = tuple((item[0] for item in arrays))
    weights_one = tuple((item[1] for item in arrays))
    sums_zero = tuple((jnp.zeros(item.shape[1:], jnp.float32) for item in arrays))
    sums_one = tuple((jnp.zeros(item.shape[1:], jnp.float32) for item in arrays))
    finals = []
    for micro in range(MB):
        start = fields[assignment[micro]]
        middle = layer(start, weights_zero)
        finals.append(layer(middle, weights_one))
        back_one, grads_one = layer_back(middle, cotangent[micro], weights_one)
        back_zero, grads_zero = layer_back(start, back_one, weights_zero)
        sums_one = tuple((total + part for total, part in zip(sums_one, grads_one)))
        sums_zero = tuple((total + part for total, part in zip(sums_zero, grads_zero)))
    stacked = tuple((jnp.stack([first, second]) for first, second in zip(sums_zero, sums_one)))
    return (jnp.stack(finals), stacked[0], stacked[1], stacked[2], stacked[3], stacked[4], stacked[5], stacked[6])
```

```python
import functools

import jax
import jax.numpy as jnp
from jax import lax
from jax.experimental import pallas as pl
from jax.experimental.pallas import tpu as pltpu
from jax.sharding import PartitionSpec as P

D = 2048
WB = 128
BS = 128
KB = 16
EPSILON = 1e-06
F32 = jnp.float32
BF16 = jnp.bfloat16
MESH = pl.DeviceIdType.MESH
VMEM = pl.BlockSpec(memory_space=pltpu.VMEM)
WIDE = 512
CHUNKS = D // WIDE
PLANE = 4


def dot(a, b, ca, cb):
    return lax.dot_general(a, b, (((ca,), (cb,)), ((), ())), preferred_element_type=F32)


def lane(k):
    return pl.ds(pl.multiple_of(k * WB, WB), WB)


def in_half(n, block):
    half = lax.axis_index("seq") // (n // 2)
    return {"section": block // (n // 2), "seq": half * (n // 2) + lax.rem(block, n // 2)}


def my_block(n):
    return lax.axis_index("section") * (n // 2) + lax.rem(lax.axis_index("seq"), n // 2)


def on_seq(n, chip):
    return {"seq": chip}


def greet(n, me, where=in_half):
    barrier = pltpu.get_barrier_semaphore()

    def one(d, c):
        pl.semaphore_signal(
            barrier, inc=1, device_id=where(n, lax.rem(me + d, n)), device_id_type=MESH
        )
        return c

    lax.fori_loop(1, n, one, 0)


def greeted(n):
    pl.semaphore_wait(pltpu.get_barrier_semaphore(), n - 1)


def piece(src, dst, sems, row, to, at, d):
    return to_device(src, dst, sems, row, {"seq": to}, at, d)


def to_device(src, dst, sems, row, device, at, d):
    return pltpu.make_async_remote_copy(
        src_ref=src.at[row],
        dst_ref=dst.at[at],
        send_sem=sems[0].at[d],
        recv_sem=sems[1].at[d],
        device_id=device,
        device_id_type=MESH,
    )


def send_all(n, me, i, src, dst, sems):
    def one(d, c):
        peer = lax.rem(me + d, n)
        to_device(src, dst, sems, (i, peer), in_half(n, peer), (i, me), (i, d)).start()
        return c

    lax.fori_loop(1, n, one, 0)
    dst[i, me] = src[i, me]


def wait_all(n, me, i, src, dst, sems):
    def one(d, c):
        peer = lax.rem(me + d, n)
        origin = lax.rem(me + n - d, n)
        copy = to_device(src, dst, sems, (i, peer), in_half(n, peer), (i, origin), (i, d))
        copy.wait_send()
        copy.wait_recv()
        return c

    lax.fori_loop(1, n, one, 0)


def chosen(section, own, other, put):
    core = lax.axis_index("section")

    @pl.when(core == section)
    def _():
        put(own)

    @pl.when(core != section)
    def _():
        put(other)


def load_weights(n, section, own, other, to):
    gain_s, w_s, vo_s, go_s, sin_s, sx_s = to
    rows = sin_s.shape[0]
    pad = rows // n

    def put(refs):
        gain, vin, vout, gin, gout, sin, sout = refs
        gain_s[...] = gain[...]
        vo_s[...] = vout[...].astype(F32)
        go_s[...] = gout[...].astype(F32)
        sin_s[...] = sin[...]
        w_s[:, :, :WB] = vin[...]
        w_s[:, :, WB:] = gin[...]
        wide = dot(sout[...], copies(n, rows), 1, 0)
        sx_s[...] = jnp.where(same_place(rows, pad), wide, 0.0).astype(BF16)

    chosen(section, own, other, put)


def copies(n, rows, dtype=BF16):
    at = lax.broadcasted_iota(jnp.int32, (n, rows), 0)
    to = lax.broadcasted_iota(jnp.int32, (n, rows), 1)
    return jnp.where(to // (rows // n) == at, 1.0, 0.0).astype(dtype)


def same_place(rows, pad):
    at = lax.broadcasted_iota(jnp.int32, (rows, rows), 0)
    to = lax.broadcasted_iota(jnp.int32, (rows, rows), 1)
    return at % pad == to % pad


def cross(read, write, b_ref, back, first=0, last=KB):
    def rows(i, c):
        at = pl.ds(pl.multiple_of(i * 16, 16), 16)
        parts = [read(k, at).astype(F32) for k in range(KB)]
        for l in range(first, last):
            total = None
            for k in range(KB):
                row = b_ref[l, k : k + 1, :] if back else b_ref[k, l : l + 1, :]
                term = parts[k] * row
                total = term if total is None else total + term
            write(l, at, total.astype(BF16))
        return c

    lax.fori_loop(0, BS // 16, rows, 0)


def row_factor(x_ref):
    wide = x_ref[...].astype(F32)
    return lax.rsqrt(jnp.mean(wide * wide, axis=-1, keepdims=True) + EPSILON)


def spread_rows(n, rows, dtype=BF16):
    pad = rows // n
    each = BS // n
    at = lax.broadcasted_iota(jnp.int32, (rows, BS), 0)
    to = lax.broadcasted_iota(jnp.int32, (rows, BS), 1)
    hit = (at // pad * each + at % pad == to) & (at % pad < each)
    return jnp.where(hit, 1.0, 0.0).astype(dtype)


def fwd_kernel(n, section, x_ref, *refs):
    own, other = refs[:7], refs[7:14]
    out_ref, h_ref, t_ref, v_ref, g_ref, sp_ref, s_ref = refs[14:21]
    weights = refs[21:27]
    gain_ref, w_ref, vo_ref, go_ref, sin_ref, sx_ref = weights
    a1, b1, a2, b2, ss1, rs1, ss2, rs2 = refs[27:]
    me = my_block(n)
    rows = sin_ref.shape[0]
    pad = rows // n
    greet(n, me)
    load_weights(n, section, own, other, weights)
    factor = row_factor(x_ref)
    for k in range(KB):
        cols = slice(k * WB, (k + 1) * WB)
        gain = gain_ref[k : k + 1, :]
        hidden = (x_ref[:, cols].astype(F32) * factor * gain).astype(BF16)
        h_ref[:, cols] = hidden
        t_ref[k] = dot(hidden, w_ref[k], 1, 0).astype(BF16)

    def put(ref):
        def write(l, at, value):
            ref[at, l * WB : (l + 1) * WB] = value

        return write

    for i in range(CHUNKS):
        each = KB // CHUNKS
        cross(lambda k, at: t_ref[k, at, :WB], put(v_ref), vo_ref, False, i * each, (i + 1) * each)
        y = dot(sin_ref[...], v_ref[:, i * WIDE : (i + 1) * WIDE], 1, 0)
        a1[i] = y.reshape(n, pad, WIDE).astype(BF16)
        if i == 0:
            greeted(n)
        send_all(n, me, i, a1, b1, (ss1, rs1))
    cross(lambda k, at: t_ref[k, at, WB:], put(g_ref), go_ref, False)
    for i in range(CHUNKS):
        wait_all(n, me, i, a1, b1, (ss1, rs1))
        got = b1[i].astype(F32).reshape(rows, WIDE).astype(BF16)
        sp_ref[:, i * WIDE : (i + 1) * WIDE] = got
        y = dot(sx_ref[...], got, 1, 0)
        a2[i] = y.reshape(n, pad, WIDE).astype(BF16)
        send_all(n, me, i, a2, b2, (ss2, rs2))
    for i in range(CHUNKS):
        wait_all(n, me, i, a2, b2, (ss2, rs2))
        cols = slice(i * WIDE, (i + 1) * WIDE)
        mixed = b2[i].astype(F32).reshape(rows, WIDE)
        if rows != BS:
            mixed = dot(spread_rows(n, rows), mixed.astype(BF16), 0, 0)
        s_ref[:, cols] = mixed.astype(BF16)
        out_ref[:, cols] = (
            x_ref[:, cols].astype(F32) + mixed * g_ref[:, cols].astype(F32)
        ).astype(BF16)


def bwd_kernel(n, section, e_ref, x_ref, h_ref, t_ref, v_ref, g_ref, sp_ref, s_ref, *refs):
    own, other = refs[:7], refs[7:14]
    dx_ref, flat_ref, esin_ref, esx_ref = refs[14:18]
    weights = refs[18:24]
    gain_ref, w_ref, vo_ref, go_ref, sin_ref, sx_ref = weights
    a1, b1, a2, b2, dt, up, dh, ss1, rs1, ss2, rs2 = refs[24:]
    me = my_block(n)
    rows = sin_ref.shape[0]
    pad = rows // n
    greet(n, me)
    for i in range(CHUNKS):
        cols = slice(i * WIDE, (i + 1) * WIDE)
        ds = e_ref[:, cols].astype(F32) * g_ref[:, cols].astype(F32)
        if rows != BS:
            ds = dot(spread_rows(n, rows), ds.astype(BF16), 1, 0)
        a1[i] = ds.reshape(n, pad, WIDE).astype(BF16)
        if i == 0:
            greeted(n)
        send_all(n, me, i, a1, b1, (ss1, rs1))
    load_weights(n, section, own, other, weights)

    def middle_back(first, b_ref):
        def write(k, at, value):
            dt[k, at, first : first + WB] = value

        cross(lambda l, at: up[at, l * WB : (l + 1) * WB], write, b_ref, True)

    def outer_grad(first, start):
        def block(k, c):
            middle = t_ref[k, :, first : first + WB].astype(F32)
            found = []
            for l in range(KB):
                both = middle * up[:, l * WB : (l + 1) * WB]
                found.append(jnp.sum(both, axis=0, keepdims=True))
            at = pl.ds(pl.multiple_of(start + k * KB, KB), KB)
            flat_ref[at, :] = jnp.concatenate(found, axis=0).astype(BF16)
            return c

        lax.fori_loop(0, KB, block, 0)

    for i in range(CHUNKS):
        cols = slice(i * WIDE, (i + 1) * WIDE)
        dg = e_ref[:, cols].astype(F32) * s_ref[:, cols].astype(F32)
        up[:, cols] = dg.astype(BF16).astype(F32)
    middle_back(WB, go_ref)
    for i in range(CHUNKS):
        wait_all(n, me, i, a1, b1, (ss1, rs1))
        got = b1[i].astype(F32).reshape(rows, WIDE).astype(BF16)
        y = dot(sx_ref[...], got, 0, 0)
        a2[i] = y.reshape(n, pad, WIDE).astype(BF16)
        send_all(n, me, i, a2, b2, (ss2, rs2))
    pairs = jnp.zeros((rows, rows), F32)
    for i in range(CHUNKS):
        got = b1[i].astype(F32).reshape(rows, WIDE).astype(BF16)
        pairs += dot(got, sp_ref[:, i * WIDE : (i + 1) * WIDE], 1, 1)
    esx_ref[...] = lax.dot_general(
        jnp.where(same_place(rows, pad), pairs, 0.0), copies(n, rows, F32),
        (((1,), (1,)), ((), ())), precision=lax.Precision.HIGHEST, preferred_element_type=F32,
    )
    outer_grad(WB, 2 * D + KB * KB)
    inner = jnp.zeros((rows, BS), F32)
    for i in range(CHUNKS):
        wait_all(n, me, i, a2, b2, (ss2, rs2))
        cols = slice(i * WIDE, (i + 1) * WIDE)
        dy = b2[i].astype(F32).reshape(rows, WIDE).astype(BF16)
        inner += dot(dy, v_ref[:, cols], 1, 1)
        up[:, cols] = dot(sin_ref[...], dy, 0, 0).astype(BF16).astype(F32)
    esin_ref[...] = inner
    middle_back(0, vo_ref)
    outer_grad(0, 2 * D)
    factor = row_factor(x_ref)
    lean = jnp.zeros((BS, WB), F32)
    gains = []
    for k in range(KB):
        cols = slice(k * WB, (k + 1) * WB)
        both = dt[k]
        pair = dot(h_ref[:, cols], both, 0, 0).astype(BF16)
        flat_ref[cols, :] = pair[:, :WB]
        flat_ref[D + k * WB : D + (k + 1) * WB, :] = pair[:, WB:]
        part = dot(both, w_ref[k], 1, 1)
        seen = part * x_ref[:, cols].astype(F32)
        gains.append(jnp.sum(seen * factor, axis=0, keepdims=True))
        gain = gain_ref[k : k + 1, :]
        lean += gain * seen
        dh[:, cols] = gain * part
    used = 2 * D + 2 * KB * KB
    flat_ref[used : used + KB, :] = jnp.concatenate(gains, axis=0).astype(BF16)
    left = flat_ref.shape[0] - used - KB
    if left:
        flat_ref[used + KB :, :] = jnp.zeros((left, WB), BF16)
    mean = jnp.sum(lean, axis=-1, keepdims=True) * (1.0 / D)
    pull = factor * factor * factor * mean
    for k in range(KB):
        cols = slice(k * WB, (k + 1) * WB)
        dx_ref[:, cols] = (
            e_ref[:, cols].astype(F32)
            + factor * dh[:, cols]
            - x_ref[:, cols].astype(F32) * pull
        ).astype(BF16)


def params(number):
    return pltpu.CompilerParams(
        collective_id=number, has_side_effects=True, vmem_limit_bytes=56 * 2**20
    )


def weight_scratch(rows):
    return [
        pltpu.VMEM((KB, WB), F32),
        pltpu.VMEM((KB, WB, 2 * WB), BF16),
        pltpu.VMEM((KB, KB, WB), F32),
        pltpu.VMEM((KB, KB, WB), F32),
        pltpu.VMEM((rows, BS), BF16),
        pltpu.VMEM((rows, rows), BF16),
    ]


def exchange_scratch(n, pad):
    return (
        [pltpu.VMEM((CHUNKS, n, pad, WIDE), BF16)] * 4,
        [pltpu.SemaphoreType.DMA((CHUNKS, n))] * 4,
    )


def forward(n, section, x, own, other):
    rows = own[5].shape[0]
    buffers, sems = exchange_scratch(n, rows // n)
    half = jax.ShapeDtypeStruct((BS, D), BF16)
    return pl.pallas_call(
        functools.partial(fwd_kernel, n, section),
        out_shape=(
            half, half, jax.ShapeDtypeStruct((KB, BS, 2 * WB), BF16), half, half,
            jax.ShapeDtypeStruct((rows, D), BF16), half,
        ),
        in_specs=[VMEM] * 15,
        out_specs=(VMEM,) * 7,
        scratch_shapes=weight_scratch(rows) + buffers + sems,
        compiler_params=params(section),
        name="layer_forward",
    )(x, *own, *other)


def backward(n, section, upstream, x, saved, own, other):
    rows = own[5].shape[0]
    buffers, sems = exchange_scratch(n, rows // n)
    return pl.pallas_call(
        functools.partial(bwd_kernel, n, section),
        out_shape=(
            jax.ShapeDtypeStruct((BS, D), BF16),
            jax.ShapeDtypeStruct((n * chunk_rows(n), WB), BF16),
            jax.ShapeDtypeStruct((rows, BS), F32),
            jax.ShapeDtypeStruct((rows, n), F32),
        ),
        in_specs=[VMEM] * 22,
        out_specs=(VMEM,) * 4,
        scratch_shapes=weight_scratch(rows)
        + buffers
        + [
            pltpu.VMEM((KB, BS, 2 * WB), BF16),
            pltpu.VMEM((BS, D), F32),
            pltpu.VMEM((BS, D), F32),
        ]
        + sems,
        compiler_params=params(2 + section),
        name="layer_backward",
    )(upstream, x, *saved, *own, *other)


def chunk_rows(n):
    return -(-(2 * D + 2 * KB * KB + KB) // (16 * n)) * 16


def sum_kernel(n, zero_ref, one_ref, *refs):
    outs = refs[:5]
    give, came, g, land, part, lines, mine, full = refs[5:13]
    sc, rc, s1, r1, s2, r2, s3, r3, s4, r4 = refs[13:]
    me = lax.axis_index("seq")
    core = lax.axis_index("section")
    depth = n // PLANE
    z, p = me // PLANE, lax.rem(me, PLANE)
    barrier = pltpu.get_barrier_semaphore()
    greet(n, me, on_seq)
    pl.semaphore_signal(
        barrier, inc=1, device_id={"section": 1 - core}, device_id_type=MESH
    )

    def put(refs):
        give[...] = refs[1][...]
        g[...] = refs[0][...]

    chosen(0, (zero_ref, one_ref), (one_ref, zero_ref), put)
    pl.semaphore_wait(barrier, n)

    def plane(d, sign=1):
        return lax.rem(p + PLANE + sign * d, PLANE)

    def line(d, sign=1):
        return lax.rem(z + depth + sign * d, depth)

    def across(q, at):
        return pltpu.make_async_remote_copy(
            src_ref=give.at[q, at], dst_ref=came.at[q, at],
            send_sem=sc.at[q, at], recv_sem=rc.at[q, at],
            device_id={"section": 1 - core}, device_id_type=MESH,
        )

    for e in range(1, depth + 1):
        for q in range(PLANE):
            across(q, line(e)).start()
    for e in range(1, depth + 1):
        at = line(e)
        for q in range(PLANE):
            across(q, at).wait()
            g[q, at] = (g[q, at].astype(F32) + came[q, at].astype(F32)).astype(BF16)
        for d in range(1, PLANE):
            q = plane(d)
            piece(g, land, (s1, r1), (q, at), z * PLANE + q, (p, at), (d, e - 1)).start()
        land[p, at] = g[p, at]
    for e in range(1, depth + 1):
        at = line(e)
        for d in range(1, PLANE):
            q = plane(d)
            copy = piece(
                g, land, (s1, r1), (q, at), z * PLANE + q, (plane(d, -1), at), (d, e - 1)
            )
            copy.wait_send()
            copy.wait_recv()
        total = land[0, at].astype(F32)
        for q in range(1, PLANE):
            total = total + land[q, at].astype(F32)
        part[at] = total.astype(BF16)
        if e < depth:
            piece(part, lines, (s2, r2), at, at * PLANE + p, z, e).start()
    lines[z] = part[z]
    for d in range(1, depth):
        q = line(d)
        copy = piece(part, lines, (s2, r2), q, q * PLANE + p, line(d, -1), d)
        copy.wait_send()
        copy.wait_recv()
    total = lines[0].astype(F32)
    for q in range(1, depth):
        total = total + lines[q].astype(F32)
    mine[0] = total.astype(BF16)
    for d in range(1, depth):
        piece(mine, full, (s3, r3), 0, line(d) * PLANE + p, (p, z), d).start()
    for d in range(1, PLANE):
        piece(mine, full, (s4, r4), 0, z * PLANE + plane(d), (p, z), (d, 0)).start()
    full[p, z] = mine[0]
    for e in range(1, depth):
        at = line(e, -1)
        copy = piece(mine, full, (s3, r3), 0, line(e) * PLANE + p, (p, at), e)
        copy.wait_send()
        copy.wait_recv()
        for d in range(1, PLANE):
            piece(full, full, (s4, r4), (p, at), z * PLANE + plane(d), (p, at), (d, e)).start()
    for e in range(depth):
        at = line(e, -1)
        for d in range(1, PLANE):
            copy = piece(
                full, full, (s4, r4), (p, at), z * PLANE + plane(d), (plane(d, -1), at), (d, e)
            )
            copy.wait_send()
            copy.wait_recv()
    each = full.shape[2]
    for j in range(n):
        start = 0
        for ref in outs:
            low, high = max(j * each, start), min((j + 1) * each, start + ref.shape[0])
            if low < high:
                ref[low - start : high - start, :] = full[
                    j // depth, j % depth, low - j * each : high - j * each, :
                ].astype(F32)
            start += ref.shape[0]


def sum_over_seq(n, zero, one):
    each = chunk_rows(n)
    depth = n // PLANE
    whole = pltpu.VMEM((PLANE, depth, each, WB), BF16)
    some = pltpu.VMEM((depth, each, WB), BF16)
    shape = (PLANE, depth, each, WB)
    return pl.pallas_call(
        functools.partial(sum_kernel, n),
        out_shape=tuple(
            jax.ShapeDtypeStruct((size, WB), F32) for size in (D, D, KB * KB, KB * KB, KB)
        ),
        in_specs=[VMEM] * 2,
        out_specs=(VMEM,) * 5,
        scratch_shapes=[whole] * 4
        + [some, some, pltpu.VMEM((1, each, WB), BF16), whole]
        + [pltpu.SemaphoreType.DMA((PLANE, depth))] * 4
        + [pltpu.SemaphoreType.DMA((depth,))] * 4
        + [pltpu.SemaphoreType.DMA((PLANE, depth))] * 2,
        compiler_params=params(4),
        name="gradient_sum",
    )(zero.reshape(shape), one.reshape(shape))


def swapped(value):
    return lax.ppermute(value, "section", [(0, 1), (1, 0)])


def to_partner(value, n, from_own):
    half = n // 2
    pairs = [
        (core * n + chip, core * n + (chip + half) % n)
        for core in range(2)
        for chip in range(n)
        if (core == chip // half) == from_own
    ]
    return lax.ppermute(value, ("section", "seq"), pairs)


def on_device(
    fields, cotangent, assignment, norm_gain, value_inner, value_outer,
    gate_inner, gate_outer, seq_inner, seq_outer,
):
    n = lax.axis_size("seq")
    core = lax.axis_index("section")
    half = lax.axis_index("seq") // (n // 2)
    is_first = core == 0
    is_own = core == half
    each = BS // n
    pad = max(each, 8)
    rows = n * pad
    sin = jnp.pad(seq_inner[0].reshape(n, each, BS), ((0, 0), (0, pad - each), (0, 0)))
    sout = jnp.pad(seq_outer[0].transpose(1, 0, 2), ((0, 0), (0, pad - each), (0, 0)))
    own = (
        norm_gain[0].reshape(KB, WB), value_inner[0], value_outer[0], gate_inner[0], gate_outer[0],
    )
    other = tuple(swapped(item) for item in own)
    seqs = jnp.concatenate([sin.reshape(rows, BS), sout.reshape(rows, n)], axis=1)
    seqs_other = swapped(seqs)
    seqs, seqs_other = jnp.where(
        is_own, jnp.stack([seqs, seqs_other]), to_partner(jnp.stack([seqs, seqs_other]), n, True)
    )
    own = own + (seqs[:, :BS], seqs[:, BS:])
    other = other + (seqs_other[:, :BS], seqs_other[:, BS:])

    def placed(array, here, there):
        local = lax.dynamic_index_in_dim(array, here, 0, keepdims=False)
        sent = lax.dynamic_index_in_dim(array, there, 0, keepdims=False)
        return jnp.where(is_own, local, to_partner(sent, n, True))

    x0 = placed(fields, assignment[half], assignment[1 - half])
    upstream = placed(cotangent, half, 1 - half)
    x1, *saved0 = forward(n, 0, x0, own, other)
    last, *saved1 = forward(n, 1, x1, own, other)
    last_other = to_partner(last, n, False)
    both = jnp.where(half == 0, jnp.stack([last, last_other]), jnp.stack([last_other, last]))
    final = jnp.where(is_own, both, swapped(both))
    dx1, flat1, esin1, esx1 = backward(n, 1, upstream, x1, saved1, own, other)
    _, flat0, esin0, esx0 = backward(n, 0, dx1, x0, saved0, own, other)
    pair = jnp.stack(
        [jnp.concatenate([esin0, esx0], axis=1), jnp.concatenate([esin1, esx1], axis=1)]
    )
    pair = pair + to_partner(pair, n, False)
    seq_grad = jnp.where(
        is_own,
        jnp.where(is_first, pair[0], pair[1]),
        swapped(jnp.where(is_first, pair[1], pair[0])),
    )
    esin = seq_grad[:, :BS].reshape(n, pad, BS)[:, :each].reshape(BS, BS)
    esx = seq_grad[:, BS:].reshape(n, pad, n)[:, :each].transpose(1, 0, 2)
    vin, gin, vout, gout, gain = sum_over_seq(n, flat0, flat1)
    return (
        final,
        gain.reshape(1, D),
        vin.reshape(1, KB, WB, WB),
        vout.reshape(1, KB, KB, WB),
        gin.reshape(1, KB, WB, WB),
        gout.reshape(1, KB, KB, WB),
        esin[None, None],
        esx[None],
    )


def solution(mesh):
    in_specs = (
        P(None, "seq", None),
        P(None, "seq", None),
        P(),
        P("section", None),
        P("section", None, None, None),
        P("section", None, None, None),
        P("section", None, None, None),
        P("section", None, None, None),
        P("section", "seq", None, None),
        P("section", "seq", None, None),
    )
    out_specs = (
        P(None, "seq", None),
        P("section", None),
        P("section", None, None, None),
        P("section", None, None, None),
        P("section", None, None, None),
        P("section", None, None, None),
        P("section", "seq", None, None),
        P("section", "seq", None, None),
    )
    return jax.shard_map(
        on_device, mesh=mesh, in_specs=in_specs, out_specs=out_specs, check_vma=False
    )
```

```python
import functools

import jax
import jax.numpy as jnp
from jax import lax
from jax.experimental import pallas as pl
from jax.experimental.pallas import tpu as pltpu
from jax.sharding import PartitionSpec as P

D = 2048
WB = 128
BS = 128
KB = 16
EPSILON = 1e-06
F32 = jnp.float32
BF16 = jnp.bfloat16
MESH = pl.DeviceIdType.MESH
WIDE = 512
CHUNKS = D // WIDE
HEAD = 4
USED = 2 * D + 2 * KB * KB


def dot(a, b, ca, cb):
    return lax.dot_general(a, b, (((ca,), (cb,)), ((), ())), preferred_element_type=F32)


def chunk_rows(n):
    return -(-(USED + KB) // (16 * n)) * 16


def remote(src, dst, send, recv, device):
    return pltpu.make_async_remote_copy(
        src_ref=src, dst_ref=dst, send_sem=send, recv_sem=recv,
        device_id=device, device_id_type=MESH,
    )


def in_half(n, block):
    half = lax.axis_index("seq") // (n // 2)
    return {"section": block // (n // 2), "seq": half * (n // 2) + lax.rem(block, n // 2)}


def send_all(n, me, i, src, dst, sems):
    def one(d, c):
        peer = lax.rem(me + d, n)
        remote(
            src.at[i, peer], dst.at[i, me], sems[0].at[i], sems[1].at[i], in_half(n, peer)
        ).start()
        return c

    lax.fori_loop(1, n, one, 0)
    dst[i, me] = src[i, me]


def wait_all(n, me, i, src, dst, sems):
    others = pl.ds(0, n - 1)
    copy = remote(
        src.at[i, others], dst.at[i, others], sems[0].at[i], sems[1].at[i],
        in_half(n, lax.rem(me + 1, n)),
    )
    copy.wait_send()
    copy.wait_recv()


def copies(count, rows, pad):
    at = lax.broadcasted_iota(jnp.int32, (count, rows), 0)
    to = lax.broadcasted_iota(jnp.int32, (count, rows), 1)
    return jnp.where(to // pad == at, 1.0, 0.0).astype(BF16)


def same_place(rows, pad):
    at = lax.broadcasted_iota(jnp.int32, (rows, rows), 0)
    to = lax.broadcasted_iota(jnp.int32, (rows, rows), 1)
    return at % pad == to % pad


def by_place(n, rows):
    pad = rows // n
    at = lax.broadcasted_iota(jnp.int32, (rows, BS), 0)
    to = lax.broadcasted_iota(jnp.int32, (rows, BS), 1)
    hit = (at % pad * n + at // pad == to) & (at % pad < BS // n)
    return jnp.where(hit, 1.0, 0.0).astype(BF16)


def spread_rows(n, rows):
    pad = rows // n
    each = BS // n
    at = lax.broadcasted_iota(jnp.int32, (rows, BS), 0)
    to = lax.broadcasted_iota(jnp.int32, (rows, BS), 1)
    hit = (at // pad * each + at % pad == to) & (at % pad < each)
    return jnp.where(hit, 1.0, 0.0).astype(BF16)


def cross(read, write, b_ref, back, cols=(0, KB), rows=(0, BS)):
    def group(i, c):
        at = pl.ds(pl.multiple_of(i * 16, 16), 16)
        parts = [read(k, at).astype(F32) for k in range(KB)]
        for l in range(*cols):
            total = None
            for k in range(KB):
                row = b_ref[l, k : k + 1, :] if back else b_ref[k, l : l + 1, :]
                term = parts[k] * row
                total = term if total is None else total + term
            write(l, at, total)
        return c

    lax.fori_loop(rows[0] // 16, rows[1] // 16, group, 0)


def row_factor(wide):
    return lax.rsqrt(jnp.mean(wide * wide, axis=-1, keepdims=True) + EPSILON)


def step_kernel(n, refs):
    hn = n // 2
    each = chunk_rows(n)
    core = lax.axis_index("section")
    chip = lax.axis_index("seq")
    half = chip // hn
    k_me = lax.rem(chip, hn)
    me = core * hn + k_me
    own = core == half
    partner_chip = lax.rem(chip + hn, n)
    partner = {"section": core, "seq": partner_chip}
    other = {"section": 1 - core, "seq": chip}
    rows = refs["sin"].shape[0]
    pad = rows // n
    x0, x1, e1, dx1 = refs["x0"], refs["x1"], refs["e"], refs["dx"]
    w, vo, go, gain = refs["w"], refs["vo"], refs["go"], refs["gain_s"]
    sins, sxs = refs["sins"], refs["sxs"]
    hid, mid, val, gat, mix = (refs[name] for name in ("h", "t", "v", "g", "s"))
    flat, es = refs["flat"], refs["es"]
    last, final = refs["last"], refs["final"]
    upv, upg, dt, dh = refs["upv"], refs["upg"], refs["dt"], refs["dh"]

    def piece_of_fields(r):
        at = pl.ds(r * (BS // HEAD), BS // HEAD)
        return pltpu.make_async_copy(
            refs["fields"].at[:, at], refs[f"fv{r}"], refs["lx"].at[r]
        )

    def own_cotangent():
        return pltpu.make_async_copy(refs["cotangent"].at[half], e1, refs["le"])

    def weight_parts():
        left, right = pl.ds(0, WB), pl.ds(WB, WB)
        return [
            (refs["vin"], w.at[core, :, :, left]),
            (refs["gin"], w.at[core, :, :, right]),
            (refs["vout"], refs["vraw"].at[core]),
            (refs["gout"], refs["graw"].at[core]),
            (refs["gain"], gain.at[core]),
        ]

    def weight_parts_of(sec):
        left, right = pl.ds(0, WB), pl.ds(WB, WB)
        return [
            (refs["vin"], w.at[sec, :, :, left]),
            (refs["gin"], w.at[sec, :, :, right]),
            (refs["vout"], refs["vraw"].at[sec]),
            (refs["gout"], refs["graw"].at[sec]),
            (refs["gain"], gain.at[sec]),
        ]

    @pl.when(own)
    def _():
        for r in range(HEAD):
            piece_of_fields(r).start()

    for j, (src, dst) in enumerate(weight_parts()):
        pltpu.make_async_copy(src, dst, refs["lw"].at[j]).start()

    barrier = pltpu.get_barrier_semaphore()

    def greet(d, c):
        pl.semaphore_signal(
            barrier, inc=1, device_id=in_half(n, lax.rem(me + d, n)), device_id_type=MESH
        )
        return c

    lax.fori_loop(1, n, greet, 0)
    for number in range(2):
        pl.semaphore_signal(
            barrier, inc=1, device_id={"section": number, "seq": partner_chip}, device_id_type=MESH
        )

    wide = dot(refs["sout"][...], copies(n, rows, pad), 1, 0).astype(BF16)
    placed = dot(by_place(n, rows), wide, 1, 0)
    refs["sxmine"][...] = jnp.where(same_place(rows, pad), placed, 0.0).astype(BF16)

    pl.semaphore_wait(barrier, n + 1)

    def x_copy(r):
        at = pl.ds(r * (BS // HEAD), BS // HEAD)
        return remote(
            refs["xs"].at[at], x0.at[at], refs["xsem"].at[0, r], refs["xsem"].at[1, r], partner
        )

    def weight_copies(sec):
        return [
            remote(src, dst, refs["wsem"].at[0, j], refs["wsem"].at[1, j], other)
            for j, (src, dst) in enumerate(weight_parts_of(sec))
        ]

    def seq_copies(sec, device, row):
        return [
            remote(
                refs[src], refs[dst].at[sec], refs["ssem"].at[0, row, j],
                refs["ssem"].at[1, sec, j], device,
            )
            for j, (src, dst) in enumerate((("sin", "sins"), ("sxmine", "sxs")))
        ]

    for copy in weight_copies(core):
        copy.start()
    for copy in seq_copies(core, {"section": half, "seq": partner_chip}, 0):
        copy.start()

    @pl.when(own)
    def _():
        sins[core] = refs["sin"][...]
        sxs[core] = refs["sxmine"][...]
        mine, theirs = refs["assignment"][half], refs["assignment"][1 - half]
        for r in range(HEAD):
            at = slice(r * (BS // HEAD), (r + 1) * (BS // HEAD))
            piece_of_fields(r).wait()
            refs["xs"][at, :] = refs[f"fv{r}"][theirs]
            x_copy(r).start()
            x0[at, :] = refs[f"fv{r}"][mine]
        own_cotangent().start()

    @pl.when(jnp.logical_not(own))
    def _():
        for copy in seq_copies(core, other, 1):
            copy.start()

    def wait_weights(sec):
        @pl.when(core == sec)
        def _():
            for j, (src, dst) in enumerate(weight_parts()):
                pltpu.make_async_copy(src, dst, refs["lw"].at[j]).wait()

        @pl.when(core != sec)
        def _():
            for copy in weight_copies(sec):
                copy.wait_recv()

        vo[sec] = refs["vraw"][sec].astype(F32)
        go[sec] = refs["graw"][sec].astype(F32)

    def wait_seq(sec):
        @pl.when(jnp.logical_not(own & (core == sec)))
        def _():
            for copy in seq_copies(sec, other, 0):
                copy.wait_recv()

    def front(sec, x_ref, low, high):
        at = slice(low, high)
        factor = row_factor(x_ref[at, :].astype(F32))
        for k in range(KB):
            cols = slice(k * WB, (k + 1) * WB)
            hidden = (
                x_ref[at, cols].astype(F32) * factor * gain[sec, k : k + 1, :]
            ).astype(BF16)
            hid[sec, at, cols] = hidden
            mid[sec, k, at, :] = dot(hidden, w[sec, k], 1, 0).astype(BF16)

    def mixed_into(ref, sec):
        def write(l, at, value):
            ref[sec, at, l * WB : (l + 1) * WB] = value.astype(BF16)

        return write

    def values(sec, cols=(0, KB), span=(0, BS)):
        cross(
            lambda k, at: mid[sec, k, at, :WB], mixed_into(val, sec), vo.at[sec], False, cols, span
        )

    def gates(sec):
        cross(lambda k, at: mid[sec, k, at, WB:], mixed_into(gat, sec), go.at[sec], False)

    def columns(i):
        return slice(i * WIDE, (i + 1) * WIDE)

    def got(ref, i):
        return ref[i].astype(F32).reshape(rows, WIDE).astype(BF16)

    def send(value, i, ex):
        a, b, sems = ex
        a[i] = value.reshape(n, pad, WIDE).astype(BF16)
        send_all(n, me, i, a, b, sems)

    def wait(i, ex):
        a, b, sems = ex
        wait_all(n, me, i, a, b, sems)

    def exchange(a, b, call, first):
        sems = refs["ex"]
        return refs["a"].at[a], refs["b"].at[b], (sems.at[first, 0, call], sems.at[first, 1, call])

    f0 = [exchange(0, 0, 0, 0), exchange(1, 1, 1, 0)]
    f1 = [exchange(0, 2, 0, 0), exchange(1, 3, 1, 0)]
    r1 = [exchange(2, 4, 0, 1), exchange(3, 5, 1, 1)]
    r0 = [exchange(0, 6, 0, 0), exchange(1, 7, 1, 0)]

    def first_mix(sec, i, ex):
        send(dot(sins[sec], val[sec, :, columns(i)], 1, 0), i, ex[0])

    def second_mix(sec, i, ex):
        wait(i, ex[0])
        send(dot(sxs[sec], got(ex[0][1], i), 1, 0), i, ex[1])

    def finish(sec, i, ex, x_ref, out_ref):
        wait(i, ex[1])
        cols = columns(i)
        mixed = ex[1][1][i].astype(F32).reshape(rows, WIDE)
        if rows != BS:
            mixed = dot(spread_rows(n, rows), mixed.astype(BF16), 0, 0)
        mix[sec, :, cols] = mixed.astype(BF16)
        out_ref[:, cols] = (
            x_ref[:, cols].astype(F32) + mixed * gat[sec, :, cols].astype(F32)
        ).astype(BF16)

    def first_back(sec, e_ref, i, ex):
        cols = columns(i)
        ds = e_ref[:, cols].astype(F32) * gat[sec, :, cols].astype(F32)
        if rows != BS:
            ds = dot(spread_rows(n, rows), ds.astype(BF16), 1, 0)
        send(ds, i, ex[0])

    def second_back(sec, i, ex):
        wait(i, ex[0])
        send(dot(sxs[sec], got(ex[0][1], i), 0, 0), i, ex[1])

    def middle_back(first, up, b_ref):
        def write(k, at, value):
            dt[k, at, first : first + WB] = value.astype(BF16)

        cross(lambda l, at: up[at, l * WB : (l + 1) * WB], write, b_ref, True)

    def gate_back(sec, e_ref):
        for i in range(CHUNKS):
            cols = columns(i)
            dg = e_ref[:, cols].astype(F32) * mix[sec, :, cols].astype(F32)
            upg[:, cols] = dg.astype(BF16).astype(F32)
        middle_back(WB, upg, go.at[sec])

    def value_back(sec, ex):
        for i in range(CHUNKS):
            wait(i, ex[1])
            upv[:, columns(i)] = (
                dot(sins[sec], got(ex[1][1], i), 0, 0).astype(BF16).astype(F32)
            )
        middle_back(0, upv, vo.at[sec])

    def outer_grad(sec, first, up, start):
        def block(k, c):
            middle = mid[sec, k, :, first : first + WB].astype(F32)
            found = []
            for l in range(KB):
                both = middle * up[:, l * WB : (l + 1) * WB]
                found.append(jnp.sum(both, axis=0, keepdims=True))
            at = pl.ds(pl.multiple_of(start + k * KB, KB), KB)
            flat[sec, at, :] = jnp.concatenate(found, axis=0).astype(BF16)
            return c

        lax.fori_loop(0, KB, block, 0)

    def inner_grad(sec):
        for k in range(KB):
            cols = slice(k * WB, (k + 1) * WB)
            pair = dot(hid[sec, :, cols], dt[k], 0, 0).astype(BF16)
            flat[sec, cols, :] = pair[:, :WB]
            flat[sec, D + k * WB : D + (k + 1) * WB, :] = pair[:, WB:]

    def hidden_back(sec, x_ref, e_ref=None, dx_ref=None):
        factor = row_factor(x_ref[...].astype(F32))
        lean = jnp.zeros((BS, WB), F32)
        gains = []
        for k in range(KB):
            cols = slice(k * WB, (k + 1) * WB)
            part = dot(dt[k], w[sec, k], 1, 1)
            seen = part * x_ref[:, cols].astype(F32)
            gains.append(jnp.sum(seen * factor, axis=0, keepdims=True))
            if dx_ref is not None:
                lean += gain[sec, k : k + 1, :] * seen
                dh[:, cols] = gain[sec, k : k + 1, :] * part
        flat[sec, USED : USED + KB, :] = jnp.concatenate(gains, axis=0).astype(BF16)
        left = n * each - USED - KB
        if left:
            flat[sec, USED + KB :, :] = jnp.zeros((left, WB), BF16)
        if dx_ref is None:
            return
        mean = jnp.sum(lean, axis=-1, keepdims=True) * (1.0 / D)
        pull = factor * factor * factor * mean
        for k in range(KB):
            cols = slice(k * WB, (k + 1) * WB)
            dx_ref[:, cols] = (
                e_ref[:, cols].astype(F32)
                + factor * dh[:, cols]
                - x_ref[:, cols].astype(F32) * pull
            ).astype(BF16)

    def seq_outer_grad(sec, fwd, back):
        pairs = jnp.zeros((rows, rows), F32)
        for i in range(CHUNKS):
            pairs += dot(got(back[0][1], i), got(fwd[0][1], i), 1, 1)
        kept = jnp.where(same_place(rows, pad), pairs, 0.0).astype(BF16)
        moved = dot(by_place(n, rows), kept, 0, 0).astype(BF16)
        es[sec, rows:, :] = dot(moved, copies(BS, rows, pad), 1, 1).astype(BF16)

    def seq_inner_grad(sec, back):
        inner = jnp.zeros((rows, BS), F32)
        for i in range(CHUNKS):
            inner += dot(got(back[1][1], i), val[sec, :, columns(i)], 1, 1)
        es[sec, :rows, :] = inner.astype(BF16)

    def width(start):
        return pl.ds(pl.multiple_of(start, 16), each)

    def across(sec, d):
        kk = lax.rem(k_me + d, hn)
        return remote(
            flat.at[sec, width(((1 - core) * hn + kk) * each)], refs["came"].at[sec, kk],
            refs["csem"].at[0, sec, d], refs["csem"].at[1, sec, d], other,
        )

    def arrived(sec, d):
        kk = lax.rem(k_me + d, hn)
        return remote(
            flat.at[sec, width(((1 - core) * hn + kk) * each)], refs["came"].at[sec, kk],
            refs["csem"].at[0, sec, d], refs["csem"].at[1, sec, d], other,
        )

    def in_core(kk):
        return {"section": core, "seq": half * hn + kk}

    def sum_cores(sec):
        def one(d, c):
            across(sec, d).start()
            return c

        lax.fori_loop(0, hn, one, 0)

    def sum_scatter(sec):
        def one(j, c):
            d = lax.rem(j + 1, hn)
            kk = lax.rem(k_me + d, hn)
            arrived(sec, d).wait_recv()
            at = width((core * hn + kk) * each)
            total = flat[sec, at, :].astype(F32) + refs["came"][sec, kk].astype(F32)
            flat[sec, at, :] = total.astype(BF16)

            @pl.when(d != 0)
            def _():
                remote(
                    flat.at[sec, at], refs["land"].at[sec, k_me], refs["rsem"].at[0, sec],
                    refs["rsem"].at[1, sec], in_core(kk),
                ).start()

            return c

        lax.fori_loop(0, hn, one, 0)
        refs["land"][sec, k_me] = flat[sec, width((core * hn + k_me) * each), :]

    def partner_copy(sec):
        return remote(
            refs["part"].at[sec], refs["came_part"].at[sec], refs["psem"].at[0, sec],
            refs["psem"].at[1, sec], partner,
        )

    def sum_partner(sec):
        others = pl.ds(0, hn - 1)
        copy = remote(
            refs["land"].at[sec, others], refs["land"].at[sec, others], refs["rsem"].at[0, sec],
            refs["rsem"].at[1, sec], in_core(lax.rem(k_me + 1, hn)),
        )
        copy.wait_send()
        copy.wait_recv()
        total = refs["land"][sec, 0].astype(F32)
        for q in range(1, hn):
            total = total + refs["land"][sec, q].astype(F32)
        refs["part"][sec] = total.astype(BF16)
        partner_copy(sec).start()

    def gather_copy(sec, kk):
        return remote(
            refs["mine"].at[sec], refs["full"].at[me], refs["gsem"].at[0, sec],
            refs["gsem"].at[1, sec], {"section": sec, "seq": half * hn + kk},
        )

    def sum_gather(sec):
        copy = partner_copy(sec)
        copy.wait_send()
        copy.wait_recv()
        total = refs["part"][sec].astype(F32) + refs["came_part"][sec].astype(F32)
        refs["mine"][sec] = total.astype(BF16)

        def one(d, c):
            gather_copy(sec, lax.rem(k_me + d, hn)).start()
            return c

        lax.fori_loop(1, hn, one, 0)

        @pl.when(core != sec)
        def _():
            gather_copy(sec, k_me).start()

        @pl.when(core == sec)
        def _():
            refs["full"][me] = refs["mine"][sec]

    def sum_finish(sec):
        def cross_sent(d, c):
            across(sec, d).wait_send()
            return c

        lax.fori_loop(0, hn, cross_sent, 0)

        def several(count):
            some = pl.ds(0, count)
            return remote(
                refs["full"].at[some], refs["full"].at[some], refs["gsem"].at[0, sec],
                refs["gsem"].at[1, sec], partner,
            )

        @pl.when(core != sec)
        def _():
            several(hn).wait_send()

        @pl.when(core == sec)
        def _():
            several(hn - 1).wait_send()
            several(n - 1).wait_recv()

    def es_copy(sec):
        return remote(
            es.at[sec], refs["es_came"].at[sec], refs["esem"].at[0, sec],
            refs["esem"].at[1, sec], partner,
        )

    def es_over(sec):
        return remote(
            refs["es_sum"], refs["es_got"], refs["osem"].at[0], refs["osem"].at[1], other
        )

    def es_start(sec):
        @pl.when(jnp.logical_not(own))
        def _():
            es_copy(sec).start()

    def es_total(sec):
        @pl.when(own)
        def _():
            es_copy(sec).wait_recv()
            total = es[sec].astype(F32) + refs["es_came"][sec].astype(F32)

            @pl.when(core == sec)
            def _():
                refs["es_out"][...] = total

            @pl.when(core != sec)
            def _():
                refs["es_sum"][...] = total
                es_over(sec).start()

        @pl.when(jnp.logical_not(own))
        def _():
            es_copy(sec).wait_send()

    def es_end():
        @pl.when(own)
        def _():
            es_over(0).wait_send()

        @pl.when(jnp.logical_not(own))
        def _():
            es_over(0).wait_recv()
            refs["es_out"][...] = refs["es_got"][...]

    wait_weights(0)
    for r in range(HEAD):
        low, high = r * (BS // HEAD), (r + 1) * (BS // HEAD)

        @pl.when(jnp.logical_not(own))
        def _():
            x_copy(r).wait_recv()

        front(0, x0, low, high)
        values(0, span=(low, high))
    wait_seq(0)
    for i in range(CHUNKS):
        first_mix(0, i, f0)
    gates(0)
    wait_weights(1)
    wait_seq(1)

    def e_copy():
        return remote(
            refs["cotangent"].at[1 - half], e1, refs["ysem"].at[0], refs["ysem"].at[1], partner
        )

    @pl.when(own)
    def _():
        for r in range(HEAD):
            x_copy(r).wait_send()
        e_copy().start()

    for i in range(CHUNKS):
        second_mix(0, i, f0)
    for i in range(CHUNKS):
        finish(0, i, f0, x0, x1)

    front(1, x1, 0, BS)
    for i in range(CHUNKS):
        each_l = KB // CHUNKS
        values(1, cols=(i * each_l, (i + 1) * each_l))
        first_mix(1, i, f1)
    gates(1)

    @pl.when(own)
    def _():
        own_cotangent().wait()

    @pl.when(jnp.logical_not(own))
    def _():
        e_copy().wait_recv()

    for i in range(CHUNKS):
        first_back(1, e1, i, r1)
    for i in range(CHUNKS):
        second_mix(1, i, f1)
    for i in range(CHUNKS):
        second_back(1, i, r1)
    for i in range(CHUNKS):
        finish(1, i, f1, x1, last)

    def fin_home():
        return remote(
            last, final.at[half], refs["fsem"].at[0, 0], refs["fsem"].at[1, 0], partner
        )

    def fin_core(m, j):
        return remote(
            final.at[m], final.at[m], refs["fsem"].at[0, j], refs["fsem"].at[1, j], other
        )

    @pl.when(jnp.logical_not(own))
    def _():
        fin_home().start()

    @pl.when(own)
    def _():
        final[half] = last[...]
        fin_core(half, 1).start()

    gate_back(1, e1)
    value_back(1, r1)
    hidden_back(1, x1, e1, dx1)

    for i in range(CHUNKS):
        first_back(0, dx1, i, r0)
    outer_grad(1, WB, upg, 2 * D + KB * KB)
    outer_grad(1, 0, upv, 2 * D)
    inner_grad(1)
    sum_cores(1)
    seq_outer_grad(1, f1, r1)
    seq_inner_grad(1, r1)
    es_start(1)
    for i in range(CHUNKS):
        second_back(0, i, r0)
    sum_scatter(1)
    gate_back(0, dx1)
    outer_grad(0, WB, upg, 2 * D + KB * KB)
    seq_outer_grad(0, f0, r0)
    value_back(0, r0)
    sum_partner(1)
    outer_grad(0, 0, upv, 2 * D)
    inner_grad(0)
    hidden_back(0, x0)
    sum_cores(0)
    sum_gather(1)
    seq_inner_grad(0, r0)
    es_start(0)
    sum_scatter(0)
    es_total(1)

    @pl.when(own)
    def _():
        e_copy().wait_send()
        fin_core(half, 1).wait_send()
        remote(
            last, final.at[1 - half], refs["fsem"].at[0, 0], refs["fsem"].at[1, 0], partner
        ).wait_recv()
        fin_core(1 - half, 2).start()

    @pl.when(jnp.logical_not(own))
    def _():
        fin_home().wait_send()

    sum_partner(0)
    sum_finish(1)
    sum_gather(0)
    es_total(0)
    es_end()

    @pl.when(own)
    def _():
        fin_core(1 - half, 2).wait_send()

    @pl.when(jnp.logical_not(own))
    def _():
        fin_core(half, 1).wait_recv()
        fin_core(1 - half, 2).wait_recv()
        for copy in seq_copies(core, other, 1):
            copy.wait_send()

    for copy in weight_copies(core):
        copy.wait_send()
    for copy in seq_copies(core, {"section": half, "seq": partner_chip}, 0):
        copy.wait_send()
    sum_finish(0)


INPUTS = (
    "fields", "cotangent", "assignment", "gain", "vin", "vout", "gin", "gout", "sin", "sout",
)
OUTPUTS = ("final", "full", "es_out")


def scratch(n, rows):
    pad = rows // n
    each = chunk_rows(n)
    hn = n // 2
    vmem, dma = pltpu.VMEM, pltpu.SemaphoreType.DMA
    plane = (BS, D)
    return {
        **{f"fv{r}": vmem((8, BS // HEAD, D), BF16) for r in range(HEAD)},
        "xs": vmem(plane, BF16),
        "x0": vmem(plane, BF16),
        "x1": vmem(plane, BF16),
        "e": vmem(plane, BF16),
        "dx": vmem(plane, BF16),
        "last": vmem(plane, BF16),
        "w": vmem((2, KB, WB, 2 * WB), BF16),
        "vraw": vmem((2, KB, KB, WB), BF16),
        "graw": vmem((2, KB, KB, WB), BF16),
        "vo": vmem((2, KB, KB, WB), F32),
        "go": vmem((2, KB, KB, WB), F32),
        "gain_s": vmem((2, KB, WB), F32),
        "sxmine": vmem((rows, rows), BF16),
        "sins": vmem((2, rows, BS), BF16),
        "sxs": vmem((2, rows, rows), BF16),
        "h": vmem((2, BS, D), BF16),
        "t": vmem((2, KB, BS, 2 * WB), BF16),
        "v": vmem((2, BS, D), BF16),
        "g": vmem((2, BS, D), BF16),
        "s": vmem((2, BS, D), BF16),
        "a": vmem((4, CHUNKS, n, pad, WIDE), BF16),
        "b": vmem((8, CHUNKS, n, pad, WIDE), BF16),
        "upv": vmem(plane, F32),
        "upg": vmem(plane, F32),
        "dt": vmem((KB, BS, 2 * WB), BF16),
        "dh": vmem(plane, F32),
        "flat": vmem((2, n * each, WB), BF16),
        "came": vmem((2, hn, each, WB), BF16),
        "land": vmem((2, hn, each, WB), BF16),
        "part": vmem((2, each, WB), BF16),
        "came_part": vmem((2, each, WB), BF16),
        "mine": vmem((2, each, WB), BF16),
        "es": vmem((2, rows + BS, BS), BF16),
        "es_came": vmem((2, rows + BS, BS), BF16),
        "es_sum": vmem((rows + BS, BS), F32),
        "es_got": vmem((rows + BS, BS), F32),
        "lx": dma((HEAD,)),
        "le": dma,
        "lw": dma((5,)),
        "xsem": dma((2, HEAD)),
        "wsem": dma((2, 5)),
        "ssem": dma((2, 2, 2)),
        "ysem": dma((2,)),
        "ex": dma((2, 2, 2, CHUNKS)),
        "csem": dma((2, 2, hn)),
        "rsem": dma((2, 2)),
        "psem": dma((2, 2)),
        "gsem": dma((2, 2)),
        "esem": dma((2, 2)),
        "osem": dma((2,)),
        "fsem": dma((2, 3)),
    }


def step(n, *args):
    rows = args[INPUTS.index("sin")].shape[0]
    whole = scratch(n, rows)
    names = INPUTS + OUTPUTS + tuple(whole)
    anywhere = pl.BlockSpec(memory_space=pl.ANY)
    vmem = pl.BlockSpec(memory_space=pltpu.VMEM)
    places = {"sin": vmem, "sout": vmem, "assignment": pl.BlockSpec(memory_space=pltpu.SMEM)}

    def kernel(*refs):
        step_kernel(n, dict(zip(names, refs)))

    return pl.pallas_call(
        kernel,
        out_shape=(
            jax.ShapeDtypeStruct((2, BS, D), BF16),
            jax.ShapeDtypeStruct((n, chunk_rows(n), WB), BF16),
            jax.ShapeDtypeStruct((rows + BS, BS), F32),
        ),
        in_specs=[places.get(name, anywhere) for name in INPUTS],
        out_specs=(vmem,) * len(OUTPUTS),
        scratch_shapes=list(whole.values()),
        compiler_params=pltpu.CompilerParams(
            collective_id=0, has_side_effects=True, vmem_limit_bytes=60 * 2**20
        ),
        name="whole_step",
    )(*args)


def on_device(
    fields, cotangent, assignment, norm_gain, value_inner, value_outer,
    gate_inner, gate_outer, seq_inner, seq_outer,
):
    n = lax.axis_size("seq")
    each = BS // n
    pad = max(each, 8)
    rows = n * pad
    sin = jnp.pad(seq_inner[0].reshape(n, each, BS), ((0, 0), (0, pad - each), (0, 0)))
    final, full, es = step(
        n, fields, cotangent, assignment, norm_gain[0].reshape(KB, WB), value_inner[0],
        value_outer[0], gate_inner[0], gate_outer[0], sin.reshape(rows, BS),
        seq_outer[0].reshape(BS, n),
    )
    flat = full.reshape(-1, WB)

    def part(low, high):
        return flat[low:high].astype(F32)

    two = 2 * D
    small = KB * KB
    return (
        final,
        part(USED, USED + KB).reshape(1, D),
        part(0, D).reshape(1, KB, WB, WB),
        part(two, two + small).reshape(1, KB, KB, WB),
        part(D, two).reshape(1, KB, WB, WB),
        part(two + small, USED).reshape(1, KB, KB, WB),
        es[:rows].reshape(n, pad, BS)[:, :each].reshape(1, 1, BS, BS),
        es[rows:, :n].reshape(1, each, n, n),
    )


def solution(mesh):
    in_specs = (
        P(None, "seq", None),
        P(None, "seq", None),
        P(),
        P("section", None),
        P("section", None, None, None),
        P("section", None, None, None),
        P("section", None, None, None),
        P("section", None, None, None),
        P("section", "seq", None, None),
        P("section", "seq", None, None),
    )
    out_specs = (
        P(None, "seq", None),
        P("section", None),
        P("section", None, None, None),
        P("section", None, None, None),
        P("section", None, None, None),
        P("section", None, None, None),
        P("section", "seq", None, None),
        P("section", "seq", None, None),
    )
    return jax.shard_map(
        on_device, mesh=mesh, in_specs=in_specs, out_specs=out_specs, check_vma=False
    )
```

```python
import functools

import jax
import jax.numpy as jnp
from jax import lax
from jax.experimental import pallas as pl
from jax.experimental.pallas import tpu as pltpu
from jax.sharding import PartitionSpec as P

D = 2048
WB = 128
BS = 128
KB = 16
EPSILON = 1e-06
F32 = jnp.float32
BF16 = jnp.bfloat16
MESH = pl.DeviceIdType.MESH
WIDE = 512
CHUNKS = D // WIDE
HEAD = 4
OUTER = KB * KB
PARTS = (D + OUTER, D + OUTER + KB)


def dot(a, b, ca, cb):
    return lax.dot_general(a, b, (((ca,), (cb,)), ((), ())), preferred_element_type=F32)


def chunk_rows(n):
    return [-(-count // (16 * n)) * 16 for count in PARTS]


def remote(src, dst, send, recv, device):
    return pltpu.make_async_remote_copy(
        src_ref=src, dst_ref=dst, send_sem=send, recv_sem=recv,
        device_id=device, device_id_type=MESH,
    )


def in_half(n, block):
    half = lax.axis_index("seq") // (n // 2)
    return {"section": block // (n // 2), "seq": half * (n // 2) + lax.rem(block, n // 2)}


def send_all(n, me, i, src, dst, sems):
    def one(d, c):
        peer = lax.rem(me + d, n)
        remote(
            src.at[i, peer], dst.at[i, me], sems[0].at[i], sems[1].at[i], in_half(n, peer)
        ).start()
        return c

    lax.fori_loop(1, n, one, 0)
    dst[i, me] = src[i, me]


def wait_all(n, me, i, src, dst, sems):
    others = pl.ds(0, n - 1)
    copy = remote(
        src.at[i, others], dst.at[i, others], sems[0].at[i], sems[1].at[i],
        in_half(n, lax.rem(me + 1, n)),
    )
    copy.wait_send()
    copy.wait_recv()


def copies(count, rows, pad):
    at = lax.broadcasted_iota(jnp.int32, (count, rows), 0)
    to = lax.broadcasted_iota(jnp.int32, (count, rows), 1)
    return jnp.where(to // pad == at, 1.0, 0.0).astype(BF16)


def same_place(rows, pad):
    at = lax.broadcasted_iota(jnp.int32, (rows, rows), 0)
    to = lax.broadcasted_iota(jnp.int32, (rows, rows), 1)
    return at % pad == to % pad


def by_place(n, rows):
    pad = rows // n
    at = lax.broadcasted_iota(jnp.int32, (rows, BS), 0)
    to = lax.broadcasted_iota(jnp.int32, (rows, BS), 1)
    hit = (at % pad * n + at // pad == to) & (at % pad < BS // n)
    return jnp.where(hit, 1.0, 0.0).astype(BF16)


def spread_rows(n, rows):
    pad = rows // n
    each = BS // n
    at = lax.broadcasted_iota(jnp.int32, (rows, BS), 0)
    to = lax.broadcasted_iota(jnp.int32, (rows, BS), 1)
    hit = (at // pad * each + at % pad == to) & (at % pad < each)
    return jnp.where(hit, 1.0, 0.0).astype(BF16)


def cross(read, write, b_ref, back, cols=(0, KB), rows=(0, BS)):
    def group(i, c):
        at = pl.ds(pl.multiple_of(i * 16, 16), 16)
        parts = [read(k, at).astype(F32) for k in range(KB)]
        for l in range(*cols):
            total = None
            for k in range(KB):
                row = b_ref[l, k : k + 1, :] if back else b_ref[k, l : l + 1, :]
                term = parts[k] * row
                total = term if total is None else total + term
            write(l, at, total)
        return c

    lax.fori_loop(rows[0] // 16, rows[1] // 16, group, 0)


def row_factor(wide):
    return lax.rsqrt(jnp.mean(wide * wide, axis=-1, keepdims=True) + EPSILON)


def step_kernel(n, refs):
    hn = n // 2
    each = chunk_rows(n)
    core = lax.axis_index("section")
    chip = lax.axis_index("seq")
    half = chip // hn
    k_me = lax.rem(chip, hn)
    me = core * hn + k_me
    own = core == half
    partner_chip = lax.rem(chip + hn, n)
    partner = {"section": core, "seq": partner_chip}
    foreign = {"section": half, "seq": partner_chip}
    other = {"section": 1 - core, "seq": chip}
    rows = refs["sin"].shape[0]
    pad = rows // n
    x0, x1, e1, dx1 = refs["x0"], refs["x1"], refs["e"], refs["dx"]
    w, vo, go, gain = refs["w"], refs["vo"], refs["go"], refs["gain_s"]
    sins, sxs = refs["sins"], refs["sxs"]
    hid, mid, val, gat, mix = (refs[name] for name in ("h", "t", "v", "g", "s"))
    flat, es = (refs["flat0"], refs["flat1"]), refs["es"]
    last, final = refs["last"], refs["final"]
    upv, upg, dt, dh = refs["upv"], refs["upg"], refs["dt"], refs["dh"]

    def piece_of_fields(r):
        at = pl.ds(r * (BS // HEAD), BS // HEAD)
        return pltpu.make_async_copy(
            refs["fields"].at[:, at], refs[f"fv{r}"], refs["lx"].at[r]
        )

    def own_cotangent():
        return pltpu.make_async_copy(refs["cotangent"].at[half], e1, refs["le"])

    def weight_parts():
        left, right = pl.ds(0, WB), pl.ds(WB, WB)
        return [
            (refs["vin"], w.at[core, :, :, left]),
            (refs["gin"], w.at[core, :, :, right]),
            (refs["vout"], refs["vraw"].at[core]),
            (refs["gout"], refs["graw"].at[core]),
            (refs["gain"], gain.at[core]),
        ]

    def weight_parts_of(sec):
        left, right = pl.ds(0, WB), pl.ds(WB, WB)
        return [
            (refs["vin"], w.at[sec, :, :, left]),
            (refs["gin"], w.at[sec, :, :, right]),
            (refs["vout"], refs["vraw"].at[sec]),
            (refs["gout"], refs["graw"].at[sec]),
            (refs["gain"], gain.at[sec]),
        ]

    @pl.when(own)
    def _():
        for r in range(HEAD):
            piece_of_fields(r).start()

    @pl.when(jnp.logical_not(own))
    def _():
        for r in range(HEAD // 2, HEAD):
            piece_of_fields(r).start()

    for j, (src, dst) in enumerate(weight_parts()):
        pltpu.make_async_copy(src, dst, refs["lw"].at[j]).start()

    barrier = pltpu.get_barrier_semaphore()

    def greet(d, c):
        pl.semaphore_signal(
            barrier, inc=1, device_id=in_half(n, lax.rem(me + d, n)), device_id_type=MESH
        )
        return c

    lax.fori_loop(1, n, greet, 0)
    for number in range(2):
        pl.semaphore_signal(
            barrier, inc=1, device_id={"section": number, "seq": partner_chip}, device_id_type=MESH
        )

    wide = dot(refs["sout"][...], copies(n, rows, pad), 1, 0).astype(BF16)
    placed = dot(by_place(n, rows), wide, 1, 0)
    refs["sxmine"][...] = jnp.where(same_place(rows, pad), placed, 0.0).astype(BF16)

    pl.semaphore_wait(barrier, n + 1)

    def x_copy(r):
        at = pl.ds(r * (BS // HEAD), BS // HEAD)
        return remote(
            refs["xs"].at[at], x0.at[at], refs["xsem"].at[0, r], refs["xsem"].at[1, r], foreign
        )

    def weight_copies(sec):
        return [
            remote(src, dst, refs["wsem"].at[0, j], refs["wsem"].at[1, j], other)
            for j, (src, dst) in enumerate(weight_parts_of(sec))
        ]

    def seq_copies(sec, device, row):
        return [
            remote(
                refs[src], refs[dst].at[sec], refs["ssem"].at[0, row, j],
                refs["ssem"].at[1, sec, j], device,
            )
            for j, (src, dst) in enumerate((("sin", "sins"), ("sxmine", "sxs")))
        ]

    mine, theirs = refs["assignment"][half], refs["assignment"][1 - half]

    def rows_of(r):
        return slice(r * (BS // HEAD), (r + 1) * (BS // HEAD))

    def send_x(r):
        refs["xs"][rows_of(r), :] = refs[f"fv{r}"][theirs]
        x_copy(r).start()

    @pl.when(own)
    def _():
        for r in range(HEAD):
            piece_of_fields(r).wait()
            if r < HEAD // 2:
                send_x(r)

    @pl.when(jnp.logical_not(own))
    def _():
        for r in range(HEAD // 2, HEAD):
            piece_of_fields(r).wait()
            send_x(r)

    for copy in weight_copies(core):
        copy.start()
    for copy in seq_copies(core, foreign, 0):
        copy.start()

    @pl.when(own)
    def _():
        sins[core] = refs["sin"][...]
        sxs[core] = refs["sxmine"][...]
        own_cotangent().start()
        for r in range(HEAD):
            x0[rows_of(r), :] = refs[f"fv{r}"][mine]

    @pl.when(jnp.logical_not(own))
    def _():
        for copy in seq_copies(core, other, 1):
            copy.start()

    def wait_weights(sec):
        @pl.when(core == sec)
        def _():
            for j, (src, dst) in enumerate(weight_parts()):
                pltpu.make_async_copy(src, dst, refs["lw"].at[j]).wait()

        @pl.when(core != sec)
        def _():
            for copy in weight_copies(sec):
                copy.wait_recv()

        vo[sec] = refs["vraw"][sec].astype(F32)
        go[sec] = refs["graw"][sec].astype(F32)

    def wait_seq(sec):
        @pl.when(jnp.logical_not(own & (core == sec)))
        def _():
            for copy in seq_copies(sec, other, 0):
                copy.wait_recv()

    def front(sec, x_ref, low, high):
        at = slice(low, high)
        factor = row_factor(x_ref[at, :].astype(F32))
        for k in range(KB):
            cols = slice(k * WB, (k + 1) * WB)
            hidden = (
                x_ref[at, cols].astype(F32) * factor * gain[sec, k : k + 1, :]
            ).astype(BF16)
            hid[sec, at, cols] = hidden
            mid[sec, k, at, :] = dot(hidden, w[sec, k], 1, 0).astype(BF16)

    def mixed_into(ref, sec):
        def write(l, at, value):
            ref[sec, at, l * WB : (l + 1) * WB] = value.astype(BF16)

        return write

    def values(sec, cols=(0, KB), span=(0, BS)):
        cross(
            lambda k, at: mid[sec, k, at, :WB], mixed_into(val, sec), vo.at[sec], False, cols, span
        )

    def gates(sec):
        cross(lambda k, at: mid[sec, k, at, WB:], mixed_into(gat, sec), go.at[sec], False)

    def columns(i):
        return slice(i * WIDE, (i + 1) * WIDE)

    def got(ref, i):
        return ref[i].astype(F32).reshape(rows, WIDE).astype(BF16)

    def send(value, i, ex):
        a, b, sems = ex
        a[i] = value.reshape(n, pad, WIDE).astype(BF16)
        send_all(n, me, i, a, b, sems)

    def wait(i, ex):
        a, b, sems = ex
        wait_all(n, me, i, a, b, sems)

    def exchange(a, b, call, first):
        sems = refs["ex"]
        return refs["a"].at[a], refs["b"].at[b], (sems.at[first, 0, call], sems.at[first, 1, call])

    f0 = [exchange(0, 0, 0, 0), exchange(1, 1, 1, 0)]
    f1 = [exchange(0, 2, 0, 0), exchange(1, 3, 1, 0)]
    r1 = [exchange(2, 4, 0, 1), exchange(3, 5, 1, 1)]
    r0 = [exchange(0, 6, 0, 0), exchange(1, 7, 1, 0)]

    def first_mix(sec, i, ex):
        send(dot(sins[sec], val[sec, :, columns(i)], 1, 0), i, ex[0])

    def second_mix(sec, i, ex):
        wait(i, ex[0])
        send(dot(sxs[sec], got(ex[0][1], i), 1, 0), i, ex[1])

    def finish(sec, i, ex, x_ref, out_ref):
        wait(i, ex[1])
        cols = columns(i)
        mixed = ex[1][1][i].astype(F32).reshape(rows, WIDE)
        if rows != BS:
            mixed = dot(spread_rows(n, rows), mixed.astype(BF16), 0, 0)
        mix[sec, :, cols] = mixed.astype(BF16)
        out_ref[:, cols] = (
            x_ref[:, cols].astype(F32) + mixed * gat[sec, :, cols].astype(F32)
        ).astype(BF16)

    def first_back(sec, e_ref, i, ex):
        cols = columns(i)
        ds = e_ref[:, cols].astype(F32) * gat[sec, :, cols].astype(F32)
        if rows != BS:
            ds = dot(spread_rows(n, rows), ds.astype(BF16), 1, 0)
        send(ds, i, ex[0])

    def second_back(sec, i, ex):
        wait(i, ex[0])
        send(dot(sxs[sec], got(ex[0][1], i), 0, 0), i, ex[1])

    def middle_back(first, up, b_ref):
        def write(k, at, value):
            dt[k, at, first : first + WB] = value.astype(BF16)

        cross(lambda l, at: up[at, l * WB : (l + 1) * WB], write, b_ref, True)

    def gate_back(sec, e_ref):
        for i in range(CHUNKS):
            cols = columns(i)
            dg = e_ref[:, cols].astype(F32) * mix[sec, :, cols].astype(F32)
            upg[:, cols] = dg.astype(BF16).astype(F32)
        middle_back(WB, upg, go.at[sec])

    def value_back(sec, ex, grads=False):
        for i in range(CHUNKS):
            wait(i, ex[1])
            upv[:, columns(i)] = (
                dot(sins[sec], got(ex[1][1], i), 0, 0).astype(BF16).astype(F32)
            )
            if grads:
                outer_grad(sec, 1, (i * KB // CHUNKS, (i + 1) * KB // CHUNKS))
        middle_back(0, upv, vo.at[sec])

    def outer_grad(sec, p, cols=(0, KB)):
        up = (upg, upv)[p]
        first = (1 - p) * WB

        def block(k, c):
            middle = mid[sec, k, :, first : first + WB].astype(F32)
            for l in range(*cols):
                both = middle * up[:, l * WB : (l + 1) * WB]
                refs["og"][pl.ds(k * KB + l, 1), :] = jnp.sum(both, axis=0, keepdims=True)
            return c

        lax.fori_loop(0, KB, block, 0)

    def inner_grad(sec, p):
        half_of = slice((1 - p) * WB, (2 - p) * WB)
        for k in range(KB):
            cols = slice(k * WB, (k + 1) * WB)
            flat[p][sec, cols, :] = dot(hid[sec, :, cols], dt[k, :, half_of], 0, 0).astype(BF16)
        flat[p][sec, D : D + OUTER, :] = refs["og"][...].astype(BF16)
        left = n * each[p] - PARTS[p]
        if left:
            flat[p][sec, PARTS[p] :, :] = jnp.zeros((left, WB), BF16)

    def hidden_back(sec, x_ref, e_ref=None, dx_ref=None):
        factor = row_factor(x_ref[...].astype(F32))
        lean = jnp.zeros((BS, WB), F32)
        gains = []
        for k in range(KB):
            cols = slice(k * WB, (k + 1) * WB)
            part = dot(dt[k], w[sec, k], 1, 1)
            seen = part * x_ref[:, cols].astype(F32)
            gains.append(jnp.sum(seen * factor, axis=0, keepdims=True))
            if dx_ref is not None:
                lean += gain[sec, k : k + 1, :] * seen
                dh[:, cols] = gain[sec, k : k + 1, :] * part
        flat[1][sec, D + OUTER : PARTS[1], :] = jnp.concatenate(gains, axis=0).astype(BF16)
        if dx_ref is None:
            return
        mean = jnp.sum(lean, axis=-1, keepdims=True) * (1.0 / D)
        pull = factor * factor * factor * mean
        for k in range(KB):
            cols = slice(k * WB, (k + 1) * WB)
            dx_ref[:, cols] = (
                e_ref[:, cols].astype(F32)
                + factor * dh[:, cols]
                - x_ref[:, cols].astype(F32) * pull
            ).astype(BF16)

    def seq_outer_grad(sec, fwd, back):
        pairs = jnp.zeros((rows, rows), F32)
        for i in range(CHUNKS):
            pairs += dot(got(back[0][1], i), got(fwd[0][1], i), 1, 1)
        kept = jnp.where(same_place(rows, pad), pairs, 0.0).astype(BF16)
        moved = dot(by_place(n, rows), kept, 0, 0).astype(BF16)
        es[sec, rows:, :] = dot(moved, copies(BS, rows, pad), 1, 1).astype(BF16)

    def seq_inner_grad(sec, back):
        inner = jnp.zeros((rows, BS), F32)
        for i in range(CHUNKS):
            inner += dot(got(back[1][1], i), val[sec, :, columns(i)], 1, 1)
        es[sec, :rows, :] = inner.astype(BF16)

    def of(name, p):
        return refs[f"{name}{p}"]

    def width(p, piece):
        return pl.ds(pl.multiple_of(piece * each[p], 16), each[p])

    def across(sec, p, d):
        kk = lax.rem(k_me + d, hn)
        return remote(
            flat[p].at[sec, width(p, (1 - core) * hn + kk)], of("came", p).at[sec, kk],
            refs["csem"].at[0, sec, p, d], refs["csem"].at[1, sec, p, d], other,
        )

    def in_core(kk):
        return {"section": core, "seq": half * hn + kk}

    def sum_cores(sec, p):
        def one(d, c):
            across(sec, p, lax.rem(d, hn)).start()
            return c

        lax.fori_loop(1, hn + 1, one, 0)

    def sum_scatter(sec, p):
        sems = (refs["rsem"].at[0, sec, p], refs["rsem"].at[1, sec, p])

        def one(j, c):
            d = lax.rem(j, hn)
            kk = lax.rem(k_me + d, hn)
            across(sec, p, d).wait_recv()
            at = width(p, core * hn + kk)
            total = flat[p][sec, at, :].astype(F32) + of("came", p)[sec, kk].astype(F32)
            flat[p][sec, at, :] = total.astype(BF16)

            @pl.when(d != 0)
            def _():
                remote(
                    flat[p].at[sec, at], of("land", p).at[sec, k_me], *sems, in_core(kk)
                ).start()

            return c

        lax.fori_loop(1, hn + 1, one, 0)
        of("land", p)[sec, k_me] = flat[p][sec, width(p, core * hn + k_me), :]

    def partner_copy(sec, p):
        return remote(
            of("part", p).at[sec], of("came_part", p).at[sec], refs["psem"].at[0, sec, p],
            refs["psem"].at[1, sec, p], partner,
        )

    def sum_partner(sec, p):
        land = of("land", p)
        others = pl.ds(0, hn - 1)
        copy = remote(
            land.at[sec, others], land.at[sec, others], refs["rsem"].at[0, sec, p],
            refs["rsem"].at[1, sec, p], in_core(lax.rem(k_me + 1, hn)),
        )
        copy.wait_send()
        copy.wait_recv()
        total = land[sec, 0].astype(F32)
        for q in range(1, hn):
            total = total + land[sec, q].astype(F32)
        of("part", p)[sec] = total.astype(BF16)
        partner_copy(sec, p).start()

    def gather_copy(sec, p, kk):
        return remote(
            of("mine", p).at[sec], of("full", p).at[me], refs["gsem"].at[0, sec, p],
            refs["gsem"].at[1, sec, p], {"section": sec, "seq": half * hn + kk},
        )

    def sum_gather(sec, p):
        copy = partner_copy(sec, p)
        copy.wait_send()
        copy.wait_recv()
        total = of("part", p)[sec].astype(F32) + of("came_part", p)[sec].astype(F32)
        of("mine", p)[sec] = total.astype(BF16)

        def one(d, c):
            gather_copy(sec, p, lax.rem(k_me + d, hn)).start()
            return c

        lax.fori_loop(1, hn, one, 0)

        @pl.when(core != sec)
        def _():
            gather_copy(sec, p, k_me).start()

        @pl.when(core == sec)
        def _():
            of("full", p)[me] = of("mine", p)[sec]

    def sum_finish(sec, p):
        def cross_sent(d, c):
            across(sec, p, d).wait_send()
            return c

        lax.fori_loop(0, hn, cross_sent, 0)

        def several(count):
            some = of("full", p).at[pl.ds(0, count)]
            return remote(
                some, some, refs["gsem"].at[0, sec, p], refs["gsem"].at[1, sec, p], partner
            )

        @pl.when(core != sec)
        def _():
            several(hn).wait_send()

        @pl.when(core == sec)
        def _():
            several(hn - 1).wait_send()
            several(n - 1).wait_recv()

    def es_copy(sec):
        return remote(
            es.at[sec], refs["es_came"].at[sec], refs["esem"].at[0, sec],
            refs["esem"].at[1, sec], partner,
        )

    def es_over(sec):
        return remote(
            refs["es_sum"], refs["es_got"], refs["osem"].at[0], refs["osem"].at[1], other
        )

    def es_start(sec):
        @pl.when(jnp.logical_not(own))
        def _():
            es_copy(sec).start()

    def es_total(sec):
        @pl.when(own)
        def _():
            es_copy(sec).wait_recv()
            total = es[sec].astype(F32) + refs["es_came"][sec].astype(F32)

            @pl.when(core == sec)
            def _():
                refs["es_out"][...] = total

            @pl.when(core != sec)
            def _():
                refs["es_sum"][...] = total
                es_over(sec).start()

        @pl.when(jnp.logical_not(own))
        def _():
            es_copy(sec).wait_send()

    def es_end():
        @pl.when(own)
        def _():
            es_over(0).wait_send()

        @pl.when(jnp.logical_not(own))
        def _():
            es_over(0).wait_recv()
            refs["es_out"][...] = refs["es_got"][...]

    wait_weights(0)
    for r in (0, 2, 1, 3):
        low, high = r * (BS // HEAD), (r + 1) * (BS // HEAD)

        @pl.when(jnp.logical_not(own))
        def _():
            x_copy(r).wait_recv()

        front(0, x0, low, high)
        values(0, span=(low, high))
    wait_seq(0)
    for i in range(CHUNKS):
        first_mix(0, i, f0)
    gates(0)
    wait_weights(1)
    wait_seq(1)

    def e_copy(j):
        at = pl.ds(j * (BS // 2), BS // 2)
        return remote(
            refs["cotangent"].at[1 - half, at], e1.at[at], refs["ysem"].at[0, j],
            refs["ysem"].at[1, j], foreign,
        )

    def send_e(j):
        for r in range(j * HEAD // 2, (j + 1) * HEAD // 2):
            x_copy(r).wait_send()
        e_copy(j).start()

    @pl.when(own)
    def _():
        send_e(0)

    @pl.when(jnp.logical_not(own))
    def _():
        send_e(1)

    for i in range(CHUNKS):
        second_mix(0, i, f0)
    for i in range(CHUNKS):
        finish(0, i, f0, x0, x1)

    front(1, x1, 0, BS)
    for i in range(CHUNKS):
        each_l = KB // CHUNKS
        values(1, cols=(i * each_l, (i + 1) * each_l))
        first_mix(1, i, f1)
    gates(1)

    @pl.when(own)
    def _():
        own_cotangent().wait()

    @pl.when(jnp.logical_not(own))
    def _():
        e_copy(0).wait_recv()
        e_copy(1).wait_recv()

    for i in range(CHUNKS):
        first_back(1, e1, i, r1)
    for i in range(CHUNKS):
        second_mix(1, i, f1)
    for i in range(CHUNKS):
        second_back(1, i, r1)
    for i in range(CHUNKS):
        finish(1, i, f1, x1, last)

    def fin_home():
        return remote(
            last, final.at[half], refs["fsem"].at[0, 0], refs["fsem"].at[1, 0], partner
        )

    def fin_core(m, j):
        return remote(
            final.at[m], final.at[m], refs["fsem"].at[0, j], refs["fsem"].at[1, j], other
        )

    @pl.when(jnp.logical_not(own))
    def _():
        fin_home().start()

    @pl.when(own)
    def _():
        final[half] = last[...]
        fin_core(half, 1).start()

    gate_back(1, e1)
    value_back(1, r1)
    hidden_back(1, x1, e1, dx1)

    for i in range(CHUNKS):
        first_back(0, dx1, i, r0)
    outer_grad(1, 0)
    inner_grad(1, 0)
    sum_cores(1, 0)
    outer_grad(1, 1)
    inner_grad(1, 1)
    sum_cores(1, 1)
    for i in range(CHUNKS):
        second_back(0, i, r0)
    sum_scatter(1, 0)
    sum_scatter(1, 1)
    gate_back(0, dx1)
    outer_grad(0, 0)
    inner_grad(0, 0)
    sum_cores(0, 0)
    sum_partner(1, 0)
    value_back(0, r0, True)
    sum_scatter(0, 0)
    sum_partner(1, 1)
    inner_grad(0, 1)
    hidden_back(0, x0)
    sum_cores(0, 1)
    sum_gather(1, 0)
    sum_partner(0, 0)
    sum_gather(1, 1)
    sum_scatter(0, 1)
    seq_outer_grad(1, f1, r1)
    seq_inner_grad(1, r1)
    es_start(1)
    seq_outer_grad(0, f0, r0)
    seq_inner_grad(0, r0)
    es_start(0)
    sum_gather(0, 0)
    es_total(1)

    @pl.when(own)
    def _():
        e_copy(0).wait_send()
        fin_core(half, 1).wait_send()
        remote(
            last, final.at[1 - half], refs["fsem"].at[0, 0], refs["fsem"].at[1, 0], partner
        ).wait_recv()
        fin_core(1 - half, 2).start()

    @pl.when(jnp.logical_not(own))
    def _():
        e_copy(1).wait_send()
        fin_home().wait_send()

    sum_partner(0, 1)
    sum_finish(1, 0)
    sum_finish(1, 1)
    sum_gather(0, 1)
    es_total(0)
    es_end()

    @pl.when(own)
    def _():
        fin_core(1 - half, 2).wait_send()

    @pl.when(jnp.logical_not(own))
    def _():
        fin_core(half, 1).wait_recv()
        fin_core(1 - half, 2).wait_recv()
        for copy in seq_copies(core, other, 1):
            copy.wait_send()

    for copy in weight_copies(core):
        copy.wait_send()
    for copy in seq_copies(core, foreign, 0):
        copy.wait_send()
    sum_finish(0, 0)
    sum_finish(0, 1)


INPUTS = (
    "fields", "cotangent", "assignment", "gain", "vin", "vout", "gin", "gout", "sin", "sout",
)
OUTPUTS = ("final", "full0", "full1", "es_out")


def scratch(n, rows):
    pad = rows // n
    each = chunk_rows(n)
    hn = n // 2
    vmem, dma = pltpu.VMEM, pltpu.SemaphoreType.DMA
    plane = (BS, D)

    def by_part(name, shape):
        return {f"{name}{p}": vmem(shape(size), BF16) for p, size in enumerate(each)}

    return {
        **{f"fv{r}": vmem((8, BS // HEAD, D), BF16) for r in range(HEAD)},
        "xs": vmem(plane, BF16),
        "x0": vmem(plane, BF16),
        "x1": vmem(plane, BF16),
        "e": vmem(plane, BF16),
        "dx": vmem(plane, BF16),
        "last": vmem(plane, BF16),
        "w": vmem((2, KB, WB, 2 * WB), BF16),
        "vraw": vmem((2, KB, KB, WB), BF16),
        "graw": vmem((2, KB, KB, WB), BF16),
        "vo": vmem((2, KB, KB, WB), F32),
        "go": vmem((2, KB, KB, WB), F32),
        "gain_s": vmem((2, KB, WB), F32),
        "sxmine": vmem((rows, rows), BF16),
        "sins": vmem((2, rows, BS), BF16),
        "sxs": vmem((2, rows, rows), BF16),
        "h": vmem((2, BS, D), BF16),
        "t": vmem((2, KB, BS, 2 * WB), BF16),
        "v": vmem((2, BS, D), BF16),
        "g": vmem((2, BS, D), BF16),
        "s": vmem((2, BS, D), BF16),
        "a": vmem((4, CHUNKS, n, pad, WIDE), BF16),
        "b": vmem((8, CHUNKS, n, pad, WIDE), BF16),
        "upv": vmem(plane, F32),
        "upg": vmem(plane, F32),
        "dt": vmem((KB, BS, 2 * WB), BF16),
        "dh": vmem(plane, F32),
        "og": vmem((OUTER, WB), F32),
        **by_part("flat", lambda size: (2, n * size, WB)),
        **by_part("came", lambda size: (2, hn, size, WB)),
        **by_part("land", lambda size: (2, hn, size, WB)),
        **by_part("part", lambda size: (2, size, WB)),
        **by_part("came_part", lambda size: (2, size, WB)),
        **by_part("mine", lambda size: (2, size, WB)),
        "es": vmem((2, rows + BS, BS), BF16),
        "es_came": vmem((2, rows + BS, BS), BF16),
        "es_sum": vmem((rows + BS, BS), F32),
        "es_got": vmem((rows + BS, BS), F32),
        "lx": dma((HEAD,)),
        "le": dma,
        "lw": dma((5,)),
        "xsem": dma((2, HEAD)),
        "wsem": dma((2, 5)),
        "ssem": dma((2, 2, 2)),
        "ysem": dma((2, 2)),
        "ex": dma((2, 2, 2, CHUNKS)),
        "csem": dma((2, 2, 2, hn)),
        "rsem": dma((2, 2, 2)),
        "psem": dma((2, 2, 2)),
        "gsem": dma((2, 2, 2)),
        "esem": dma((2, 2)),
        "osem": dma((2,)),
        "fsem": dma((2, 3)),
    }


def step(n, *args):
    rows = args[INPUTS.index("sin")].shape[0]
    whole = scratch(n, rows)
    names = INPUTS + OUTPUTS + tuple(whole)
    anywhere = pl.BlockSpec(memory_space=pl.ANY)
    vmem = pl.BlockSpec(memory_space=pltpu.VMEM)
    places = {"sin": vmem, "sout": vmem, "assignment": pl.BlockSpec(memory_space=pltpu.SMEM)}

    def kernel(*refs):
        step_kernel(n, dict(zip(names, refs)))

    return pl.pallas_call(
        kernel,
        out_shape=(
            jax.ShapeDtypeStruct((2, BS, D), BF16),
            *(jax.ShapeDtypeStruct((n, size, WB), BF16) for size in chunk_rows(n)),
            jax.ShapeDtypeStruct((rows + BS, BS), F32),
        ),
        in_specs=[places.get(name, anywhere) for name in INPUTS],
        out_specs=(vmem,) * len(OUTPUTS),
        scratch_shapes=list(whole.values()),
        compiler_params=pltpu.CompilerParams(
            collective_id=0, has_side_effects=True, vmem_limit_bytes=60 * 2**20
        ),
        name="whole_step",
    )(*args)


def on_device(
    fields, cotangent, assignment, norm_gain, value_inner, value_outer,
    gate_inner, gate_outer, seq_inner, seq_outer,
):
    n = lax.axis_size("seq")
    each = BS // n
    pad = max(each, 8)
    rows = n * pad
    sin = jnp.pad(seq_inner[0].reshape(n, each, BS), ((0, 0), (0, pad - each), (0, 0)))
    final, gate, value, es = step(
        n, fields, cotangent, assignment, norm_gain[0].reshape(KB, WB), value_inner[0],
        value_outer[0], gate_inner[0], gate_outer[0], sin.reshape(rows, BS),
        seq_outer[0].reshape(BS, n),
    )
    final, gain, vin, vout, gin, gout, esin, esx = write_outputs(
        n, rows, final, gate.reshape(-1, WB), value.reshape(-1, WB), es
    )
    return (
        final,
        gain,
        vin.reshape(1, KB, WB, WB),
        vout.reshape(1, KB, KB, WB),
        gin.reshape(1, KB, WB, WB),
        gout.reshape(1, KB, KB, WB),
        esin.reshape(n, pad, BS)[:, :each].reshape(1, 1, BS, BS),
        esx.reshape(1, each, n, n),
    )


def write_kernel(
    rows, final_ref, gate_ref, value_ref, es_ref, final_out, gain_out, vin_out, vout_out,
    gin_out, gout_out, esin_out, esx_out, sem,
):
    copy = pltpu.make_async_copy(final_ref, final_out, sem)
    copy.start()
    for ref, inner, outer in ((gate_ref, gin_out, gout_out), (value_ref, vin_out, vout_out)):
        inner[...] = ref[:D, :].astype(F32)
        outer[...] = ref[D : D + OUTER, :].astype(F32)
    gains = value_ref[D + OUTER : PARTS[1], :].astype(F32)
    for k in range(KB):
        gain_out[:, k * WB : (k + 1) * WB] = gains[k : k + 1, :]
    esin_out[...] = es_ref[:rows, :]
    esx_out[...] = es_ref[rows:, : esx_out.shape[1]]
    copy.wait()


def write_outputs(n, rows, final, gate, value, es):
    vmem = pl.BlockSpec(memory_space=pltpu.VMEM)
    anywhere = pl.BlockSpec(memory_space=pl.ANY)
    shapes = ((1, D), (D, WB), (OUTER, WB), (D, WB), (OUTER, WB), (rows, BS), (BS, n))
    return pl.pallas_call(
        functools.partial(write_kernel, rows),
        out_shape=(
            jax.ShapeDtypeStruct((2, BS, D), BF16),
            *(jax.ShapeDtypeStruct(shape, F32) for shape in shapes),
        ),
        in_specs=[anywhere] + [vmem] * 3,
        out_specs=(anywhere,) + (vmem,) * len(shapes),
        scratch_shapes=[pltpu.SemaphoreType.DMA],
        compiler_params=pltpu.CompilerParams(vmem_limit_bytes=60 * 2**20),
        name="write_outputs",
    )(final, gate, value, es)


def solution(mesh):
    in_specs = (
        P(None, "seq", None),
        P(None, "seq", None),
        P(),
        P("section", None),
        P("section", None, None, None),
        P("section", None, None, None),
        P("section", None, None, None),
        P("section", None, None, None),
        P("section", "seq", None, None),
        P("section", "seq", None, None),
    )
    out_specs = (
        P(None, "seq", None),
        P("section", None),
        P("section", None, None, None),
        P("section", None, None, None),
        P("section", None, None, None),
        P("section", None, None, None),
        P("section", "seq", None, None),
        P("section", "seq", None, None),
    )
    return jax.shard_map(
        on_device, mesh=mesh, in_specs=in_specs, out_specs=out_specs, check_vma=False
    )
```

```python
import functools

import jax
import jax.numpy as jnp
from jax import lax
from jax.experimental import pallas as pl
from jax.experimental.pallas import tpu as pltpu
from jax.sharding import PartitionSpec as P

D = 2048
WB = 128
BS = 128
KB = 16
EPSILON = 1e-06
F32 = jnp.float32
BF16 = jnp.bfloat16
MESH = pl.DeviceIdType.MESH
WIDE = 512
CHUNKS = D // WIDE
HEAD = 4
OUTER = KB * KB
PARTS = (D + OUTER, D + OUTER + KB)


def dot(a, b, ca, cb):
    return lax.dot_general(a, b, (((ca,), (cb,)), ((), ())), preferred_element_type=F32)


def chunk_rows(n):
    return [-(-count // (16 * n)) * 16 for count in PARTS]


def remote(src, dst, send, recv, device):
    return pltpu.make_async_remote_copy(
        src_ref=src, dst_ref=dst, send_sem=send, recv_sem=recv,
        device_id=device, device_id_type=MESH,
    )


def in_half(n, block):
    half = lax.axis_index("seq") // (n // 2)
    return {"section": block // (n // 2), "seq": half * (n // 2) + lax.rem(block, n // 2)}


def send_all(n, me, i, src, dst, sems):
    def one(d, c):
        peer = lax.rem(me + d, n)
        remote(
            src.at[i, peer], dst.at[i, me], sems[0].at[i], sems[1].at[i], in_half(n, peer)
        ).start()
        return c

    lax.fori_loop(1, n, one, 0)
    dst[i, me] = src[i, me]


def wait_all(n, me, i, src, dst, sems):
    others = pl.ds(0, n - 1)
    copy = remote(
        src.at[i, others], dst.at[i, others], sems[0].at[i], sems[1].at[i],
        in_half(n, lax.rem(me + 1, n)),
    )
    copy.wait_send()
    copy.wait_recv()


def copies(count, rows, pad):
    at = lax.broadcasted_iota(jnp.int32, (count, rows), 0)
    to = lax.broadcasted_iota(jnp.int32, (count, rows), 1)
    return jnp.where(to // pad == at, 1.0, 0.0).astype(BF16)


def same_place(rows, pad):
    at = lax.broadcasted_iota(jnp.int32, (rows, rows), 0)
    to = lax.broadcasted_iota(jnp.int32, (rows, rows), 1)
    return at % pad == to % pad


def by_place(n, rows):
    pad = rows // n
    at = lax.broadcasted_iota(jnp.int32, (rows, BS), 0)
    to = lax.broadcasted_iota(jnp.int32, (rows, BS), 1)
    hit = (at % pad * n + at // pad == to) & (at % pad < BS // n)
    return jnp.where(hit, 1.0, 0.0).astype(BF16)


def spread_rows(n, rows):
    pad = rows // n
    each = BS // n
    at = lax.broadcasted_iota(jnp.int32, (rows, BS), 0)
    to = lax.broadcasted_iota(jnp.int32, (rows, BS), 1)
    hit = (at // pad * each + at % pad == to) & (at % pad < each)
    return jnp.where(hit, 1.0, 0.0).astype(BF16)


def cross(read, write, b_ref, back, cols=(0, KB), rows=(0, BS)):
    def group(i, c):
        at = pl.ds(pl.multiple_of(i * 16, 16), 16)
        parts = [read(k, at).astype(F32) for k in range(KB)]
        for l in range(*cols):
            total = None
            for k in range(KB):
                row = b_ref[l, k : k + 1, :] if back else b_ref[k, l : l + 1, :]
                term = parts[k] * row
                total = term if total is None else total + term
            write(l, at, total)
        return c

    lax.fori_loop(rows[0] // 16, rows[1] // 16, group, 0)


def row_factor(wide):
    return lax.rsqrt(jnp.mean(wide * wide, axis=-1, keepdims=True) + EPSILON)


def step_kernel(n, refs):
    hn = n // 2
    each = chunk_rows(n)
    core = lax.axis_index("section")
    chip = lax.axis_index("seq")
    half = chip // hn
    k_me = lax.rem(chip, hn)
    me = core * hn + k_me
    own = core == half
    partner_chip = lax.rem(chip + hn, n)
    partner = {"section": core, "seq": partner_chip}
    foreign = {"section": half, "seq": partner_chip}
    other = {"section": 1 - core, "seq": chip}
    rows = refs["sin"].shape[0]
    pad = rows // n
    x0, x1, e1, dx1 = refs["x0"], refs["x1"], refs["e"], refs["dx"]
    w, vo, go, gain = refs["w"], refs["vo"], refs["go"], refs["gain_s"]
    sins, sxs = refs["sins"], refs["sxs"]
    hid, mid, val, gat, mix = (refs[name] for name in ("h", "t", "v", "g", "s"))
    flat, es = (refs["flat0"], refs["flat1"]), refs["es"]
    last, final = refs["last"], refs["final"]
    upv, upg, dt, dh = refs["upv"], refs["upg"], refs["dt"], refs["dh"]

    def piece_of_fields(r):
        at = pl.ds(r * (BS // HEAD), BS // HEAD)
        return pltpu.make_async_copy(
            refs["fields"].at[:, at], refs[f"fv{r}"], refs["lx"].at[r]
        )

    def own_cotangent():
        return pltpu.make_async_copy(refs["cotangent"].at[half], e1, refs["le"])

    def weight_parts():
        left, right = pl.ds(0, WB), pl.ds(WB, WB)
        return [
            (refs["vin"], w.at[core, :, :, left]),
            (refs["gin"], w.at[core, :, :, right]),
            (refs["vout"], refs["vraw"].at[core]),
            (refs["gout"], refs["graw"].at[core]),
            (refs["gain"], gain.at[core]),
        ]

    def weight_parts_of(sec):
        left, right = pl.ds(0, WB), pl.ds(WB, WB)
        return [
            (refs["vin"], w.at[sec, :, :, left]),
            (refs["gin"], w.at[sec, :, :, right]),
            (refs["vout"], refs["vraw"].at[sec]),
            (refs["gout"], refs["graw"].at[sec]),
            (refs["gain"], gain.at[sec]),
        ]

    @pl.when(own)
    def _():
        for r in range(HEAD):
            piece_of_fields(r).start()

    @pl.when(jnp.logical_not(own))
    def _():
        for r in range(HEAD // 2, HEAD):
            piece_of_fields(r).start()

    for j, (src, dst) in enumerate(weight_parts()):
        pltpu.make_async_copy(src, dst, refs["lw"].at[j]).start()

    barrier = pltpu.get_barrier_semaphore()

    def greet(d, c):
        pl.semaphore_signal(
            barrier, inc=1, device_id=in_half(n, lax.rem(me + d, n)), device_id_type=MESH
        )
        return c

    lax.fori_loop(1, n, greet, 0)
    for number in range(2):
        pl.semaphore_signal(
            barrier, inc=1, device_id={"section": number, "seq": partner_chip}, device_id_type=MESH
        )

    wide = dot(refs["sout"][...], copies(n, rows, pad), 1, 0).astype(BF16)
    placed = dot(by_place(n, rows), wide, 1, 0)
    refs["sxmine"][...] = jnp.where(same_place(rows, pad), placed, 0.0).astype(BF16)

    pl.semaphore_wait(barrier, n + 1)

    def x_copy(r):
        at = pl.ds(r * (BS // HEAD), BS // HEAD)
        return remote(
            refs["xs"].at[at], x0.at[at], refs["xsem"].at[0, r], refs["xsem"].at[1, r], foreign
        )

    def weight_copies(sec):
        return [
            remote(src, dst, refs["wsem"].at[0, j], refs["wsem"].at[1, j], other)
            for j, (src, dst) in enumerate(weight_parts_of(sec))
        ]

    def seq_copies(sec, device, row):
        return [
            remote(
                refs[src], refs[dst].at[sec], refs["ssem"].at[0, row, j],
                refs["ssem"].at[1, sec, j], device,
            )
            for j, (src, dst) in enumerate((("sin", "sins"), ("sxmine", "sxs")))
        ]

    mine, theirs = refs["assignment"][half], refs["assignment"][1 - half]

    def rows_of(r):
        return slice(r * (BS // HEAD), (r + 1) * (BS // HEAD))

    def send_x(r):
        refs["xs"][rows_of(r), :] = refs[f"fv{r}"][theirs]
        x_copy(r).start()

    @pl.when(own)
    def _():
        for r in range(HEAD):
            piece_of_fields(r).wait()
            if r < HEAD // 2:
                send_x(r)

    @pl.when(jnp.logical_not(own))
    def _():
        for r in range(HEAD // 2, HEAD):
            piece_of_fields(r).wait()
            send_x(r)

    for copy in weight_copies(core):
        copy.start()
    def send_seq():
        for copy in seq_copies(core, foreign, 0):
            copy.start()

        @pl.when(jnp.logical_not(own))
        def _():
            for copy in seq_copies(core, other, 1):
                copy.start()

    @pl.when(core == 0)
    def _():
        send_seq()

    @pl.when(own)
    def _():
        sins[core] = refs["sin"][...]
        sxs[core] = refs["sxmine"][...]
        own_cotangent().start()
        for r in range(HEAD):
            x0[rows_of(r), :] = refs[f"fv{r}"][mine]

    def wait_weights(sec):
        @pl.when(core == sec)
        def _():
            for j, (src, dst) in enumerate(weight_parts()):
                pltpu.make_async_copy(src, dst, refs["lw"].at[j]).wait()

        @pl.when(core != sec)
        def _():
            for copy in weight_copies(sec):
                copy.wait_recv()

        vo[sec] = refs["vraw"][sec].astype(F32)
        go[sec] = refs["graw"][sec].astype(F32)

    def wait_seq(sec):
        @pl.when(jnp.logical_not(own & (core == sec)))
        def _():
            for copy in seq_copies(sec, other, 0):
                copy.wait_recv()

    def front(sec, x_ref, low, high):
        at = slice(low, high)
        factor = row_factor(x_ref[at, :].astype(F32))
        for k in range(KB):
            cols = slice(k * WB, (k + 1) * WB)
            hidden = (
                x_ref[at, cols].astype(F32) * factor * gain[sec, k : k + 1, :]
            ).astype(BF16)
            hid[sec, at, cols] = hidden
            mid[sec, k, at, :] = dot(hidden, w[sec, k], 1, 0).astype(BF16)

    def mixed_into(ref, sec):
        def write(l, at, value):
            ref[sec, at, l * WB : (l + 1) * WB] = value.astype(BF16)

        return write

    def values(sec, cols=(0, KB), span=(0, BS)):
        cross(
            lambda k, at: mid[sec, k, at, :WB], mixed_into(val, sec), vo.at[sec], False, cols, span
        )

    def gates(sec):
        cross(lambda k, at: mid[sec, k, at, WB:], mixed_into(gat, sec), go.at[sec], False)

    def columns(i):
        return slice(i * WIDE, (i + 1) * WIDE)

    def got(ref, i):
        return ref[i].astype(F32).reshape(rows, WIDE).astype(BF16)

    def send(value, i, ex):
        a, b, sems = ex
        a[i] = value.reshape(n, pad, WIDE).astype(BF16)
        send_all(n, me, i, a, b, sems)

    def wait(i, ex):
        a, b, sems = ex
        wait_all(n, me, i, a, b, sems)

    def exchange(a, b, call, first):
        sems = refs["ex"]
        return refs["a"].at[a], refs["b"].at[b], (sems.at[first, 0, call], sems.at[first, 1, call])

    f0 = [exchange(0, 0, 0, 0), exchange(1, 1, 1, 0)]
    f1 = [exchange(0, 2, 0, 0), exchange(1, 3, 1, 0)]
    r1 = [exchange(2, 4, 0, 1), exchange(3, 5, 1, 1)]
    r0 = [exchange(0, 6, 0, 0), exchange(1, 7, 1, 0)]

    def first_mix(sec, i, ex):
        send(dot(sins[sec], val[sec, :, columns(i)], 1, 0), i, ex[0])

    def second_mix(sec, i, ex):
        wait(i, ex[0])
        send(dot(sxs[sec], got(ex[0][1], i), 1, 0), i, ex[1])

    def finish(sec, i, ex, x_ref, out_ref):
        wait(i, ex[1])
        cols = columns(i)
        mixed = ex[1][1][i].astype(F32).reshape(rows, WIDE)
        if rows != BS:
            mixed = dot(spread_rows(n, rows), mixed.astype(BF16), 0, 0)
        mix[sec, :, cols] = mixed.astype(BF16)
        out_ref[:, cols] = (
            x_ref[:, cols].astype(F32) + mixed * gat[sec, :, cols].astype(F32)
        ).astype(BF16)

    def first_back(sec, e_ref, i, ex):
        cols = columns(i)
        ds = e_ref[:, cols].astype(F32) * gat[sec, :, cols].astype(F32)
        if rows != BS:
            ds = dot(spread_rows(n, rows), ds.astype(BF16), 1, 0)
        send(ds, i, ex[0])

    def second_back(sec, i, ex):
        wait(i, ex[0])
        send(dot(sxs[sec], got(ex[0][1], i), 0, 0), i, ex[1])

    def middle_back(first, up, b_ref):
        def write(k, at, value):
            dt[k, at, first : first + WB] = value.astype(BF16)

        cross(lambda l, at: up[at, l * WB : (l + 1) * WB], write, b_ref, True)

    def gate_back(sec, e_ref):
        for i in range(CHUNKS):
            cols = columns(i)
            dg = e_ref[:, cols].astype(F32) * mix[sec, :, cols].astype(F32)
            upg[:, cols] = dg.astype(BF16).astype(F32)
        middle_back(WB, upg, go.at[sec])

    def value_back(sec, ex):
        for i in range(CHUNKS):
            wait(i, ex[1])
            upv[:, columns(i)] = (
                dot(sins[sec], got(ex[1][1], i), 0, 0).astype(BF16).astype(F32)
            )
            outer_grad(sec, 1, (i * KB // CHUNKS, (i + 1) * KB // CHUNKS))

    def outer_grad(sec, p, cols=(0, KB)):
        up = (upg, upv)[p]
        first = (1 - p) * WB

        def block(k, c):
            middle = mid[sec, k, :, first : first + WB].astype(F32)
            for l in range(*cols):
                both = middle * up[:, l * WB : (l + 1) * WB]
                refs["og"][pl.ds(k * KB + l, 1), :] = jnp.sum(both, axis=0, keepdims=True)
            return c

        lax.fori_loop(0, KB, block, 0)

    def inner_grad(sec, p):
        half_of = slice((1 - p) * WB, (2 - p) * WB)
        for k in range(KB):
            cols = slice(k * WB, (k + 1) * WB)
            flat[p][sec, cols, :] = dot(hid[sec, :, cols], dt[k, :, half_of], 0, 0).astype(BF16)
        flat[p][sec, D : D + OUTER, :] = refs["og"][...].astype(BF16)
        left = n * each[p] - PARTS[p]
        if left:
            flat[p][sec, PARTS[p] :, :] = jnp.zeros((left, WB), BF16)

    def hidden_back(sec, x_ref, e_ref=None, dx_ref=None):
        factor = row_factor(x_ref[...].astype(F32))
        lean = jnp.zeros((BS, WB), F32)
        gains = []
        for k in range(KB):
            cols = slice(k * WB, (k + 1) * WB)
            part = dot(dt[k], w[sec, k], 1, 1)
            seen = part * x_ref[:, cols].astype(F32)
            gains.append(jnp.sum(seen * factor, axis=0, keepdims=True))
            if dx_ref is not None:
                lean += gain[sec, k : k + 1, :] * seen
                dh[:, cols] = gain[sec, k : k + 1, :] * part
        flat[1][sec, D + OUTER : PARTS[1], :] = jnp.concatenate(gains, axis=0).astype(BF16)
        if dx_ref is None:
            return
        mean = jnp.sum(lean, axis=-1, keepdims=True) * (1.0 / D)
        pull = factor * factor * factor * mean
        for k in range(KB):
            cols = slice(k * WB, (k + 1) * WB)
            dx_ref[:, cols] = (
                e_ref[:, cols].astype(F32)
                + factor * dh[:, cols]
                - x_ref[:, cols].astype(F32) * pull
            ).astype(BF16)

    def seq_outer_grad(sec, fwd, back):
        pairs = jnp.zeros((rows, rows), F32)
        for i in range(CHUNKS):
            pairs += dot(got(back[0][1], i), got(fwd[0][1], i), 1, 1)
        kept = jnp.where(same_place(rows, pad), pairs, 0.0).astype(BF16)
        moved = dot(by_place(n, rows), kept, 0, 0).astype(BF16)
        es[sec, rows:, :] = dot(moved, copies(BS, rows, pad), 1, 1).astype(BF16)

    def seq_inner_grad(sec, back):
        inner = jnp.zeros((rows, BS), F32)
        for i in range(CHUNKS):
            inner += dot(got(back[1][1], i), val[sec, :, columns(i)], 1, 1)
        es[sec, :rows, :] = inner.astype(BF16)

    def of(name, p):
        return refs[f"{name}{p}"]

    def width(p, piece):
        return pl.ds(pl.multiple_of(piece * each[p], 16), each[p])

    def across(sec, p, d):
        kk = lax.rem(k_me + d, hn)
        return remote(
            flat[p].at[sec, width(p, (1 - core) * hn + kk)], of("came", p).at[sec, kk],
            refs["csem"].at[0, sec, p, d], refs["csem"].at[1, sec, p, d], other,
        )

    def in_core(kk):
        return {"section": core, "seq": half * hn + kk}

    def sum_cores(sec, p):
        def one(d, c):
            across(sec, p, lax.rem(d, hn)).start()
            return c

        lax.fori_loop(1, hn + 1, one, 0)

    def sum_scatter(sec, p):
        sems = (refs["rsem"].at[0, sec, p], refs["rsem"].at[1, sec, p])

        def one(j, c):
            d = lax.rem(j, hn)
            kk = lax.rem(k_me + d, hn)
            across(sec, p, d).wait_recv()
            at = width(p, core * hn + kk)
            total = flat[p][sec, at, :].astype(F32) + of("came", p)[sec, kk].astype(F32)
            flat[p][sec, at, :] = total.astype(BF16)

            @pl.when(d != 0)
            def _():
                remote(
                    flat[p].at[sec, at], of("land", p).at[sec, k_me], *sems, in_core(kk)
                ).start()

            return c

        lax.fori_loop(1, hn + 1, one, 0)
        of("land", p)[sec, k_me] = flat[p][sec, width(p, core * hn + k_me), :]

    def partner_copy(sec, p):
        return remote(
            of("part", p).at[sec], of("came_part", p).at[sec], refs["psem"].at[0, sec, p],
            refs["psem"].at[1, sec, p], partner,
        )

    def sum_partner(sec, p):
        land = of("land", p)
        others = pl.ds(0, hn - 1)
        copy = remote(
            land.at[sec, others], land.at[sec, others], refs["rsem"].at[0, sec, p],
            refs["rsem"].at[1, sec, p], in_core(lax.rem(k_me + 1, hn)),
        )
        copy.wait_send()
        copy.wait_recv()
        total = land[sec, 0].astype(F32)
        for q in range(1, hn):
            total = total + land[sec, q].astype(F32)
        of("part", p)[sec] = total.astype(BF16)
        partner_copy(sec, p).start()

    def gather_copy(sec, p, kk):
        return remote(
            of("mine", p).at[sec], of("full", p).at[me], refs["gsem"].at[0, sec, p],
            refs["gsem"].at[1, sec, p], {"section": sec, "seq": half * hn + kk},
        )

    def sum_gather(sec, p):
        copy = partner_copy(sec, p)
        copy.wait_send()
        copy.wait_recv()
        total = of("part", p)[sec].astype(F32) + of("came_part", p)[sec].astype(F32)
        of("mine", p)[sec] = total.astype(BF16)

        def one(d, c):
            gather_copy(sec, p, lax.rem(k_me + d, hn)).start()
            return c

        lax.fori_loop(1, hn, one, 0)

        @pl.when(core != sec)
        def _():
            gather_copy(sec, p, k_me).start()

        @pl.when(core == sec)
        def _():
            of("full", p)[me] = of("mine", p)[sec]

    def sum_finish(sec, p):
        def cross_sent(d, c):
            across(sec, p, d).wait_send()
            return c

        lax.fori_loop(0, hn, cross_sent, 0)

        def several(count):
            some = of("full", p).at[pl.ds(0, count)]
            return remote(
                some, some, refs["gsem"].at[0, sec, p], refs["gsem"].at[1, sec, p], partner
            )

        @pl.when(core != sec)
        def _():
            several(hn).wait_send()

        @pl.when(core == sec)
        def _():
            several(hn - 1).wait_send()
            several(n - 1).wait_recv()

    def es_copy(sec):
        return remote(
            es.at[sec], refs["es_came"].at[sec], refs["esem"].at[0, sec],
            refs["esem"].at[1, sec], partner,
        )

    def es_over(sec):
        return remote(
            refs["es_sum"], refs["es_got"], refs["osem"].at[0], refs["osem"].at[1], other
        )

    def es_start(sec):
        @pl.when(jnp.logical_not(own))
        def _():
            es_copy(sec).start()

    def es_total(sec):
        @pl.when(own)
        def _():
            es_copy(sec).wait_recv()
            total = es[sec].astype(F32) + refs["es_came"][sec].astype(F32)

            @pl.when(core == sec)
            def _():
                refs["es_out"][...] = total

            @pl.when(core != sec)
            def _():
                refs["es_sum"][...] = total
                es_over(sec).start()

        @pl.when(jnp.logical_not(own))
        def _():
            es_copy(sec).wait_send()

    def es_end():
        @pl.when(own)
        def _():
            es_over(0).wait_send()

        @pl.when(jnp.logical_not(own))
        def _():
            es_over(0).wait_recv()
            refs["es_out"][...] = refs["es_got"][...]

    wait_weights(0)
    for r in (0, 2, 1, 3):
        low, high = r * (BS // HEAD), (r + 1) * (BS // HEAD)

        @pl.when(jnp.logical_not(own))
        def _():
            x_copy(r).wait_recv()

        front(0, x0, low, high)
        values(0, span=(low, high))
    wait_seq(0)
    for i in range(CHUNKS):
        first_mix(0, i, f0)
    gates(0)

    def e_copy(j):
        at = pl.ds(j * (BS // 2), BS // 2)
        return remote(
            refs["cotangent"].at[1 - half, at], e1.at[at], refs["ysem"].at[0, j],
            refs["ysem"].at[1, j], foreign,
        )

    def send_e(j):
        for r in range(j * HEAD // 2, (j + 1) * HEAD // 2):
            x_copy(r).wait_send()

        @pl.when(core == 1)
        def _():
            send_seq()

        e_copy(j).start()

    @pl.when(own)
    def _():
        send_e(0)

    @pl.when(jnp.logical_not(own))
    def _():
        send_e(1)

    for i in range(CHUNKS):
        second_mix(0, i, f0)
    for i in range(CHUNKS):
        finish(0, i, f0, x0, x1)

    wait_weights(1)
    wait_seq(1)
    front(1, x1, 0, BS)
    for i in range(CHUNKS):
        each_l = KB // CHUNKS
        values(1, cols=(i * each_l, (i + 1) * each_l))
        first_mix(1, i, f1)
    gates(1)

    @pl.when(own)
    def _():
        own_cotangent().wait()

    @pl.when(jnp.logical_not(own))
    def _():
        e_copy(0).wait_recv()
        e_copy(1).wait_recv()

    for i in range(CHUNKS):
        first_back(1, e1, i, r1)
    for i in range(CHUNKS):
        second_mix(1, i, f1)
    for i in range(CHUNKS):
        second_back(1, i, r1)
    for i in range(CHUNKS):
        finish(1, i, f1, x1, last)

    def fin_home():
        return remote(
            last, final.at[half], refs["fsem"].at[0, 0], refs["fsem"].at[1, 0], partner
        )

    def fin_core(m, j):
        return remote(
            final.at[m], final.at[m], refs["fsem"].at[0, j], refs["fsem"].at[1, j], other
        )

    @pl.when(jnp.logical_not(own))
    def _():
        fin_home().start()

    @pl.when(own)
    def _():
        final[half] = last[...]
        fin_core(half, 1).start()

    gate_back(1, e1)
    outer_grad(1, 0)
    inner_grad(1, 0)
    sum_cores(1, 0)
    seq_outer_grad(1, f1, r1)
    value_back(1, r1)
    sum_scatter(1, 0)
    middle_back(0, upv, vo.at[1])
    hidden_back(1, x1, e1, dx1)

    for i in range(CHUNKS):
        first_back(0, dx1, i, r0)
    inner_grad(1, 1)
    sum_cores(1, 1)
    seq_inner_grad(1, r1)
    es_start(1)
    sum_partner(1, 0)
    for i in range(CHUNKS):
        second_back(0, i, r0)
    sum_scatter(1, 1)
    gate_back(0, dx1)
    outer_grad(0, 0)
    inner_grad(0, 0)
    sum_cores(0, 0)
    seq_outer_grad(0, f0, r0)
    sum_gather(1, 0)
    value_back(0, r0)
    sum_scatter(0, 0)
    sum_partner(1, 1)
    middle_back(0, upv, vo.at[0])
    inner_grad(0, 1)
    hidden_back(0, x0)
    sum_cores(0, 1)
    sum_gather(1, 1)
    seq_inner_grad(0, r0)
    es_start(0)
    sum_scatter(0, 1)
    sum_partner(0, 0)
    es_total(1)
    sum_gather(0, 0)

    @pl.when(own)
    def _():
        e_copy(0).wait_send()
        fin_core(half, 1).wait_send()
        remote(
            last, final.at[1 - half], refs["fsem"].at[0, 0], refs["fsem"].at[1, 0], partner
        ).wait_recv()
        fin_core(1 - half, 2).start()

    @pl.when(jnp.logical_not(own))
    def _():
        e_copy(1).wait_send()
        fin_home().wait_send()

    sum_partner(0, 1)
    sum_finish(1, 0)
    sum_finish(1, 1)
    sum_gather(0, 1)
    es_total(0)
    es_end()

    @pl.when(own)
    def _():
        fin_core(1 - half, 2).wait_send()

    @pl.when(jnp.logical_not(own))
    def _():
        fin_core(half, 1).wait_recv()
        fin_core(1 - half, 2).wait_recv()
        for copy in seq_copies(core, other, 1):
            copy.wait_send()

    for copy in weight_copies(core):
        copy.wait_send()
    for copy in seq_copies(core, foreign, 0):
        copy.wait_send()
    sum_finish(0, 0)
    sum_finish(0, 1)


INPUTS = (
    "fields", "cotangent", "assignment", "gain", "vin", "vout", "gin", "gout", "sin", "sout",
)
OUTPUTS = ("final", "full0", "full1", "es_out")


def scratch(n, rows):
    pad = rows // n
    each = chunk_rows(n)
    hn = n // 2
    vmem, dma = pltpu.VMEM, pltpu.SemaphoreType.DMA
    plane = (BS, D)

    def by_part(name, shape):
        return {f"{name}{p}": vmem(shape(size), BF16) for p, size in enumerate(each)}

    return {
        **{f"fv{r}": vmem((8, BS // HEAD, D), BF16) for r in range(HEAD)},
        "xs": vmem(plane, BF16),
        "x0": vmem(plane, BF16),
        "x1": vmem(plane, BF16),
        "e": vmem(plane, BF16),
        "dx": vmem(plane, BF16),
        "last": vmem(plane, BF16),
        "w": vmem((2, KB, WB, 2 * WB), BF16),
        "vraw": vmem((2, KB, KB, WB), BF16),
        "graw": vmem((2, KB, KB, WB), BF16),
        "vo": vmem((2, KB, KB, WB), F32),
        "go": vmem((2, KB, KB, WB), F32),
        "gain_s": vmem((2, KB, WB), F32),
        "sxmine": vmem((rows, rows), BF16),
        "sins": vmem((2, rows, BS), BF16),
        "sxs": vmem((2, rows, rows), BF16),
        "h": vmem((2, BS, D), BF16),
        "t": vmem((2, KB, BS, 2 * WB), BF16),
        "v": vmem((2, BS, D), BF16),
        "g": vmem((2, BS, D), BF16),
        "s": vmem((2, BS, D), BF16),
        "a": vmem((4, CHUNKS, n, pad, WIDE), BF16),
        "b": vmem((8, CHUNKS, n, pad, WIDE), BF16),
        "upv": vmem(plane, F32),
        "upg": vmem(plane, F32),
        "dt": vmem((KB, BS, 2 * WB), BF16),
        "dh": vmem(plane, F32),
        "og": vmem((OUTER, WB), F32),
        **by_part("flat", lambda size: (2, n * size, WB)),
        **by_part("came", lambda size: (2, hn, size, WB)),
        **by_part("land", lambda size: (2, hn, size, WB)),
        **by_part("part", lambda size: (2, size, WB)),
        **by_part("came_part", lambda size: (2, size, WB)),
        **by_part("mine", lambda size: (2, size, WB)),
        "es": vmem((2, rows + BS, BS), BF16),
        "es_came": vmem((2, rows + BS, BS), BF16),
        "es_sum": vmem((rows + BS, BS), F32),
        "es_got": vmem((rows + BS, BS), F32),
        "lx": dma((HEAD,)),
        "le": dma,
        "lw": dma((5,)),
        "xsem": dma((2, HEAD)),
        "wsem": dma((2, 5)),
        "ssem": dma((2, 2, 2)),
        "ysem": dma((2, 2)),
        "ex": dma((2, 2, 2, CHUNKS)),
        "csem": dma((2, 2, 2, hn)),
        "rsem": dma((2, 2, 2)),
        "psem": dma((2, 2, 2)),
        "gsem": dma((2, 2, 2)),
        "esem": dma((2, 2)),
        "osem": dma((2,)),
        "fsem": dma((2, 3)),
    }


def step(n, *args):
    rows = args[INPUTS.index("sin")].shape[0]
    whole = scratch(n, rows)
    names = INPUTS + OUTPUTS + tuple(whole)
    anywhere = pl.BlockSpec(memory_space=pl.ANY)
    vmem = pl.BlockSpec(memory_space=pltpu.VMEM)
    places = {"sin": vmem, "sout": vmem, "assignment": pl.BlockSpec(memory_space=pltpu.SMEM)}

    def kernel(*refs):
        step_kernel(n, dict(zip(names, refs)))

    return pl.pallas_call(
        kernel,
        out_shape=(
            jax.ShapeDtypeStruct((2, BS, D), BF16),
            *(jax.ShapeDtypeStruct((n, size, WB), BF16) for size in chunk_rows(n)),
            jax.ShapeDtypeStruct((rows + BS, BS), F32),
        ),
        in_specs=[places.get(name, anywhere) for name in INPUTS],
        out_specs=(vmem,) * len(OUTPUTS),
        scratch_shapes=list(whole.values()),
        compiler_params=pltpu.CompilerParams(
            collective_id=0, has_side_effects=True, vmem_limit_bytes=60 * 2**20
        ),
        name="whole_step",
    )(*args)


def on_device(
    fields, cotangent, assignment, norm_gain, value_inner, value_outer,
    gate_inner, gate_outer, seq_inner, seq_outer,
):
    n = lax.axis_size("seq")
    each = BS // n
    pad = max(each, 8)
    rows = n * pad
    sin = jnp.pad(seq_inner[0].reshape(n, each, BS), ((0, 0), (0, pad - each), (0, 0)))
    final, gate, value, es = step(
        n, fields, cotangent, assignment, norm_gain[0].reshape(KB, WB), value_inner[0],
        value_outer[0], gate_inner[0], gate_outer[0], sin.reshape(rows, BS),
        seq_outer[0].reshape(BS, n),
    )
    final, gain, vin, vout, gin, gout, esin, esx = write_outputs(
        n, rows, final, gate.reshape(-1, WB), value.reshape(-1, WB), es
    )
    return (
        final,
        gain,
        vin.reshape(1, KB, WB, WB),
        vout.reshape(1, KB, KB, WB),
        gin.reshape(1, KB, WB, WB),
        gout.reshape(1, KB, KB, WB),
        esin.reshape(n, pad, BS)[:, :each].reshape(1, 1, BS, BS),
        esx.reshape(1, each, n, n),
    )


def write_kernel(
    rows, final_ref, gate_ref, value_ref, es_ref, final_out, gain_out, vin_out, vout_out,
    gin_out, gout_out, esin_out, esx_out, held, sems,
):
    fetch = pltpu.make_async_copy(final_ref, held, sems.at[0])
    store = pltpu.make_async_copy(held, final_out, sems.at[1])
    fetch.start()
    for ref, inner, outer in ((gate_ref, gin_out, gout_out), (value_ref, vin_out, vout_out)):
        inner[...] = ref[:D, :].astype(F32)
        outer[...] = ref[D : D + OUTER, :].astype(F32)
        if ref is gate_ref:
            fetch.wait()
            store.start()
    gains = value_ref[D + OUTER : PARTS[1], :].astype(F32)
    for k in range(KB):
        gain_out[:, k * WB : (k + 1) * WB] = gains[k : k + 1, :]
    esin_out[...] = es_ref[:rows, :]
    esx_out[...] = es_ref[rows:, : esx_out.shape[1]]
    store.wait()


def write_outputs(n, rows, final, gate, value, es):
    vmem = pl.BlockSpec(memory_space=pltpu.VMEM)
    anywhere = pl.BlockSpec(memory_space=pl.ANY)
    shapes = ((1, D), (D, WB), (OUTER, WB), (D, WB), (OUTER, WB), (rows, BS), (BS, n))
    return pl.pallas_call(
        functools.partial(write_kernel, rows),
        out_shape=(
            jax.ShapeDtypeStruct((2, BS, D), BF16),
            *(jax.ShapeDtypeStruct(shape, F32) for shape in shapes),
        ),
        in_specs=[anywhere] + [vmem] * 3,
        out_specs=(anywhere,) + (vmem,) * len(shapes),
        scratch_shapes=[pltpu.VMEM((2, BS, D), BF16), pltpu.SemaphoreType.DMA((2,))],
        compiler_params=pltpu.CompilerParams(vmem_limit_bytes=60 * 2**20),
        name="write_outputs",
    )(final, gate, value, es)


def solution(mesh):
    in_specs = (
        P(None, "seq", None),
        P(None, "seq", None),
        P(),
        P("section", None),
        P("section", None, None, None),
        P("section", None, None, None),
        P("section", None, None, None),
        P("section", None, None, None),
        P("section", "seq", None, None),
        P("section", "seq", None, None),
    )
    out_specs = (
        P(None, "seq", None),
        P("section", None),
        P("section", None, None, None),
        P("section", None, None, None),
        P("section", None, None, None),
        P("section", None, None, None),
        P("section", "seq", None, None),
        P("section", "seq", None, None),
    )
    return jax.shard_map(
        on_device, mesh=mesh, in_specs=in_specs, out_specs=out_specs, check_vma=False
    )
```

```python
import functools

import jax
import jax.numpy as jnp
from jax import lax
from jax.experimental import pallas as pl
from jax.experimental.pallas import tpu as pltpu
from jax.sharding import PartitionSpec as P

D = 2048
WB = 128
BS = 128
KB = 16
EPSILON = 1e-06
F32 = jnp.float32
BF16 = jnp.bfloat16
MESH = pl.DeviceIdType.MESH
WIDE = 512
CHUNKS = D // WIDE
HEAD = 4
OUTER = KB * KB
PARTS = (D + OUTER, D + OUTER + KB)


def dot(a, b, ca, cb):
    return lax.dot_general(a, b, (((ca,), (cb,)), ((), ())), preferred_element_type=F32)


def chunk_rows(n):
    return [-(-count // (16 * n)) * 16 for count in PARTS]


def remote(src, dst, send, recv, device):
    return pltpu.make_async_remote_copy(
        src_ref=src, dst_ref=dst, send_sem=send, recv_sem=recv,
        device_id=device, device_id_type=MESH,
    )


def in_half(n, block):
    half = lax.axis_index("seq") // (n // 2)
    return {"section": block // (n // 2), "seq": half * (n // 2) + lax.rem(block, n // 2)}


def send_all(n, me, i, src, dst, sems):
    def one(d, c):
        peer = lax.rem(me + d, n)
        remote(
            src.at[i, peer], dst.at[i, me], sems[0].at[i], sems[1].at[i], in_half(n, peer)
        ).start()
        return c

    lax.fori_loop(1, n, one, 0)
    dst[i, me] = src[i, me]


def wait_all(n, me, i, src, dst, sems):
    others = pl.ds(0, n - 1)
    copy = remote(
        src.at[i, others], dst.at[i, others], sems[0].at[i], sems[1].at[i],
        in_half(n, lax.rem(me + 1, n)),
    )
    copy.wait_send()
    copy.wait_recv()


def copies(count, rows, pad):
    at = lax.broadcasted_iota(jnp.int32, (count, rows), 0)
    to = lax.broadcasted_iota(jnp.int32, (count, rows), 1)
    return jnp.where(to // pad == at, 1.0, 0.0).astype(BF16)


def same_place(rows, pad):
    at = lax.broadcasted_iota(jnp.int32, (rows, rows), 0)
    to = lax.broadcasted_iota(jnp.int32, (rows, rows), 1)
    return at % pad == to % pad


def by_place(n, rows):
    pad = rows // n
    at = lax.broadcasted_iota(jnp.int32, (rows, BS), 0)
    to = lax.broadcasted_iota(jnp.int32, (rows, BS), 1)
    hit = (at % pad * n + at // pad == to) & (at % pad < BS // n)
    return jnp.where(hit, 1.0, 0.0).astype(BF16)


def spread_rows(n, rows):
    pad = rows // n
    each = BS // n
    at = lax.broadcasted_iota(jnp.int32, (rows, BS), 0)
    to = lax.broadcasted_iota(jnp.int32, (rows, BS), 1)
    hit = (at // pad * each + at % pad == to) & (at % pad < each)
    return jnp.where(hit, 1.0, 0.0).astype(BF16)


def cross(read, write, b_ref, back, cols=(0, KB), rows=(0, BS)):
    def group(i, c):
        at = pl.ds(pl.multiple_of(i * 16, 16), 16)
        parts = [read(k, at).astype(F32) for k in range(KB)]
        for l in range(*cols):
            total = None
            for k in range(KB):
                row = b_ref[l, k : k + 1, :] if back else b_ref[k, l : l + 1, :]
                term = parts[k] * row
                total = term if total is None else total + term
            write(l, at, total)
        return c

    lax.fori_loop(rows[0] // 16, rows[1] // 16, group, 0)


def row_factor(wide):
    return lax.rsqrt(jnp.mean(wide * wide, axis=-1, keepdims=True) + EPSILON)


def step_kernel(n, refs):
    hn = n // 2
    each = chunk_rows(n)
    core = lax.axis_index("section")
    chip = lax.axis_index("seq")
    half = chip // hn
    k_me = lax.rem(chip, hn)
    me = core * hn + k_me
    own = core == half
    partner_chip = lax.rem(chip + hn, n)
    partner = {"section": core, "seq": partner_chip}
    foreign = {"section": half, "seq": partner_chip}
    other = {"section": 1 - core, "seq": chip}
    rows = refs["sin"].shape[0]
    pad = rows // n
    x0, x1, e1, dx1 = refs["x0"], refs["x1"], refs["e"], refs["dx"]
    w, vo, go, gain = refs["w"], refs["vo"], refs["go"], refs["gain_s"]
    sins, sxs = refs["sins"], refs["sxs"]
    hid, mid, val, gat, mix = (refs[name] for name in ("h", "t", "v", "g", "s"))
    flat, es = (refs["flat0"], refs["flat1"]), refs["es"]
    last, final = refs["last"], refs["final"]
    upv, upg, dt, dh = refs["upv"], refs["upg"], refs["dt"], refs["dh"]

    def piece_of_fields(r):
        at = pl.ds(r * (BS // HEAD), BS // HEAD)
        return pltpu.make_async_copy(
            refs["fields"].at[:, at], refs[f"fv{r}"], refs["lx"].at[r]
        )

    def own_cotangent():
        return pltpu.make_async_copy(refs["cotangent"].at[half], e1, refs["le"])

    def weight_parts():
        left, right = pl.ds(0, WB), pl.ds(WB, WB)
        return [
            (refs["vin"], w.at[core, :, :, left]),
            (refs["gin"], w.at[core, :, :, right]),
            (refs["vout"], refs["vraw"].at[core]),
            (refs["gout"], refs["graw"].at[core]),
            (refs["gain"], gain.at[core]),
        ]

    def weight_parts_of(sec):
        left, right = pl.ds(0, WB), pl.ds(WB, WB)
        return [
            (refs["vin"], w.at[sec, :, :, left]),
            (refs["gin"], w.at[sec, :, :, right]),
            (refs["vout"], refs["vraw"].at[sec]),
            (refs["gout"], refs["graw"].at[sec]),
            (refs["gain"], gain.at[sec]),
        ]

    @pl.when(own)
    def _():
        for r in range(HEAD):
            piece_of_fields(r).start()

    @pl.when(jnp.logical_not(own))
    def _():
        for r in range(HEAD // 2, HEAD):
            piece_of_fields(r).start()

    for j, (src, dst) in enumerate(weight_parts()):
        pltpu.make_async_copy(src, dst, refs["lw"].at[j]).start()

    barrier = pltpu.get_barrier_semaphore()

    def greet(d, c):
        pl.semaphore_signal(
            barrier, inc=1, device_id=in_half(n, lax.rem(me + d, n)), device_id_type=MESH
        )
        return c

    lax.fori_loop(1, n, greet, 0)
    for number in range(2):
        pl.semaphore_signal(
            barrier, inc=1, device_id={"section": number, "seq": partner_chip}, device_id_type=MESH
        )

    wide = dot(refs["sout"][...], copies(n, rows, pad), 1, 0).astype(BF16)
    placed = dot(by_place(n, rows), wide, 1, 0)
    refs["sxmine"][...] = jnp.where(same_place(rows, pad), placed, 0.0).astype(BF16)

    pl.semaphore_wait(barrier, n + 1)

    def x_copy(r):
        at = pl.ds(r * (BS // HEAD), BS // HEAD)
        return remote(
            refs["xs"].at[at], x0.at[at], refs["xsem"].at[0, r], refs["xsem"].at[1, r], foreign
        )

    def weight_copies(sec):
        return [
            remote(src, dst, refs["wsem"].at[0, j], refs["wsem"].at[1, j], other)
            for j, (src, dst) in enumerate(weight_parts_of(sec))
        ]

    def seq_copies(sec, device, row):
        return [
            remote(
                refs[src], refs[dst].at[sec], refs["ssem"].at[0, row, j],
                refs["ssem"].at[1, sec, j], device,
            )
            for j, (src, dst) in enumerate((("sin", "sins"), ("sxmine", "sxs")))
        ]

    mine, theirs = refs["assignment"][half], refs["assignment"][1 - half]

    def rows_of(r):
        return slice(r * (BS // HEAD), (r + 1) * (BS // HEAD))

    def send_x(r):
        refs["xs"][rows_of(r), :] = refs[f"fv{r}"][theirs]
        x_copy(r).start()

    @pl.when(own)
    def _():
        for r in range(HEAD):
            piece_of_fields(r).wait()
            if r < HEAD // 2:
                send_x(r)

    @pl.when(jnp.logical_not(own))
    def _():
        for r in range(HEAD // 2, HEAD):
            piece_of_fields(r).wait()
            send_x(r)

    for copy in weight_copies(core):
        copy.start()
    def send_seq():
        for copy in seq_copies(core, foreign, 0):
            copy.start()

        @pl.when(jnp.logical_not(own))
        def _():
            for copy in seq_copies(core, other, 1):
                copy.start()

    @pl.when(core == 0)
    def _():
        send_seq()

    @pl.when(own)
    def _():
        sins[core] = refs["sin"][...]
        sxs[core] = refs["sxmine"][...]
        own_cotangent().start()
        for r in range(HEAD):
            x0[rows_of(r), :] = refs[f"fv{r}"][mine]

    def wait_weights(sec):
        @pl.when(core == sec)
        def _():
            for j, (src, dst) in enumerate(weight_parts()):
                pltpu.make_async_copy(src, dst, refs["lw"].at[j]).wait()

        @pl.when(core != sec)
        def _():
            for copy in weight_copies(sec):
                copy.wait_recv()

        vo[sec] = refs["vraw"][sec].astype(F32)
        go[sec] = refs["graw"][sec].astype(F32)

    def wait_seq(sec):
        @pl.when(jnp.logical_not(own & (core == sec)))
        def _():
            for copy in seq_copies(sec, other, 0):
                copy.wait_recv()

    def front(sec, x_ref, low, high):
        at = slice(low, high)
        factor = row_factor(x_ref[at, :].astype(F32))
        for k in range(KB):
            cols = slice(k * WB, (k + 1) * WB)
            hidden = (
                x_ref[at, cols].astype(F32) * factor * gain[sec, k : k + 1, :]
            ).astype(BF16)
            hid[sec, at, cols] = hidden
            mid[sec, k, at, :] = dot(hidden, w[sec, k], 1, 0).astype(BF16)

    def mixed_into(ref, sec):
        def write(l, at, value):
            ref[sec, at, l * WB : (l + 1) * WB] = value.astype(BF16)

        return write

    def values(sec, cols=(0, KB), span=(0, BS)):
        cross(
            lambda k, at: mid[sec, k, at, :WB], mixed_into(val, sec), vo.at[sec], False, cols, span
        )

    def gates(sec):
        cross(lambda k, at: mid[sec, k, at, WB:], mixed_into(gat, sec), go.at[sec], False)

    def columns(i):
        return slice(i * WIDE, (i + 1) * WIDE)

    def got(ref, i):
        return ref[i].astype(F32).reshape(rows, WIDE).astype(BF16)

    def send(value, i, ex):
        a, b, sems = ex
        a[i] = value.reshape(n, pad, WIDE).astype(BF16)
        send_all(n, me, i, a, b, sems)

    def wait(i, ex):
        a, b, sems = ex
        wait_all(n, me, i, a, b, sems)

    def exchange(a, b, call, first):
        sems = refs["ex"]
        return refs["a"].at[a], refs["b"].at[b], (sems.at[first, 0, call], sems.at[first, 1, call])

    f0 = [exchange(0, 0, 0, 0), exchange(1, 1, 1, 0)]
    f1 = [exchange(0, 2, 0, 0), exchange(1, 3, 1, 0)]
    r1 = [exchange(2, 4, 0, 1), exchange(3, 5, 1, 1)]
    r0 = [exchange(0, 6, 0, 0), exchange(1, 7, 1, 0)]

    def first_mix(sec, i, ex):
        send(dot(sins[sec], val[sec, :, columns(i)], 1, 0), i, ex[0])

    def second_mix(sec, i, ex):
        wait(i, ex[0])
        send(dot(sxs[sec], got(ex[0][1], i), 1, 0), i, ex[1])

    def finish(sec, i, ex, x_ref, out_ref):
        wait(i, ex[1])
        cols = columns(i)
        mixed = ex[1][1][i].astype(F32).reshape(rows, WIDE)
        if rows != BS:
            mixed = dot(spread_rows(n, rows), mixed.astype(BF16), 0, 0)
        mix[sec, :, cols] = mixed.astype(BF16)
        out_ref[:, cols] = (
            x_ref[:, cols].astype(F32) + mixed * gat[sec, :, cols].astype(F32)
        ).astype(BF16)

    def first_back(sec, e_ref, i, ex):
        cols = columns(i)
        ds = e_ref[:, cols].astype(F32) * gat[sec, :, cols].astype(F32)
        if rows != BS:
            ds = dot(spread_rows(n, rows), ds.astype(BF16), 1, 0)
        send(ds, i, ex[0])

    def second_back(sec, i, ex):
        wait(i, ex[0])
        send(dot(sxs[sec], got(ex[0][1], i), 0, 0), i, ex[1])

    def middle_back(first, up, b_ref):
        def write(k, at, value):
            dt[k, at, first : first + WB] = value.astype(BF16)

        cross(lambda l, at: up[at, l * WB : (l + 1) * WB], write, b_ref, True)

    def gate_back(sec, e_ref):
        for i in range(CHUNKS):
            cols = columns(i)
            dg = e_ref[:, cols].astype(F32) * mix[sec, :, cols].astype(F32)
            upg[:, cols] = dg.astype(BF16).astype(F32)
        middle_back(WB, upg, go.at[sec])

    def value_back(sec, ex):
        for i in range(CHUNKS):
            wait(i, ex[1])
            upv[:, columns(i)] = (
                dot(sins[sec], got(ex[1][1], i), 0, 0).astype(BF16).astype(F32)
            )
            outer_grad(sec, 1, (i * KB // CHUNKS, (i + 1) * KB // CHUNKS))

    def outer_grad(sec, p, cols=(0, KB)):
        up = (upg, upv)[p]
        first = (1 - p) * WB

        def block(k, c):
            middle = mid[sec, k, :, first : first + WB].astype(F32)
            for l in range(*cols):
                both = middle * up[:, l * WB : (l + 1) * WB]
                refs["og"][pl.ds(k * KB + l, 1), :] = jnp.sum(both, axis=0, keepdims=True)
            return c

        lax.fori_loop(0, KB, block, 0)

    def inner_grad(sec, p):
        half_of = slice((1 - p) * WB, (2 - p) * WB)
        for k in range(KB):
            cols = slice(k * WB, (k + 1) * WB)
            flat[p][sec, cols, :] = dot(hid[sec, :, cols], dt[k, :, half_of], 0, 0).astype(BF16)
        flat[p][sec, D : D + OUTER, :] = refs["og"][...].astype(BF16)
        left = n * each[p] - PARTS[p]
        if left:
            flat[p][sec, PARTS[p] :, :] = jnp.zeros((left, WB), BF16)

    def hidden_back(sec, x_ref, e_ref=None, dx_ref=None):
        factor = row_factor(x_ref[...].astype(F32))
        lean = jnp.zeros((BS, WB), F32)
        gains = []
        for k in range(KB):
            cols = slice(k * WB, (k + 1) * WB)
            part = dot(dt[k], w[sec, k], 1, 1)
            seen = part * x_ref[:, cols].astype(F32)
            gains.append(jnp.sum(seen * factor, axis=0, keepdims=True))
            if dx_ref is not None:
                lean += gain[sec, k : k + 1, :] * seen
                dh[:, cols] = gain[sec, k : k + 1, :] * part
        flat[1][sec, D + OUTER : PARTS[1], :] = jnp.concatenate(gains, axis=0).astype(BF16)
        if dx_ref is None:
            return
        mean = jnp.sum(lean, axis=-1, keepdims=True) * (1.0 / D)
        pull = factor * factor * factor * mean
        for k in range(KB):
            cols = slice(k * WB, (k + 1) * WB)
            dx_ref[:, cols] = (
                e_ref[:, cols].astype(F32)
                + factor * dh[:, cols]
                - x_ref[:, cols].astype(F32) * pull
            ).astype(BF16)

    def seq_outer_grad(sec, fwd, back):
        pairs = jnp.zeros((rows, rows), F32)
        for i in range(CHUNKS):
            pairs += dot(got(back[0][1], i), got(fwd[0][1], i), 1, 1)
        kept = jnp.where(same_place(rows, pad), pairs, 0.0).astype(BF16)
        moved = dot(by_place(n, rows), kept, 0, 0).astype(BF16)
        es[sec, rows:, :] = dot(moved, copies(BS, rows, pad), 1, 1).astype(BF16)

    def seq_inner_grad(sec, back):
        inner = jnp.zeros((rows, BS), F32)
        for i in range(CHUNKS):
            inner += dot(got(back[1][1], i), val[sec, :, columns(i)], 1, 1)
        es[sec, :rows, :] = inner.astype(BF16)

    def of(name, p):
        return refs[f"{name}{p}"]

    def width(p, piece):
        return pl.ds(pl.multiple_of(piece * each[p], 16), each[p])

    def across(sec, p, d):
        kk = lax.rem(k_me + d, hn)
        return remote(
            flat[p].at[sec, width(p, (1 - core) * hn + kk)], of("came", p).at[sec, kk],
            refs["csem"].at[0, sec, p, d], refs["csem"].at[1, sec, p, d], other,
        )

    def in_core(kk):
        return {"section": core, "seq": half * hn + kk}

    def sum_cores(sec, p):
        def one(d, c):
            across(sec, p, lax.rem(d, hn)).start()
            return c

        lax.fori_loop(1, hn + 1, one, 0)

    def sum_scatter(sec, p):
        sems = (refs["rsem"].at[0, sec, p], refs["rsem"].at[1, sec, p])

        def one(j, c):
            d = lax.rem(j, hn)
            kk = lax.rem(k_me + d, hn)
            across(sec, p, d).wait_recv()
            at = width(p, core * hn + kk)
            total = flat[p][sec, at, :].astype(F32) + of("came", p)[sec, kk].astype(F32)
            flat[p][sec, at, :] = total.astype(BF16)

            @pl.when(d != 0)
            def _():
                remote(
                    flat[p].at[sec, at], of("land", p).at[sec, k_me], *sems, in_core(kk)
                ).start()

            return c

        lax.fori_loop(1, hn + 1, one, 0)
        of("land", p)[sec, k_me] = flat[p][sec, width(p, core * hn + k_me), :]

    def partner_copy(sec, p):
        return remote(
            of("part", p).at[sec], of("came_part", p).at[sec], refs["psem"].at[0, sec, p],
            refs["psem"].at[1, sec, p], partner,
        )

    def sum_partner(sec, p):
        land = of("land", p)
        others = pl.ds(0, hn - 1)
        copy = remote(
            land.at[sec, others], land.at[sec, others], refs["rsem"].at[0, sec, p],
            refs["rsem"].at[1, sec, p], in_core(lax.rem(k_me + 1, hn)),
        )
        copy.wait_send()
        copy.wait_recv()
        total = land[sec, 0].astype(F32)
        for q in range(1, hn):
            total = total + land[sec, q].astype(F32)
        of("part", p)[sec] = total.astype(BF16)
        partner_copy(sec, p).start()

    def gather_copy(sec, p, kk):
        return remote(
            of("mine", p).at[sec], of("full", p).at[me], refs["gsem"].at[0, sec, p],
            refs["gsem"].at[1, sec, p], {"section": sec, "seq": half * hn + kk},
        )

    def sum_gather(sec, p):
        copy = partner_copy(sec, p)
        copy.wait_send()
        copy.wait_recv()
        total = of("part", p)[sec].astype(F32) + of("came_part", p)[sec].astype(F32)
        of("mine", p)[sec] = total.astype(BF16)

        def one(d, c):
            gather_copy(sec, p, lax.rem(k_me + d, hn)).start()
            return c

        lax.fori_loop(1, hn, one, 0)

        @pl.when(core != sec)
        def _():
            gather_copy(sec, p, k_me).start()

        @pl.when(core == sec)
        def _():
            of("full", p)[me] = of("mine", p)[sec]

    def sum_finish(sec, p):
        def cross_sent(d, c):
            across(sec, p, d).wait_send()
            return c

        lax.fori_loop(0, hn, cross_sent, 0)

        def several(count):
            some = of("full", p).at[pl.ds(0, count)]
            return remote(
                some, some, refs["gsem"].at[0, sec, p], refs["gsem"].at[1, sec, p], partner
            )

        @pl.when(core != sec)
        def _():
            several(hn).wait_send()

        @pl.when(core == sec)
        def _():
            several(hn - 1).wait_send()
            several(n - 1).wait_recv()

    def es_copy(sec):
        return remote(
            es.at[sec], refs["es_came"].at[sec], refs["esem"].at[0, sec],
            refs["esem"].at[1, sec], partner,
        )

    def es_over(sec):
        return remote(
            refs["es_sum"], refs["es_got"], refs["osem"].at[0], refs["osem"].at[1], other
        )

    def es_start(sec):
        @pl.when(jnp.logical_not(own))
        def _():
            es_copy(sec).start()

    def es_total(sec):
        @pl.when(own)
        def _():
            es_copy(sec).wait_recv()
            total = es[sec].astype(F32) + refs["es_came"][sec].astype(F32)

            @pl.when(core == sec)
            def _():
                refs["es_out"][...] = total

            @pl.when(core != sec)
            def _():
                refs["es_sum"][...] = total
                es_over(sec).start()

        @pl.when(jnp.logical_not(own))
        def _():
            es_copy(sec).wait_send()

    def es_end():
        @pl.when(own)
        def _():
            es_over(0).wait_send()

        @pl.when(jnp.logical_not(own))
        def _():
            es_over(0).wait_recv()
            refs["es_out"][...] = refs["es_got"][...]

    wait_weights(0)
    for r in (0, 2, 1, 3):
        low, high = r * (BS // HEAD), (r + 1) * (BS // HEAD)

        @pl.when(jnp.logical_not(own))
        def _():
            x_copy(r).wait_recv()

        front(0, x0, low, high)
        values(0, span=(low, high))
    wait_seq(0)
    for i in range(CHUNKS):
        first_mix(0, i, f0)
    gates(0)

    def e_copy(j):
        at = pl.ds(j * (BS // 2), BS // 2)
        return remote(
            refs["cotangent"].at[1 - half, at], e1.at[at], refs["ysem"].at[0, j],
            refs["ysem"].at[1, j], foreign,
        )

    def send_e(j):
        for r in range(j * HEAD // 2, (j + 1) * HEAD // 2):
            x_copy(r).wait_send()

        @pl.when(core == 1)
        def _():
            send_seq()

        e_copy(j).start()

    @pl.when(own)
    def _():
        send_e(0)

    @pl.when(jnp.logical_not(own))
    def _():
        send_e(1)

    for i in range(CHUNKS):
        second_mix(0, i, f0)
    for i in range(CHUNKS):
        finish(0, i, f0, x0, x1)

    wait_weights(1)
    wait_seq(1)
    front(1, x1, 0, BS)
    for i in range(CHUNKS):
        each_l = KB // CHUNKS
        values(1, cols=(i * each_l, (i + 1) * each_l))
        first_mix(1, i, f1)
    gates(1)

    @pl.when(own)
    def _():
        own_cotangent().wait()

    @pl.when(jnp.logical_not(own))
    def _():
        e_copy(0).wait_recv()
        e_copy(1).wait_recv()

    for i in range(CHUNKS):
        first_back(1, e1, i, r1)
    for i in range(CHUNKS):
        second_mix(1, i, f1)
    for i in range(CHUNKS):
        second_back(1, i, r1)
    for i in range(CHUNKS):
        finish(1, i, f1, x1, last)

    def fin_home():
        return remote(
            last, final.at[half], refs["fsem"].at[0, 0], refs["fsem"].at[1, 0], partner
        )

    def fin_core(m, j):
        return remote(
            final.at[m], final.at[m], refs["fsem"].at[0, j], refs["fsem"].at[1, j], other
        )

    @pl.when(jnp.logical_not(own))
    def _():
        fin_home().start()

    @pl.when(own)
    def _():
        final[half] = last[...]
        fin_core(half, 1).start()

    gate_back(1, e1)
    outer_grad(1, 0)
    inner_grad(1, 0)
    sum_cores(1, 0)
    seq_outer_grad(1, f1, r1)
    value_back(1, r1)
    sum_scatter(1, 0)
    middle_back(0, upv, vo.at[1])
    hidden_back(1, x1, e1, dx1)

    for i in range(CHUNKS):
        first_back(0, dx1, i, r0)
    inner_grad(1, 1)
    sum_cores(1, 1)
    seq_inner_grad(1, r1)
    es_start(1)
    sum_partner(1, 0)
    for i in range(CHUNKS):
        second_back(0, i, r0)
    sum_scatter(1, 1)
    gate_back(0, dx1)
    outer_grad(0, 0)
    inner_grad(0, 0)
    sum_cores(0, 0)
    seq_outer_grad(0, f0, r0)
    sum_gather(1, 0)
    value_back(0, r0)
    sum_scatter(0, 0)
    sum_partner(1, 1)
    middle_back(0, upv, vo.at[0])
    inner_grad(0, 1)
    hidden_back(0, x0)
    sum_cores(0, 1)
    seq_inner_grad(0, r0)
    es_start(0)
    sum_scatter(0, 1)
    sum_gather(1, 1)
    sum_partner(0, 0)
    es_total(1)
    sum_gather(0, 0)


    @pl.when(own)
    def _():
        e_copy(0).wait_send()
        fin_core(half, 1).wait_send()
        remote(
            last, final.at[1 - half], refs["fsem"].at[0, 0], refs["fsem"].at[1, 0], partner
        ).wait_recv()
        fin_core(1 - half, 2).start()

    @pl.when(jnp.logical_not(own))
    def _():
        e_copy(1).wait_send()
        fin_home().wait_send()

    sum_partner(0, 1)
    sum_finish(1, 0)
    sum_finish(1, 1)
    sum_gather(0, 1)
    es_total(0)
    es_end()

    @pl.when(own)
    def _():
        fin_core(1 - half, 2).wait_send()

    @pl.when(jnp.logical_not(own))
    def _():
        fin_core(half, 1).wait_recv()
        fin_core(1 - half, 2).wait_recv()
        for copy in seq_copies(core, other, 1):
            copy.wait_send()

    for copy in weight_copies(core):
        copy.wait_send()
    for copy in seq_copies(core, foreign, 0):
        copy.wait_send()
    sum_finish(0, 0)
    sum_finish(0, 1)


INPUTS = (
    "fields", "cotangent", "assignment", "gain", "vin", "vout", "gin", "gout", "sin", "sout",
)
OUTPUTS = ("final", "full0", "full1", "es_out")


def scratch(n, rows):
    pad = rows // n
    each = chunk_rows(n)
    hn = n // 2
    vmem, dma = pltpu.VMEM, pltpu.SemaphoreType.DMA
    plane = (BS, D)

    def by_part(name, shape):
        return {f"{name}{p}": vmem(shape(size), BF16) for p, size in enumerate(each)}

    return {
        **{f"fv{r}": vmem((8, BS // HEAD, D), BF16) for r in range(HEAD)},
        "xs": vmem(plane, BF16),
        "x0": vmem(plane, BF16),
        "x1": vmem(plane, BF16),
        "e": vmem(plane, BF16),
        "dx": vmem(plane, BF16),
        "last": vmem(plane, BF16),
        "w": vmem((2, KB, WB, 2 * WB), BF16),
        "vraw": vmem((2, KB, KB, WB), BF16),
        "graw": vmem((2, KB, KB, WB), BF16),
        "vo": vmem((2, KB, KB, WB), F32),
        "go": vmem((2, KB, KB, WB), F32),
        "gain_s": vmem((2, KB, WB), F32),
        "sxmine": vmem((rows, rows), BF16),
        "sins": vmem((2, rows, BS), BF16),
        "sxs": vmem((2, rows, rows), BF16),
        "h": vmem((2, BS, D), BF16),
        "t": vmem((2, KB, BS, 2 * WB), BF16),
        "v": vmem((2, BS, D), BF16),
        "g": vmem((2, BS, D), BF16),
        "s": vmem((2, BS, D), BF16),
        "a": vmem((4, CHUNKS, n, pad, WIDE), BF16),
        "b": vmem((8, CHUNKS, n, pad, WIDE), BF16),
        "upv": vmem(plane, F32),
        "upg": vmem(plane, F32),
        "dt": vmem((KB, BS, 2 * WB), BF16),
        "dh": vmem(plane, F32),
        "og": vmem((OUTER, WB), F32),
        **by_part("flat", lambda size: (2, n * size, WB)),
        **by_part("came", lambda size: (2, hn, size, WB)),
        **by_part("land", lambda size: (2, hn, size, WB)),
        **by_part("part", lambda size: (2, size, WB)),
        **by_part("came_part", lambda size: (2, size, WB)),
        **by_part("mine", lambda size: (2, size, WB)),
        "es": vmem((2, rows + BS, BS), BF16),
        "es_came": vmem((2, rows + BS, BS), BF16),
        "es_sum": vmem((rows + BS, BS), F32),
        "es_got": vmem((rows + BS, BS), F32),
        "lx": dma((HEAD,)),
        "le": dma,
        "lw": dma((5,)),
        "xsem": dma((2, HEAD)),
        "wsem": dma((2, 5)),
        "ssem": dma((2, 2, 2)),
        "ysem": dma((2, 2)),
        "ex": dma((2, 2, 2, CHUNKS)),
        "csem": dma((2, 2, 2, hn)),
        "rsem": dma((2, 2, 2)),
        "psem": dma((2, 2, 2)),
        "gsem": dma((2, 2, 2)),
        "esem": dma((2, 2)),
        "osem": dma((2,)),
        "fsem": dma((2, 3)),
    }


def step(n, *args):
    rows = args[INPUTS.index("sin")].shape[0]
    whole = scratch(n, rows)
    names = INPUTS + OUTPUTS + tuple(whole)
    anywhere = pl.BlockSpec(memory_space=pl.ANY)
    vmem = pl.BlockSpec(memory_space=pltpu.VMEM)
    places = {"sin": vmem, "sout": vmem, "assignment": pl.BlockSpec(memory_space=pltpu.SMEM)}

    def kernel(*refs):
        step_kernel(n, dict(zip(names, refs)))

    return pl.pallas_call(
        kernel,
        out_shape=(
            jax.ShapeDtypeStruct((2, BS, D), BF16),
            *(jax.ShapeDtypeStruct((n, size, WB), BF16) for size in chunk_rows(n)),
            jax.ShapeDtypeStruct((rows + BS, BS), F32),
        ),
        in_specs=[places.get(name, anywhere) for name in INPUTS],
        out_specs=(vmem,) * len(OUTPUTS),
        scratch_shapes=list(whole.values()),
        compiler_params=pltpu.CompilerParams(
            collective_id=0, has_side_effects=True, vmem_limit_bytes=60 * 2**20
        ),
        name="whole_step",
    )(*args)


def on_device(
    fields, cotangent, assignment, norm_gain, value_inner, value_outer,
    gate_inner, gate_outer, seq_inner, seq_outer,
):
    n = lax.axis_size("seq")
    each = BS // n
    pad = max(each, 8)
    rows = n * pad
    sin = jnp.pad(seq_inner[0].reshape(n, each, BS), ((0, 0), (0, pad - each), (0, 0)))
    final, gate, value, es = step(
        n, fields, cotangent, assignment, norm_gain[0].reshape(KB, WB), value_inner[0],
        value_outer[0], gate_inner[0], gate_outer[0], sin.reshape(rows, BS),
        seq_outer[0].reshape(BS, n),
    )
    final, gain, vin, vout, gin, gout, esin, esx = write_outputs(
        n, rows, final, gate.reshape(-1, WB), value.reshape(-1, WB), es
    )
    return (
        final,
        gain,
        vin.reshape(1, KB, WB, WB),
        vout.reshape(1, KB, KB, WB),
        gin.reshape(1, KB, WB, WB),
        gout.reshape(1, KB, KB, WB),
        esin.reshape(n, pad, BS)[:, :each].reshape(1, 1, BS, BS),
        esx.reshape(1, each, n, n),
    )


def write_kernel(
    rows, final_ref, gate_ref, value_ref, es_ref, final_out, gain_out, vin_out, vout_out,
    gin_out, gout_out, esin_out, esx_out, final_in, gate_in, value_in, es_in, gin_s, gout_s,
    vin_s, vout_s, sems,
):
    def copy(src, dst, j):
        made = pltpu.make_async_copy(src, dst, sems.at[j])
        made.start()
        return made

    gate = copy(gate_ref, gate_in, 0)
    value = copy(value_ref, value_in, 1)
    final = copy(final_ref, final_in, 2)
    es = copy(es_ref, es_in, 3)
    gate.wait()
    gin_s[...] = gate_in[:D, :].astype(F32)
    stores = [copy(gin_s, gin_out, 4)]
    gout_s[...] = gate_in[D : D + OUTER, :].astype(F32)
    stores.append(copy(gout_s, gout_out, 5))
    value.wait()
    vin_s[...] = value_in[:D, :].astype(F32)
    stores.append(copy(vin_s, vin_out, 6))
    vout_s[...] = value_in[D : D + OUTER, :].astype(F32)
    stores.append(copy(vout_s, vout_out, 7))
    final.wait()
    stores.append(copy(final_in, final_out, 8))
    gains = value_in[D + OUTER : PARTS[1], :].astype(F32)
    for k in range(KB):
        gain_out[:, k * WB : (k + 1) * WB] = gains[k : k + 1, :]
    es.wait()
    esin_out[...] = es_in[:rows, :]
    esx_out[...] = es_in[rows:, : esx_out.shape[1]]
    for store in stores:
        store.wait()


def write_outputs(n, rows, final, gate, value, es):
    vmem = pl.BlockSpec(memory_space=pltpu.VMEM)
    anywhere = pl.BlockSpec(memory_space=pl.ANY)
    shapes = ((1, D), (D, WB), (OUTER, WB), (D, WB), (OUTER, WB), (rows, BS), (BS, n))
    return pl.pallas_call(
        functools.partial(write_kernel, rows),
        out_shape=(
            jax.ShapeDtypeStruct((2, BS, D), BF16),
            *(jax.ShapeDtypeStruct(shape, F32) for shape in shapes),
        ),
        in_specs=[anywhere] * 4,
        out_specs=(anywhere, vmem, anywhere, anywhere, anywhere, anywhere, vmem, vmem),
        scratch_shapes=[
            *(pltpu.VMEM(array.shape, array.dtype) for array in (final, gate, value, es)),
            *(pltpu.VMEM(shape, F32) for shape in ((D, WB), (OUTER, WB)) * 2),
            pltpu.SemaphoreType.DMA((9,)),
        ],
        compiler_params=pltpu.CompilerParams(vmem_limit_bytes=60 * 2**20),
        name="write_outputs",
    )(final, gate, value, es)


def solution(mesh):
    in_specs = (
        P(None, "seq", None),
        P(None, "seq", None),
        P(),
        P("section", None),
        P("section", None, None, None),
        P("section", None, None, None),
        P("section", None, None, None),
        P("section", None, None, None),
        P("section", "seq", None, None),
        P("section", "seq", None, None),
    )
    out_specs = (
        P(None, "seq", None),
        P("section", None),
        P("section", None, None, None),
        P("section", None, None, None),
        P("section", None, None, None),
        P("section", None, None, None),
        P("section", "seq", None, None),
        P("section", "seq", None, None),
    )
    return jax.shard_map(
        on_device, mesh=mesh, in_specs=in_specs, out_specs=out_specs, check_vma=False
    )
```

```python
import functools

import jax
import jax.numpy as jnp
from jax import lax
from jax.experimental import pallas as pl
from jax.experimental.pallas import tpu as pltpu
from jax.sharding import PartitionSpec as P

D = 2048
WB = 128
BS = 128
KB = 16
EPSILON = 1e-06
F32 = jnp.float32
BF16 = jnp.bfloat16
MESH = pl.DeviceIdType.MESH
WIDE = 512
CHUNKS = D // WIDE
HEAD = 4
OUTER = KB * KB
PARTS = (D + OUTER, D + OUTER + KB)


def dot(a, b, ca, cb):
    return lax.dot_general(a, b, (((ca,), (cb,)), ((), ())), preferred_element_type=F32)


def chunk_rows(n):
    return [-(-count // (16 * n)) * 16 for count in PARTS]


def remote(src, dst, send, recv, device):
    return pltpu.make_async_remote_copy(
        src_ref=src, dst_ref=dst, send_sem=send, recv_sem=recv,
        device_id=device, device_id_type=MESH,
    )


def in_half(n, block):
    half = lax.axis_index("seq") // (n // 2)
    return {"section": block // (n // 2), "seq": half * (n // 2) + lax.rem(block, n // 2)}


def send_all(n, me, i, src, dst, sems):
    def one(d, c):
        peer = lax.rem(me + d, n)
        remote(
            src.at[i, peer], dst.at[i, me], sems[0].at[i], sems[1].at[i], in_half(n, peer)
        ).start()
        return c

    lax.fori_loop(1, n, one, 0)
    dst[i, me] = src[i, me]


def wait_all(n, me, i, src, dst, sems):
    others = pl.ds(0, n - 1)
    copy = remote(
        src.at[i, others], dst.at[i, others], sems[0].at[i], sems[1].at[i],
        in_half(n, lax.rem(me + 1, n)),
    )
    copy.wait_send()
    copy.wait_recv()


def copies(count, rows, pad):
    at = lax.broadcasted_iota(jnp.int32, (count, rows), 0)
    to = lax.broadcasted_iota(jnp.int32, (count, rows), 1)
    return jnp.where(to // pad == at, 1.0, 0.0).astype(BF16)


def same_place(rows, pad):
    at = lax.broadcasted_iota(jnp.int32, (rows, rows), 0)
    to = lax.broadcasted_iota(jnp.int32, (rows, rows), 1)
    return at % pad == to % pad


def by_place(n, rows):
    pad = rows // n
    at = lax.broadcasted_iota(jnp.int32, (rows, BS), 0)
    to = lax.broadcasted_iota(jnp.int32, (rows, BS), 1)
    hit = (at % pad * n + at // pad == to) & (at % pad < BS // n)
    return jnp.where(hit, 1.0, 0.0).astype(BF16)


def spread_rows(n, rows):
    pad = rows // n
    each = BS // n
    at = lax.broadcasted_iota(jnp.int32, (rows, BS), 0)
    to = lax.broadcasted_iota(jnp.int32, (rows, BS), 1)
    hit = (at // pad * each + at % pad == to) & (at % pad < each)
    return jnp.where(hit, 1.0, 0.0).astype(BF16)


def cross(read, write, b_ref, back, cols=(0, KB), rows=(0, BS)):
    def group(i, c):
        at = pl.ds(pl.multiple_of(i * 16, 16), 16)
        parts = [read(k, at).astype(F32) for k in range(KB)]
        for l in range(*cols):
            total = None
            for k in range(KB):
                row = b_ref[l, k : k + 1, :] if back else b_ref[k, l : l + 1, :]
                term = parts[k] * row
                total = term if total is None else total + term
            write(l, at, total)
        return c

    lax.fori_loop(rows[0] // 16, rows[1] // 16, group, 0)


def row_factor(wide):
    return lax.rsqrt(jnp.mean(wide * wide, axis=-1, keepdims=True) + EPSILON)


def step_kernel(n, refs):
    hn = n // 2
    each = chunk_rows(n)
    core = lax.axis_index("section")
    chip = lax.axis_index("seq")
    half = chip // hn
    k_me = lax.rem(chip, hn)
    me = core * hn + k_me
    own = core == half
    partner_chip = lax.rem(chip + hn, n)
    partner = {"section": core, "seq": partner_chip}
    foreign = {"section": half, "seq": partner_chip}
    other = {"section": 1 - core, "seq": chip}
    rows = refs["sin"].shape[0]
    pad = rows // n
    x0, x1, e1, dx1 = refs["x0"], refs["x1"], refs["e"], refs["dx"]
    w, vo, go, gain = refs["w"], refs["vo"], refs["go"], refs["gain_s"]
    sins, sxs = refs["sins"], refs["sxs"]
    hid, mid, val, gat, mix = (refs[name] for name in ("h", "t", "v", "g", "s"))
    flat, es = (refs["flat0"], refs["flat1"]), refs["es"]
    last, final = refs["last"], refs["final"]
    upv, upg, dt, dh = refs["upv"], refs["upg"], refs["dt"], refs["dh"]

    def piece_of_fields(r):
        at = pl.ds(r * (BS // HEAD), BS // HEAD)
        return pltpu.make_async_copy(
            refs["fields"].at[:, at], refs[f"fv{r}"], refs["lx"].at[r]
        )

    def own_cotangent():
        return pltpu.make_async_copy(refs["cotangent"].at[half], e1, refs["le"])

    def weight_parts():
        left, right = pl.ds(0, WB), pl.ds(WB, WB)
        return [
            (refs["vin"], w.at[core, :, :, left]),
            (refs["gin"], w.at[core, :, :, right]),
            (refs["vout"], refs["vraw"].at[core]),
            (refs["gout"], refs["graw"].at[core]),
            (refs["gain"], gain.at[core]),
        ]

    def weight_parts_of(sec):
        left, right = pl.ds(0, WB), pl.ds(WB, WB)
        return [
            (refs["vin"], w.at[sec, :, :, left]),
            (refs["gin"], w.at[sec, :, :, right]),
            (refs["vout"], refs["vraw"].at[sec]),
            (refs["gout"], refs["graw"].at[sec]),
            (refs["gain"], gain.at[sec]),
        ]

    @pl.when(own)
    def _():
        for r in range(HEAD):
            piece_of_fields(r).start()

    @pl.when(jnp.logical_not(own))
    def _():
        for r in range(HEAD // 2, HEAD):
            piece_of_fields(r).start()

    for j, (src, dst) in enumerate(weight_parts()):
        pltpu.make_async_copy(src, dst, refs["lw"].at[j]).start()

    barrier = pltpu.get_barrier_semaphore()

    def greet(d, c):
        pl.semaphore_signal(
            barrier, inc=1, device_id=in_half(n, lax.rem(me + d, n)), device_id_type=MESH
        )
        return c

    lax.fori_loop(1, n, greet, 0)
    for number in range(2):
        pl.semaphore_signal(
            barrier, inc=1, device_id={"section": number, "seq": partner_chip}, device_id_type=MESH
        )

    wide = dot(refs["sout"][...], copies(n, rows, pad), 1, 0).astype(BF16)
    placed = dot(by_place(n, rows), wide, 1, 0)
    refs["sxmine"][...] = jnp.where(same_place(rows, pad), placed, 0.0).astype(BF16)

    pl.semaphore_wait(barrier, n + 1)

    def x_copy(r):
        at = pl.ds(r * (BS // HEAD), BS // HEAD)
        return remote(
            refs["xs"].at[at], x0.at[at], refs["xsem"].at[0, r], refs["xsem"].at[1, r], foreign
        )

    def weight_copies(sec):
        return [
            remote(src, dst, refs["wsem"].at[0, j], refs["wsem"].at[1, j], other)
            for j, (src, dst) in enumerate(weight_parts_of(sec))
        ]

    def seq_copies(sec, device, row):
        return [
            remote(
                refs[src], refs[dst].at[sec], refs["ssem"].at[0, row, j],
                refs["ssem"].at[1, sec, j], device,
            )
            for j, (src, dst) in enumerate((("sin", "sins"), ("sxmine", "sxs")))
        ]

    mine, theirs = refs["assignment"][half], refs["assignment"][1 - half]

    def rows_of(r):
        return slice(r * (BS // HEAD), (r + 1) * (BS // HEAD))

    def send_x(r):
        refs["xs"][rows_of(r), :] = refs[f"fv{r}"][theirs]
        x_copy(r).start()

    @pl.when(own)
    def _():
        for r in range(HEAD):
            piece_of_fields(r).wait()
            if r < HEAD // 2:
                send_x(r)

    @pl.when(jnp.logical_not(own))
    def _():
        for r in range(HEAD // 2, HEAD):
            piece_of_fields(r).wait()
            send_x(r)

    for copy in weight_copies(core):
        copy.start()
    def send_seq():
        for copy in seq_copies(core, foreign, 0):
            copy.start()

        @pl.when(jnp.logical_not(own))
        def _():
            for copy in seq_copies(core, other, 1):
                copy.start()

    @pl.when(core == 0)
    def _():
        send_seq()

    @pl.when(own)
    def _():
        sins[core] = refs["sin"][...]
        sxs[core] = refs["sxmine"][...]
        own_cotangent().start()
        for r in range(HEAD):
            x0[rows_of(r), :] = refs[f"fv{r}"][mine]

    def wait_weights(sec):
        @pl.when(core == sec)
        def _():
            for j, (src, dst) in enumerate(weight_parts()):
                pltpu.make_async_copy(src, dst, refs["lw"].at[j]).wait()

        @pl.when(core != sec)
        def _():
            for copy in weight_copies(sec):
                copy.wait_recv()

        vo[sec] = refs["vraw"][sec].astype(F32)
        go[sec] = refs["graw"][sec].astype(F32)

    def wait_seq(sec):
        @pl.when(jnp.logical_not(own & (core == sec)))
        def _():
            for copy in seq_copies(sec, other, 0):
                copy.wait_recv()

    def front(sec, x_ref, low, high):
        at = slice(low, high)
        factor = row_factor(x_ref[at, :].astype(F32))
        for k in range(KB):
            cols = slice(k * WB, (k + 1) * WB)
            hidden = (
                x_ref[at, cols].astype(F32) * factor * gain[sec, k : k + 1, :]
            ).astype(BF16)
            hid[sec, at, cols] = hidden
            mid[sec, k, at, :] = dot(hidden, w[sec, k], 1, 0).astype(BF16)

    def mixed_into(ref, sec):
        def write(l, at, value):
            ref[sec, at, l * WB : (l + 1) * WB] = value.astype(BF16)

        return write

    def values(sec, cols=(0, KB), span=(0, BS)):
        cross(
            lambda k, at: mid[sec, k, at, :WB], mixed_into(val, sec), vo.at[sec], False, cols, span
        )

    def gates(sec):
        cross(lambda k, at: mid[sec, k, at, WB:], mixed_into(gat, sec), go.at[sec], False)

    def columns(i):
        return slice(i * WIDE, (i + 1) * WIDE)

    def got(ref, i):
        return ref[i].astype(F32).reshape(rows, WIDE).astype(BF16)

    def send(value, i, ex):
        a, b, sems = ex
        a[i] = value.reshape(n, pad, WIDE).astype(BF16)
        send_all(n, me, i, a, b, sems)

    def wait(i, ex):
        a, b, sems = ex
        wait_all(n, me, i, a, b, sems)

    def exchange(a, b, call, first):
        sems = refs["ex"]
        return refs["a"].at[a], refs["b"].at[b], (sems.at[first, 0, call], sems.at[first, 1, call])

    f0 = [exchange(0, 0, 0, 0), exchange(1, 1, 1, 0)]
    f1 = [exchange(0, 2, 0, 0), exchange(1, 3, 1, 0)]
    r1 = [exchange(2, 4, 0, 1), exchange(3, 5, 1, 1)]
    r0 = [exchange(0, 6, 0, 0), exchange(1, 7, 1, 0)]

    def first_mix(sec, i, ex):
        send(dot(sins[sec], val[sec, :, columns(i)], 1, 0), i, ex[0])

    def second_mix(sec, i, ex):
        wait(i, ex[0])
        send(dot(sxs[sec], got(ex[0][1], i), 1, 0), i, ex[1])

    def finish(sec, i, ex, x_ref, out_ref):
        wait(i, ex[1])
        cols = columns(i)
        mixed = ex[1][1][i].astype(F32).reshape(rows, WIDE)
        if rows != BS:
            mixed = dot(spread_rows(n, rows), mixed.astype(BF16), 0, 0)
        mix[sec, :, cols] = mixed.astype(BF16)
        out_ref[:, cols] = (
            x_ref[:, cols].astype(F32) + mixed * gat[sec, :, cols].astype(F32)
        ).astype(BF16)

    def first_back(sec, e_ref, i, ex):
        cols = columns(i)
        ds = e_ref[:, cols].astype(F32) * gat[sec, :, cols].astype(F32)
        if rows != BS:
            ds = dot(spread_rows(n, rows), ds.astype(BF16), 1, 0)
        send(ds, i, ex[0])

    def second_back(sec, i, ex):
        wait(i, ex[0])
        send(dot(sxs[sec], got(ex[0][1], i), 0, 0), i, ex[1])

    def middle_back(first, up, b_ref):
        def write(k, at, value):
            dt[k, at, first : first + WB] = value.astype(BF16)

        cross(lambda l, at: up[at, l * WB : (l + 1) * WB], write, b_ref, True)

    def gate_back(sec, e_ref):
        for i in range(CHUNKS):
            cols = columns(i)
            dg = e_ref[:, cols].astype(F32) * mix[sec, :, cols].astype(F32)
            upg[:, cols] = dg.astype(BF16).astype(F32)
        middle_back(WB, upg, go.at[sec])

    def value_back(sec, ex):
        for i in range(CHUNKS):
            wait(i, ex[1])
            upv[:, columns(i)] = (
                dot(sins[sec], got(ex[1][1], i), 0, 0).astype(BF16).astype(F32)
            )
            outer_grad(sec, 1, (i * KB // CHUNKS, (i + 1) * KB // CHUNKS))

    def outer_grad(sec, p, cols=(0, KB)):
        up = (upg, upv)[p]
        first = (1 - p) * WB

        def block(k, c):
            middle = mid[sec, k, :, first : first + WB].astype(F32)
            for l in range(*cols):
                both = middle * up[:, l * WB : (l + 1) * WB]
                refs["og"][pl.ds(k * KB + l, 1), :] = jnp.sum(both, axis=0, keepdims=True)
            return c

        lax.fori_loop(0, KB, block, 0)

    def inner_grad(sec, p):
        half_of = slice((1 - p) * WB, (2 - p) * WB)
        for k in range(KB):
            cols = slice(k * WB, (k + 1) * WB)
            flat[p][sec, cols, :] = dot(hid[sec, :, cols], dt[k, :, half_of], 0, 0).astype(BF16)
        flat[p][sec, D : D + OUTER, :] = refs["og"][...].astype(BF16)
        left = n * each[p] - PARTS[p]
        if left:
            flat[p][sec, PARTS[p] :, :] = jnp.zeros((left, WB), BF16)

    def hidden_back(sec, x_ref, e_ref=None, dx_ref=None):
        factor = row_factor(x_ref[...].astype(F32))
        lean = jnp.zeros((BS, WB), F32)
        gains = []
        for k in range(KB):
            cols = slice(k * WB, (k + 1) * WB)
            part = dot(dt[k], w[sec, k], 1, 1)
            seen = part * x_ref[:, cols].astype(F32)
            gains.append(jnp.sum(seen * factor, axis=0, keepdims=True))
            if dx_ref is not None:
                lean += gain[sec, k : k + 1, :] * seen
                dh[:, cols] = gain[sec, k : k + 1, :] * part
        flat[1][sec, D + OUTER : PARTS[1], :] = jnp.concatenate(gains, axis=0).astype(BF16)
        if dx_ref is None:
            return
        mean = jnp.sum(lean, axis=-1, keepdims=True) * (1.0 / D)
        pull = factor * factor * factor * mean
        for k in range(KB):
            cols = slice(k * WB, (k + 1) * WB)
            dx_ref[:, cols] = (
                e_ref[:, cols].astype(F32)
                + factor * dh[:, cols]
                - x_ref[:, cols].astype(F32) * pull
            ).astype(BF16)

    def seq_outer_grad(sec, fwd, back):
        pairs = jnp.zeros((rows, rows), F32)
        for i in range(CHUNKS):
            pairs += dot(got(back[0][1], i), got(fwd[0][1], i), 1, 1)
        kept = jnp.where(same_place(rows, pad), pairs, 0.0).astype(BF16)
        moved = dot(by_place(n, rows), kept, 0, 0).astype(BF16)
        es[sec, rows:, :] = dot(moved, copies(BS, rows, pad), 1, 1).astype(BF16)

    def seq_inner_grad(sec, back):
        inner = jnp.zeros((rows, BS), F32)
        for i in range(CHUNKS):
            inner += dot(got(back[1][1], i), val[sec, :, columns(i)], 1, 1)
        es[sec, :rows, :] = inner.astype(BF16)

    def of(name, p):
        return refs[f"{name}{p}"]

    def width(p, piece):
        return pl.ds(pl.multiple_of(piece * each[p], 16), each[p])

    def across(sec, p, d):
        kk = lax.rem(k_me + d, hn)
        return remote(
            flat[p].at[sec, width(p, (1 - core) * hn + kk)], of("came", p).at[sec, kk],
            refs["csem"].at[0, sec, p, d], refs["csem"].at[1, sec, p, d], other,
        )

    def in_core(kk):
        return {"section": core, "seq": half * hn + kk}

    def sum_cores(sec, p):
        def one(d, c):
            across(sec, p, lax.rem(d, hn)).start()
            return c

        lax.fori_loop(1, hn + 1, one, 0)

    def sum_scatter(sec, p):
        sems = (refs["rsem"].at[0, sec, p], refs["rsem"].at[1, sec, p])

        def one(j, c):
            d = lax.rem(j, hn)
            kk = lax.rem(k_me + d, hn)
            across(sec, p, d).wait_recv()
            at = width(p, core * hn + kk)
            total = flat[p][sec, at, :].astype(F32) + of("came", p)[sec, kk].astype(F32)
            flat[p][sec, at, :] = total.astype(BF16)

            @pl.when(d != 0)
            def _():
                remote(
                    flat[p].at[sec, at], of("land", p).at[sec, k_me], *sems, in_core(kk)
                ).start()

            return c

        lax.fori_loop(1, hn + 1, one, 0)
        of("land", p)[sec, k_me] = flat[p][sec, width(p, core * hn + k_me), :]

    def partner_copy(sec, p):
        return remote(
            of("part", p).at[sec], of("came_part", p).at[sec], refs["psem"].at[0, sec, p],
            refs["psem"].at[1, sec, p], partner,
        )

    def sum_partner(sec, p):
        land = of("land", p)
        others = pl.ds(0, hn - 1)
        copy = remote(
            land.at[sec, others], land.at[sec, others], refs["rsem"].at[0, sec, p],
            refs["rsem"].at[1, sec, p], in_core(lax.rem(k_me + 1, hn)),
        )
        copy.wait_send()
        copy.wait_recv()
        total = land[sec, 0].astype(F32)
        for q in range(1, hn):
            total = total + land[sec, q].astype(F32)
        of("part", p)[sec] = total.astype(BF16)
        partner_copy(sec, p).start()

    def gather_copy(sec, p, kk):
        return remote(
            of("mine", p).at[sec], of("full", p).at[me], refs["gsem"].at[0, sec, p],
            refs["gsem"].at[1, sec, p], {"section": sec, "seq": half * hn + kk},
        )

    def sum_gather(sec, p):
        copy = partner_copy(sec, p)
        copy.wait_send()
        copy.wait_recv()
        total = of("part", p)[sec].astype(F32) + of("came_part", p)[sec].astype(F32)
        of("mine", p)[sec] = total.astype(BF16)

        def one(d, c):
            gather_copy(sec, p, lax.rem(k_me + d, hn)).start()
            return c

        lax.fori_loop(1, hn, one, 0)

        @pl.when(core != sec)
        def _():
            gather_copy(sec, p, k_me).start()

        @pl.when(core == sec)
        def _():
            of("full", p)[me] = of("mine", p)[sec]

    def sum_finish(sec, p):
        def cross_sent(d, c):
            across(sec, p, d).wait_send()
            return c

        lax.fori_loop(0, hn, cross_sent, 0)

        def several(count):
            some = of("full", p).at[pl.ds(0, count)]
            return remote(
                some, some, refs["gsem"].at[0, sec, p], refs["gsem"].at[1, sec, p], partner
            )

        @pl.when(core != sec)
        def _():
            several(hn).wait_send()

        @pl.when(core == sec)
        def _():
            several(hn - 1).wait_send()
            several(n - 1).wait_recv()

    def es_copy(sec):
        return remote(
            es.at[sec], refs["es_came"].at[sec], refs["esem"].at[0, sec],
            refs["esem"].at[1, sec], partner,
        )

    def es_over(sec):
        return remote(
            refs["es_sum"], refs["es_got"], refs["osem"].at[0], refs["osem"].at[1], other
        )

    def es_start(sec):
        @pl.when(jnp.logical_not(own))
        def _():
            es_copy(sec).start()

    def es_total(sec):
        @pl.when(own)
        def _():
            es_copy(sec).wait_recv()
            total = es[sec].astype(F32) + refs["es_came"][sec].astype(F32)

            @pl.when(core == sec)
            def _():
                refs["es_out"][...] = total

            @pl.when(core != sec)
            def _():
                refs["es_sum"][...] = total
                es_over(sec).start()

        @pl.when(jnp.logical_not(own))
        def _():
            es_copy(sec).wait_send()

    def es_end():
        @pl.when(own)
        def _():
            es_over(0).wait_send()

        @pl.when(jnp.logical_not(own))
        def _():
            es_over(0).wait_recv()
            refs["es_out"][...] = refs["es_got"][...]

    wait_weights(0)
    for r in (0, 2, 1, 3):
        low, high = r * (BS // HEAD), (r + 1) * (BS // HEAD)

        @pl.when(jnp.logical_not(own))
        def _():
            x_copy(r).wait_recv()

        front(0, x0, low, high)
        values(0, span=(low, high))
    wait_seq(0)
    for i in range(CHUNKS):
        first_mix(0, i, f0)
    gates(0)

    def e_copy(j):
        at = pl.ds(j * (BS // 2), BS // 2)
        return remote(
            refs["cotangent"].at[1 - half, at], e1.at[at], refs["ysem"].at[0, j],
            refs["ysem"].at[1, j], foreign,
        )

    def send_e(j):
        for r in range(j * HEAD // 2, (j + 1) * HEAD // 2):
            x_copy(r).wait_send()

        @pl.when(core == 1)
        def _():
            send_seq()

        e_copy(j).start()

    @pl.when(own)
    def _():
        send_e(0)

    @pl.when(jnp.logical_not(own))
    def _():
        send_e(1)

    for i in range(CHUNKS):
        second_mix(0, i, f0)
    for i in range(CHUNKS):
        finish(0, i, f0, x0, x1)

    wait_weights(1)
    wait_seq(1)
    front(1, x1, 0, BS)
    for i in range(CHUNKS):
        each_l = KB // CHUNKS
        values(1, cols=(i * each_l, (i + 1) * each_l))
        first_mix(1, i, f1)
    gates(1)

    @pl.when(own)
    def _():
        own_cotangent().wait()

    @pl.when(jnp.logical_not(own))
    def _():
        e_copy(0).wait_recv()
        e_copy(1).wait_recv()

    for i in range(CHUNKS):
        first_back(1, e1, i, r1)
    for i in range(CHUNKS):
        second_mix(1, i, f1)
    for i in range(CHUNKS):
        second_back(1, i, r1)
    for i in range(CHUNKS):
        finish(1, i, f1, x1, last)

    left, right = pl.ds(0, D // 2), pl.ds(D // 2, D // 2)
    home = {"section": 1 - half, "seq": partner_chip}

    def fin_home():
        return remote(
            last.at[:, left], final.at[half, :, left], refs["fsem"].at[0, 0],
            refs["fsem"].at[1, 0], partner,
        )

    def fin_lend():
        return remote(
            last.at[:, right], refs["lent"], refs["fsem"].at[0, 3], refs["fsem"].at[1, 3], other
        )

    def fin_lent():
        return remote(
            refs["lent"], final.at[half, :, right], refs["fsem"].at[0, 4],
            refs["fsem"].at[1, 4], home,
        )

    def fin_core(m, j):
        return remote(
            final.at[m], final.at[m], refs["fsem"].at[0, j], refs["fsem"].at[1, j], other
        )

    @pl.when(jnp.logical_not(own))
    def _():
        fin_lend().start()
        fin_home().start()

    @pl.when(own)
    def _():
        final[half] = last[...]
        fin_core(half, 1).start()

    gate_back(1, e1)

    @pl.when(own)
    def _():
        fin_lend().wait_recv()
        fin_lent().start()

    outer_grad(1, 0)
    inner_grad(1, 0)
    sum_cores(1, 0)
    seq_outer_grad(1, f1, r1)
    value_back(1, r1)
    sum_scatter(1, 0)
    middle_back(0, upv, vo.at[1])
    hidden_back(1, x1, e1, dx1)

    for i in range(CHUNKS):
        first_back(0, dx1, i, r0)
    inner_grad(1, 1)
    sum_cores(1, 1)
    seq_inner_grad(1, r1)
    es_start(1)
    sum_partner(1, 0)
    for i in range(CHUNKS):
        second_back(0, i, r0)
    sum_scatter(1, 1)
    gate_back(0, dx1)
    outer_grad(0, 0)
    inner_grad(0, 0)
    sum_cores(0, 0)
    seq_outer_grad(0, f0, r0)
    sum_gather(1, 0)
    value_back(0, r0)
    sum_scatter(0, 0)
    sum_partner(1, 1)
    middle_back(0, upv, vo.at[0])
    inner_grad(0, 1)
    hidden_back(0, x0)
    sum_cores(0, 1)
    seq_inner_grad(0, r0)
    es_start(0)
    sum_scatter(0, 1)
    sum_gather(1, 1)
    sum_partner(0, 0)
    es_total(1)
    sum_gather(0, 0)


    @pl.when(own)
    def _():
        e_copy(0).wait_send()
        fin_core(half, 1).wait_send()
        fin_lent().wait_send()
        for cols, j in ((left, 0), (right, 4)):
            into = final.at[1 - half, :, cols]
            remote(into, into, refs["fsem"].at[0, j], refs["fsem"].at[1, j], partner).wait_recv()
        fin_core(1 - half, 2).start()

    @pl.when(jnp.logical_not(own))
    def _():
        e_copy(1).wait_send()
        fin_home().wait_send()
        fin_lend().wait_send()

    sum_partner(0, 1)
    sum_gather(0, 1)
    sum_finish(1, 0)
    sum_finish(1, 1)
    es_total(0)
    es_end()

    @pl.when(own)
    def _():
        fin_core(1 - half, 2).wait_send()

    @pl.when(jnp.logical_not(own))
    def _():
        fin_core(half, 1).wait_recv()
        fin_core(1 - half, 2).wait_recv()
        for copy in seq_copies(core, other, 1):
            copy.wait_send()

    for copy in weight_copies(core):
        copy.wait_send()
    for copy in seq_copies(core, foreign, 0):
        copy.wait_send()
    sum_finish(0, 0)
    sum_finish(0, 1)


INPUTS = (
    "fields", "cotangent", "assignment", "gain", "vin", "vout", "gin", "gout", "sin", "sout",
)
OUTPUTS = ("final", "full0", "full1", "es_out")


def scratch(n, rows):
    pad = rows // n
    each = chunk_rows(n)
    hn = n // 2
    vmem, dma = pltpu.VMEM, pltpu.SemaphoreType.DMA
    plane = (BS, D)

    def by_part(name, shape):
        return {f"{name}{p}": vmem(shape(size), BF16) for p, size in enumerate(each)}

    return {
        **{f"fv{r}": vmem((8, BS // HEAD, D), BF16) for r in range(HEAD)},
        "xs": vmem(plane, BF16),
        "x0": vmem(plane, BF16),
        "x1": vmem(plane, BF16),
        "e": vmem(plane, BF16),
        "dx": vmem(plane, BF16),
        "last": vmem(plane, BF16),
        "lent": vmem((BS, D // 2), BF16),
        "w": vmem((2, KB, WB, 2 * WB), BF16),
        "vraw": vmem((2, KB, KB, WB), BF16),
        "graw": vmem((2, KB, KB, WB), BF16),
        "vo": vmem((2, KB, KB, WB), F32),
        "go": vmem((2, KB, KB, WB), F32),
        "gain_s": vmem((2, KB, WB), F32),
        "sxmine": vmem((rows, rows), BF16),
        "sins": vmem((2, rows, BS), BF16),
        "sxs": vmem((2, rows, rows), BF16),
        "h": vmem((2, BS, D), BF16),
        "t": vmem((2, KB, BS, 2 * WB), BF16),
        "v": vmem((2, BS, D), BF16),
        "g": vmem((2, BS, D), BF16),
        "s": vmem((2, BS, D), BF16),
        "a": vmem((4, CHUNKS, n, pad, WIDE), BF16),
        "b": vmem((8, CHUNKS, n, pad, WIDE), BF16),
        "upv": vmem(plane, F32),
        "upg": vmem(plane, F32),
        "dt": vmem((KB, BS, 2 * WB), BF16),
        "dh": vmem(plane, F32),
        "og": vmem((OUTER, WB), F32),
        **by_part("flat", lambda size: (2, n * size, WB)),
        **by_part("came", lambda size: (2, hn, size, WB)),
        **by_part("land", lambda size: (2, hn, size, WB)),
        **by_part("part", lambda size: (2, size, WB)),
        **by_part("came_part", lambda size: (2, size, WB)),
        **by_part("mine", lambda size: (2, size, WB)),
        "es": vmem((2, rows + BS, BS), BF16),
        "es_came": vmem((2, rows + BS, BS), BF16),
        "es_sum": vmem((rows + BS, BS), F32),
        "es_got": vmem((rows + BS, BS), F32),
        "lx": dma((HEAD,)),
        "le": dma,
        "lw": dma((5,)),
        "xsem": dma((2, HEAD)),
        "wsem": dma((2, 5)),
        "ssem": dma((2, 2, 2)),
        "ysem": dma((2, 2)),
        "ex": dma((2, 2, 2, CHUNKS)),
        "csem": dma((2, 2, 2, hn)),
        "rsem": dma((2, 2, 2)),
        "psem": dma((2, 2, 2)),
        "gsem": dma((2, 2, 2)),
        "esem": dma((2, 2)),
        "osem": dma((2,)),
        "fsem": dma((2, 5)),
    }


def step(n, *args):
    rows = args[INPUTS.index("sin")].shape[0]
    whole = scratch(n, rows)
    names = INPUTS + OUTPUTS + tuple(whole)
    anywhere = pl.BlockSpec(memory_space=pl.ANY)
    vmem = pl.BlockSpec(memory_space=pltpu.VMEM)
    places = {"sin": vmem, "sout": vmem, "assignment": pl.BlockSpec(memory_space=pltpu.SMEM)}

    def kernel(*refs):
        step_kernel(n, dict(zip(names, refs)))

    return pl.pallas_call(
        kernel,
        out_shape=(
            jax.ShapeDtypeStruct((2, BS, D), BF16),
            *(jax.ShapeDtypeStruct((n, size, WB), BF16) for size in chunk_rows(n)),
            jax.ShapeDtypeStruct((rows + BS, BS), F32),
        ),
        in_specs=[places.get(name, anywhere) for name in INPUTS],
        out_specs=(vmem,) * len(OUTPUTS),
        scratch_shapes=list(whole.values()),
        compiler_params=pltpu.CompilerParams(
            collective_id=0, has_side_effects=True, vmem_limit_bytes=60 * 2**20
        ),
        name="whole_step",
    )(*args)


def on_device(
    fields, cotangent, assignment, norm_gain, value_inner, value_outer,
    gate_inner, gate_outer, seq_inner, seq_outer,
):
    n = lax.axis_size("seq")
    each = BS // n
    pad = max(each, 8)
    rows = n * pad
    sin = jnp.pad(seq_inner[0].reshape(n, each, BS), ((0, 0), (0, pad - each), (0, 0)))
    final, gate, value, es = step(
        n, fields, cotangent, assignment, norm_gain[0].reshape(KB, WB), value_inner[0],
        value_outer[0], gate_inner[0], gate_outer[0], sin.reshape(rows, BS),
        seq_outer[0].reshape(BS, n),
    )
    final, gain, vin, vout, gin, gout, esin, esx = write_outputs(
        n, rows, final, gate.reshape(-1, WB), value.reshape(-1, WB), es
    )
    return (
        final,
        gain,
        vin.reshape(1, KB, WB, WB),
        vout.reshape(1, KB, KB, WB),
        gin.reshape(1, KB, WB, WB),
        gout.reshape(1, KB, KB, WB),
        esin.reshape(n, pad, BS)[:, :each].reshape(1, 1, BS, BS),
        esx.reshape(1, each, n, n),
    )


def write_kernel(
    rows, final_ref, gate_ref, value_ref, es_ref, final_out, gain_out, vin_out, vout_out,
    gin_out, gout_out, esin_out, esx_out, final_in, gate_in, value_in, es_in, gin_s, gout_s,
    vin_s, vout_s, sems,
):
    def copy(src, dst, j):
        made = pltpu.make_async_copy(src, dst, sems.at[j])
        made.start()
        return made

    gate = copy(gate_ref, gate_in, 0)
    value = copy(value_ref, value_in, 1)
    final = copy(final_ref, final_in, 2)
    es = copy(es_ref, es_in, 3)
    gate.wait()
    gin_s[...] = gate_in[:D, :].astype(F32)
    stores = [copy(gin_s, gin_out, 4)]
    gout_s[...] = gate_in[D : D + OUTER, :].astype(F32)
    stores.append(copy(gout_s, gout_out, 5))
    value.wait()
    vin_s[...] = value_in[:D, :].astype(F32)
    stores.append(copy(vin_s, vin_out, 6))
    vout_s[...] = value_in[D : D + OUTER, :].astype(F32)
    stores.append(copy(vout_s, vout_out, 7))
    final.wait()
    stores.append(copy(final_in, final_out, 8))
    gains = value_in[D + OUTER : PARTS[1], :].astype(F32)
    for k in range(KB):
        gain_out[:, k * WB : (k + 1) * WB] = gains[k : k + 1, :]
    es.wait()
    esin_out[...] = es_in[:rows, :]
    esx_out[...] = es_in[rows:, : esx_out.shape[1]]
    for store in stores:
        store.wait()


def write_outputs(n, rows, final, gate, value, es):
    vmem = pl.BlockSpec(memory_space=pltpu.VMEM)
    anywhere = pl.BlockSpec(memory_space=pl.ANY)
    shapes = ((1, D), (D, WB), (OUTER, WB), (D, WB), (OUTER, WB), (rows, BS), (BS, n))
    return pl.pallas_call(
        functools.partial(write_kernel, rows),
        out_shape=(
            jax.ShapeDtypeStruct((2, BS, D), BF16),
            *(jax.ShapeDtypeStruct(shape, F32) for shape in shapes),
        ),
        in_specs=[anywhere] * 4,
        out_specs=(anywhere, vmem, anywhere, anywhere, anywhere, anywhere, vmem, vmem),
        scratch_shapes=[
            *(pltpu.VMEM(array.shape, array.dtype) for array in (final, gate, value, es)),
            *(pltpu.VMEM(shape, F32) for shape in ((D, WB), (OUTER, WB)) * 2),
            pltpu.SemaphoreType.DMA((9,)),
        ],
        compiler_params=pltpu.CompilerParams(vmem_limit_bytes=60 * 2**20),
        name="write_outputs",
    )(final, gate, value, es)


def solution(mesh):
    in_specs = (
        P(None, "seq", None),
        P(None, "seq", None),
        P(),
        P("section", None),
        P("section", None, None, None),
        P("section", None, None, None),
        P("section", None, None, None),
        P("section", None, None, None),
        P("section", "seq", None, None),
        P("section", "seq", None, None),
    )
    out_specs = (
        P(None, "seq", None),
        P("section", None),
        P("section", None, None, None),
        P("section", None, None, None),
        P("section", None, None, None),
        P("section", None, None, None),
        P("section", "seq", None, None),
        P("section", "seq", None, None),
    )
    return jax.shard_map(
        on_device, mesh=mesh, in_specs=in_specs, out_specs=out_specs, check_vma=False
    )
```
